32 devices in a mesh: dp: 16 (over z, y, core), tensor: 2 (over x).
Axes of the slice: x: 2, y: 2, z: 4, core: 2. Of those that a mesh axis runs over, the one named last changes fastest.
Arguments:
- layer_input: bfloat16 [32768, 1024], P(('dp', 'tensor')), may hold values from -6 to 6
- target: bfloat16 [32768, 1024], P(('dp', 'tensor')), may hold values from -6 to 6
- segment: int32 [32768], P('dp'), may hold values from 0 to 2047, as said below
- pad_mask: int32 [32768], P(('dp', 'tensor')), may hold values from 0 to 1, as said below
- norm1_gain: float32 [1024], replicated, may hold values from 0.5 to 1.5
- w_query: bfloat16 [1024, 1024], P('dp', 'tensor'), may hold values from -0.1875 to 0.1875
- w_key: bfloat16 [1024, 1024], P('dp', 'tensor'), may hold values from -0.1875 to 0.1875
- w_value: bfloat16 [1024, 2048], P('dp', 'tensor'), may hold values from -0.1875 to 0.1875
- w_gate_out: bfloat16 [1024, 2048], P('dp', 'tensor'), may hold values from -0.1875 to 0.1875
- w_decay: bfloat16 [1024, 8], P('dp', 'tensor'), may hold values from -0.1875 to 0.1875
- w_beta: bfloat16 [1024, 8], P('dp', 'tensor'), may hold values from -0.1875 to 0.1875
- conv_query: float32 [4, 1024], replicated, may hold values from -3 to 3
- conv_key: float32 [4, 1024], replicated, may hold values from -3 to 3
- conv_value: float32 [4, 2048], replicated, may hold values from -3 to 3
- decay_scale: float32 [8], replicated, may hold values from 0.3 to 8
- decay_bias: float32 [8], replicated, may hold values from -5 to -2
- out_norm_gain: float32 [256], replicated, may hold values from 0.5 to 1.5
- w_out: bfloat16 [1024, 2048], P('dp', 'tensor'), may hold values from -0.25 to 0.25
- norm2_gain: float32 [1024], replicated, may hold values from 0.5 to 1.5
- w_ffn_gate: bfloat16 [1024, 2816], P('dp', 'tensor'), may hold values from -0.1875 to 0.1875
- w_ffn_up: bfloat16 [1024, 2816], P('dp', 'tensor'), may hold values from -0.1875 to 0.1875
- w_ffn_down: bfloat16 [1024, 2816], P('dp', 'tensor'), may hold values from -0.109375 to 0.109375
Outputs:
- output: float32 [32768, 1024], P(('dp', 'tensor'))
- loss: float32 [], replicated
- grad_input: float32 [32768, 1024], P(('dp', 'tensor'))
- grad_norm1_gain: float32 [1024], replicated
- grad_w_query: float32 [1024, 1024], P('dp', 'tensor')
- grad_w_key: float32 [1024, 1024], P('dp', 'tensor')
- grad_w_value: float32 [1024, 2048], P('dp', 'tensor')
- grad_w_gate_out: float32 [1024, 2048], P('dp', 'tensor')
- grad_w_decay: float32 [1024, 8], P('dp', 'tensor')
- grad_w_beta: float32 [1024, 8], P('dp', 'tensor')
- grad_conv_query: float32 [4, 1024], replicated
- grad_conv_key: float32 [4, 1024], replicated
- grad_conv_value: float32 [4, 2048], replicated
- grad_decay_scale: float32 [8], replicated
- grad_decay_bias: float32 [8], replicated
- grad_out_norm_gain: float32 [256], replicated
- grad_w_out: float32 [1024, 2048], P('dp', 'tensor')
- grad_norm2_gain: float32 [1024], replicated
- grad_w_ffn_gate: float32 [1024, 2816], P('dp', 'tensor')
- grad_w_ffn_up: float32 [1024, 2816], P('dp', 'tensor')
- grad_w_ffn_down: float32 [1024, 2816], P('dp', 'tensor')
The draws below stay inside these ranges and needn't reach their ends.
Inputs may be any that keep to these rules, and one draw needn't show every extreme that they name: `segment`: ids never decrease within a sequence of 1024 tokens; each document's tokens share one id, the padding at a sequence's end has an id of its own, and different sequences share no id. Documents have 1 to 800 tokens, the last of a sequence cut to fit. `pad_mask`: each sequence of 1024 tokens ends with 1 to max(64, 2) padding tokens, marked 0; all other tokens are 1.
All inputs are finite; a program needn't handle non-finite values.
Results may differ from the reference program's by a relative error of at most 0.015.
Values may be sent and summed in bfloat16 or wider, within the bound.
No kernel may reach another device: no remote copies, remote signals or barrier semaphores. Data moves between devices by JAX's collectives and lax.ppermute only.
A program may use at most 384 MiB of HBM per device.

```python
import math
import jax
import jax.numpy as jnp
from jax import lax

D = 1024
H = 8
DK = 128
DV = 256
FF = 2816
KCONV = 4
CH = 64
LENGTH = 1024
SEQS = 2
TOKENS = 32768
N_DP = 16


def layout_draw(key):
    seq_count = TOKENS // LENGTH
    shortest = max(LENGTH * 60 // 1024, 2)
    longest = max(LENGTH * 800 // 1024, shortest + 1)
    most_docs = LENGTH // shortest + 2
    folded = jax.random.fold_in(key, 11)
    key_length, key_padding = jax.random.split(folded)
    doc_lengths = jax.random.randint(key_length, (seq_count, most_docs), shortest, longest + 1)
    padding = jax.random.randint(key_padding, (seq_count, 1), 1, max(LENGTH // 16, 2) + 1)
    doc_ends = jnp.cumsum(doc_lengths, axis=1)
    position = jnp.arange(LENGTH)
    doc_index = jnp.sum((doc_ends[:, None, :] <= position[None, :, None]).astype(jnp.int32), axis=2)
    live_tokens = position[None, :] < LENGTH - padding
    base_ids = jnp.arange(seq_count)[:, None] * 64
    ids = jnp.where(live_tokens, base_ids + doc_index, base_ids + 63)
    return (ids.reshape(-1).astype(jnp.int32), live_tokens.astype(jnp.int32).reshape(-1))


def draw_segment(key, part):
    return layout_draw(key)[0]


def draw_pad_mask(key, part):
    return layout_draw(key)[1]


def shard_levels(rng, shape, cuts, least, high):
    level, own = 1.0, jax.random.fold_in(rng, 6)
    for dim, shards_of in cuts:
        heights = jnp.exp(jax.random.uniform(jax.random.fold_in(own, dim), (shards_of,), jnp.float32, least / len(cuts), high / len(cuts)))
        level = level * jnp.repeat(heights, shape[dim] // shards_of).reshape([-1 if axis == dim else 1 for axis in range(len(shape))])
    return level


def centred(stream_key, shape, deviation, limit, cuts=(), kind=jnp.bfloat16):
    level = shard_levels(stream_key, shape, cuts, -0.22, 0.18) if cuts else 1.0
    array = jax.random.normal(stream_key, shape, jnp.float32) * deviation * level
    return jnp.minimum(jnp.maximum(array, -limit), limit).astype(kind)


def setup_inputs(seed: int = 0) -> dict:
    streams_of = jax.random.split(jax.random.key(seed), 23)
    return {
        "layer_input": centred(streams_of[0], (TOKENS, D), 1.0, 6.0, ((0, 32),)),
        "target": centred(streams_of[1], (TOKENS, D), 1.0, 6.0, ((0, 32),)),
        "segment": draw_segment(jax.random.fold_in(streams_of[22], 71), 0),
        "pad_mask": draw_pad_mask(jax.random.fold_in(streams_of[22], 71), 0),
        "norm1_gain": jnp.clip(1.0 + 0.1 * jax.random.normal(streams_of[4], (D,), jnp.float32), 0.5, 1.5),
        "w_query": centred(streams_of[5], (D, H * DK), D ** -0.5, 0.1875, ((0, 16), (1, 2))),
        "w_key": centred(streams_of[6], (D, H * DK), D ** -0.5, 0.1875, ((0, 16), (1, 2))),
        "w_value": centred(streams_of[7], (D, H * DV), D ** -0.5, 0.1875, ((0, 16), (1, 2))),
        "w_gate_out": centred(streams_of[8], (D, H * DV), D ** -0.5, 0.1875, ((0, 16), (1, 2))),
        "w_decay": centred(streams_of[9], (D, H), D ** -0.5, 0.1875, ((0, 16), (1, 2))),
        "w_beta": centred(streams_of[10], (D, H), D ** -0.5, 0.1875, ((0, 16), (1, 2))),
        "conv_query": centred(streams_of[11], (KCONV, H * DK), 0.5, 3.0, (), jnp.float32),
        "conv_key": centred(streams_of[12], (KCONV, H * DK), 0.5, 3.0, (), jnp.float32),
        "conv_value": centred(streams_of[13], (KCONV, H * DV), 0.5, 3.0, (), jnp.float32),
        "decay_scale": jnp.clip(jnp.exp(jax.random.uniform(streams_of[14], (H,), jnp.float32, math.log(0.3), math.log(8.0))), 0.3, 8.0),
        "decay_bias": jnp.clip(jax.random.uniform(streams_of[15], (H,), jnp.float32, -5.0, -2.0), -5.0, -2.0),
        "out_norm_gain": jnp.clip(1.0 + 0.1 * jax.random.normal(streams_of[16], (DV,), jnp.float32), 0.5, 1.5),
        "w_out": centred(streams_of[17], (D, H * DV), (H * DV // 4) ** -0.5, 0.25, ((0, 16), (1, 2))),
        "norm2_gain": jnp.clip(1.0 + 0.1 * jax.random.normal(streams_of[18], (D,), jnp.float32), 0.5, 1.5),
        "w_ffn_gate": centred(streams_of[19], (D, FF), D ** -0.5, 0.1875, ((0, 16), (1, 2))),
        "w_ffn_up": centred(streams_of[20], (D, FF), D ** -0.5, 0.1875, ((0, 16), (1, 2))),
        "w_ffn_down": centred(streams_of[21], (D, FF), FF ** -0.5, 0.109375, ((0, 16), (1, 2))),
    }


@jax.custom_vjp
def low(v):
    return lax.optimization_barrier(v.astype(jnp.bfloat16)).astype(jnp.float32)

@jax.custom_vjp
def low_back(v):
    return v

def low_keep(v):
    return (low(v), None)

def low_pass(kept, grad):
    return (grad,)

def back_keep(v):
    return (v, None)

def back_low(kept, grad):
    return (low(grad),)
low.defvjp(low_keep, low_pass)
low_back.defvjp(back_keep, back_low)
exact_precision = lax.Precision.HIGHEST

def rms_scale(values, gain):
    return values * lax.rsqrt(lax.optimization_barrier(jnp.mean(values * values, axis=-1, keepdims=True)) + 1e-06) * gain

def exact_dot(left, right):
    return jnp.dot(left, right, precision=exact_precision)

def shift_masks(segment_ids, taps):
    masks = [jnp.ones(segment_ids.shape, jnp.float32)]
    for offset in range(1, taps):
        earlier = jnp.concatenate([jnp.full((offset,), -1, jnp.int32), segment_ids[:-offset].astype(jnp.int32)])
        masks.append((segment_ids == earlier).astype(jnp.float32))
    return masks

def short_conv(values, kernel, masks):
    result = values * kernel[0]
    for offset in range(1, len(masks)):
        shifted = jnp.concatenate([jnp.zeros((offset, values.shape[1]), jnp.float32), values[:-offset]])
        result = result + shifted * masks[offset][:, None] * kernel[offset]
    return result

def unit_rows(values):
    return values * lax.rsqrt(lax.optimization_barrier(jnp.sum(values * values, axis=-1, keepdims=True)) + 1e-06)

def lower_inverse(lower_part, length):
    negative = -lower_part
    inverse = jnp.eye(length, dtype=jnp.float32) + negative
    power = negative
    covered = 2
    while covered < length:
        power = jnp.einsum('hij,hjk->hik', power, power, precision=exact_precision)
        inverse = inverse + jnp.einsum('hij,hjk->hik', inverse, power, precision=exact_precision)
        covered = covered * 2
    return inverse

def block_update(state, inputs):
    queries, keys, values, betas, log_decay, seg_block, previous = inputs
    length = queries.shape[0]
    cumulative = jnp.cumsum(log_decay, axis=0)
    order = jnp.arange(length)
    causal = order[:, None] >= order[None, :]
    strict = order[:, None] > order[None, :]
    same_doc = seg_block[:, None] == seg_block[None, :]
    visible = (same_doc & causal)[:, :, None]
    spread = cumulative[:, None, :] - cumulative[None, :, :]
    weights = jnp.where(visible, jnp.exp(jnp.where(visible, spread, 0.0)), 0.0)
    carried = (seg_block == previous).astype(jnp.float32)
    carry_decay = jnp.exp(cumulative) * carried[:, None]
    key_gram = jnp.einsum('ihd,jhd->ijh', keys, keys, precision=exact_precision)
    lower_part = jnp.where(strict[:, :, None], betas[:, None, :] * weights * key_gram, 0.0)
    inverse = lower_inverse(jnp.transpose(lower_part, (2, 0, 1)), length)
    key_state = jnp.einsum('ihd,hde->ihe', keys, state, precision=exact_precision)
    target_rows = betas[:, :, None] * (values - carry_decay[:, :, None] * key_state)
    pseudo = jnp.einsum('hij,jhe->hie', inverse, target_rows, precision=exact_precision)
    scores = jnp.einsum('ihd,jhd->hij', queries, keys, precision=exact_precision) * jnp.transpose(weights, (2, 0, 1))
    query_state = jnp.einsum('ihd,hde->ihe', queries, state, precision=exact_precision)
    outputs = carry_decay[:, :, None] * query_state + jnp.einsum('hij,hje->ihe', scores, pseudo, precision=exact_precision)
    last_weights = weights[-1]
    new_state = (carried[-1] * jnp.exp(cumulative[-1]))[:, None, None] * state + jnp.einsum('jh,jhd,hje->hde', last_weights, keys, pseudo, precision=exact_precision)
    return (new_state, outputs)

def mixer_sequence(q_pre, k_pre, v_pre, g_pre, a_pre, b_pre, segment_ids, conv_q, conv_k, conv_v, scale_rate, bias_rate, out_gain):
    length = q_pre.shape[0]
    heads = a_pre.shape[1]
    key_size = q_pre.shape[1] // heads
    value_size = v_pre.shape[1] // heads
    masks = shift_masks(segment_ids, conv_q.shape[0])
    queries = unit_rows(jax.nn.silu(short_conv(q_pre, conv_q, masks)).reshape(length, heads, key_size)) * key_size ** (-0.5)
    keys = unit_rows(jax.nn.silu(short_conv(k_pre, conv_k, masks)).reshape(length, heads, key_size))
    values = jax.nn.silu(short_conv(v_pre, conv_v, masks)).reshape(length, heads, value_size)
    betas = jax.nn.sigmoid(b_pre)
    log_decay = -scale_rate * jax.nn.softplus(a_pre + bias_rate)
    blocks = length // CH
    seg_blocks = segment_ids.reshape(blocks, CH)
    previous = jnp.concatenate([jnp.full((1,), -1, jnp.int32), seg_blocks[:-1, -1].astype(jnp.int32)])
    state = jnp.zeros((heads, key_size, value_size), jnp.float32)
    carried_in = (queries.reshape(blocks, CH, heads, key_size), keys.reshape(blocks, CH, heads, key_size), values.reshape(blocks, CH, heads, value_size), betas.reshape(blocks, CH, heads), log_decay.reshape(blocks, CH, heads), seg_blocks, previous)
    final_state, outputs = lax.scan(jax.checkpoint(block_update), state, carried_in)
    outputs = outputs.reshape(length, heads, value_size)
    gated = rms_scale(outputs, out_gain) * jax.nn.silu(g_pre.reshape(length, heads, value_size))
    return gated.reshape(length, heads * value_size)

def reference(layer_input, target, segment, pad_mask, norm1_gain, w_query, w_key, w_value, w_gate_out, w_decay, w_beta, conv_query, conv_key, conv_value, decay_scale, decay_bias, out_norm_gain, w_out, norm2_gain, w_ffn_gate, w_ffn_up, w_ffn_down):
    floats = [item.astype(jnp.float32) for item in (layer_input, norm1_gain, w_query, w_key, w_value, w_gate_out, w_decay, w_beta, conv_query, conv_key, conv_value, decay_scale, decay_bias, out_norm_gain, w_out, norm2_gain, w_ffn_gate, w_ffn_up, w_ffn_down)]

    def forward(input_float, gain_one, wq, wk, wv, wg, wa, wb, conv_q, conv_k, conv_v, scale_rate, bias_rate, out_gain, wo, gain_two, ffn_gate, ffn_up, ffn_down):
        normed = low(rms_scale(input_float, gain_one))
        projected = [low_back(exact_dot(normed, weight)) for weight in (wq, wk, wv, wg, wa, wb)]

        def group_mix(items):
            return jax.vmap(mixer_sequence, in_axes=(0, 0, 0, 0, 0, 0, 0, None, None, None, None, None, None))(*items, conv_q, conv_k, conv_v, scale_rate, bias_rate, out_gain)
        grouped = tuple([item.reshape(N_DP, SEQS, LENGTH, item.shape[1]) for item in projected] + [segment.reshape(N_DP, SEQS, LENGTH)])
        mixed = lax.map(jax.checkpoint(group_mix), grouped)
        mixed = low(mixed.reshape(TOKENS, mixed.shape[-1]))
        attention = low_back(exact_dot(mixed, wo.T))
        residual = input_float + attention
        normed_two = low(rms_scale(residual, gain_two))
        gate_pre = low_back(exact_dot(normed_two, ffn_gate))
        up_pre = low_back(exact_dot(normed_two, ffn_up))
        hidden = low(jax.nn.silu(gate_pre) * up_pre)
        ffn_out = low_back(exact_dot(hidden, ffn_down.T))
        return residual + ffn_out
    output, pullback = jax.vjp(forward, *floats)
    live = pad_mask.astype(jnp.float32)
    error = output - target.astype(jnp.float32)
    count = jnp.sum(live)
    loss = jnp.sum(live[:, None] * error * error) / (count * D)
    grad_output = error * live[:, None] * (TOKENS / count)
    grads = pullback(grad_output)
    return (output, loss, grads[0], grads[1], grads[2], grads[3], grads[4], grads[5], grads[6], grads[7], grads[8], grads[9], grads[10], grads[11], grads[12], grads[13], grads[14], grads[15], grads[16], grads[17], grads[18])
```

```python
import jax
import jax.numpy as jnp
from jax import lax
from jax.sharding import PartitionSpec as P

CH = 64
LENGTH = 1024


exact_precision = lax.Precision.HIGHEST


def rms_scale(values, gain):
    return values * lax.rsqrt(jnp.mean(values * values, axis=-1, keepdims=True) + 1e-06) * gain


def shift_masks(segment_ids, taps):
    masks = [jnp.ones(segment_ids.shape, jnp.float32)]
    for offset in range(1, taps):
        earlier = jnp.concatenate([jnp.full((offset,), -1, jnp.int32), segment_ids[:-offset]])
        masks.append((segment_ids == earlier).astype(jnp.float32))
    return masks


def short_conv(values, kernel, masks):
    result = values * kernel[0]
    for offset in range(1, len(masks)):
        shifted = jnp.concatenate(
            [jnp.zeros((offset, values.shape[1]), jnp.float32), values[:-offset]]
        )
        result = result + shifted * masks[offset][:, None] * kernel[offset]
    return result


def unit_rows(values):
    return values * lax.rsqrt(jnp.sum(values * values, axis=-1, keepdims=True) + 1e-06)


def lower_inverse(lower_part, length):
    negative = -lower_part
    inverse = jnp.eye(length, dtype=jnp.float32) + negative
    power = negative
    covered = 2
    while covered < length:
        power = jnp.einsum("hij,hjk->hik", power, power, precision=exact_precision)
        inverse = inverse + jnp.einsum("hij,hjk->hik", inverse, power, precision=exact_precision)
        covered = covered * 2
    return inverse


def block_update(state, inputs):
    queries, keys, values, betas, log_decay, seg_block, previous = inputs
    length = queries.shape[0]
    cumulative = jnp.cumsum(log_decay, axis=0)
    order = jnp.arange(length)
    causal = order[:, None] >= order[None, :]
    strict = order[:, None] > order[None, :]
    same_doc = seg_block[:, None] == seg_block[None, :]
    visible = (same_doc & causal)[:, :, None]
    spread = cumulative[:, None, :] - cumulative[None, :, :]
    weights = jnp.where(visible, jnp.exp(jnp.where(visible, spread, 0.0)), 0.0)
    carried = (seg_block == previous).astype(jnp.float32)
    carry_decay = jnp.exp(cumulative) * carried[:, None]
    key_gram = jnp.einsum("ihd,jhd->ijh", keys, keys, precision=exact_precision)
    lower_part = jnp.where(strict[:, :, None], betas[:, None, :] * weights * key_gram, 0.0)
    inverse = lower_inverse(jnp.transpose(lower_part, (2, 0, 1)), length)
    key_state = jnp.einsum("ihd,hde->ihe", keys, state, precision=exact_precision)
    target_rows = betas[:, :, None] * (values - carry_decay[:, :, None] * key_state)
    pseudo = jnp.einsum("hij,jhe->hie", inverse, target_rows, precision=exact_precision)
    scores = jnp.einsum("ihd,jhd->hij", queries, keys, precision=exact_precision) * jnp.transpose(
        weights, (2, 0, 1)
    )
    query_state = jnp.einsum("ihd,hde->ihe", queries, state, precision=exact_precision)
    outputs = carry_decay[:, :, None] * query_state + jnp.einsum(
        "hij,hje->ihe", scores, pseudo, precision=exact_precision
    )
    last_weights = weights[-1]
    new_state = (carried[-1] * jnp.exp(cumulative[-1]))[:, None, None] * state + jnp.einsum(
        "jh,jhd,hje->hde", last_weights, keys, pseudo, precision=exact_precision
    )
    return (new_state, outputs)


def mixer_sequence(
    q_pre,
    k_pre,
    v_pre,
    g_pre,
    a_pre,
    b_pre,
    segment_ids,
    conv_q,
    conv_k,
    conv_v,
    scale_rate,
    bias_rate,
    out_gain,
):
    length = q_pre.shape[0]
    heads = a_pre.shape[1]
    key_size = q_pre.shape[1] // heads
    value_size = v_pre.shape[1] // heads
    masks = shift_masks(segment_ids, conv_q.shape[0])
    queries = unit_rows(
        jax.nn.silu(short_conv(q_pre, conv_q, masks)).reshape(length, heads, key_size)
    ) * key_size ** (-0.5)
    keys = unit_rows(jax.nn.silu(short_conv(k_pre, conv_k, masks)).reshape(length, heads, key_size))
    values = jax.nn.silu(short_conv(v_pre, conv_v, masks)).reshape(length, heads, value_size)
    betas = jax.nn.sigmoid(b_pre)
    log_decay = -scale_rate * jax.nn.softplus(a_pre + bias_rate)
    blocks = length // CH
    seg_blocks = segment_ids.reshape(blocks, CH)
    previous = jnp.concatenate([jnp.full((1,), -1, jnp.int32), seg_blocks[:-1, -1]])
    state = jnp.zeros((heads, key_size, value_size), jnp.float32)
    carried_in = (
        queries.reshape(blocks, CH, heads, key_size),
        keys.reshape(blocks, CH, heads, key_size),
        values.reshape(blocks, CH, heads, value_size),
        betas.reshape(blocks, CH, heads),
        log_decay.reshape(blocks, CH, heads),
        seg_blocks,
        previous,
    )
    final_state, outputs = lax.scan(jax.checkpoint(block_update), state, carried_in)
    outputs = outputs.reshape(length, heads, value_size)
    gated = rms_scale(outputs, out_gain) * jax.nn.silu(g_pre.reshape(length, heads, value_size))
    return gated.reshape(length, heads * value_size)


def contract_rows(left, right):
    return lax.dot_general(
        left, right, (((0,), (0,)), ((), ())), preferred_element_type=jnp.float32
    )


def contract_cols(left, right):
    return lax.dot_general(
        left, right, (((1,), (1,)), ((), ())), preferred_element_type=jnp.float32
    )


def feed_inputs(normed_rows, gate_weight, up_weight):
    gate_pre = jnp.dot(normed_rows, gate_weight, preferred_element_type=jnp.float32)
    up_pre = jnp.dot(normed_rows, up_weight, preferred_element_type=jnp.float32)
    return (gate_pre, up_pre)


def on_device_split(
    layer_input,
    target,
    segment,
    pad_mask,
    norm1_gain,
    w_query,
    w_key,
    w_value,
    w_gate_out,
    w_decay,
    w_beta,
    conv_query,
    conv_key,
    conv_value,
    decay_scale,
    decay_bias,
    out_norm_gain,
    w_out,
    norm2_gain,
    w_ffn_gate,
    w_ffn_up,
    w_ffn_down,
):
    own_rows, width = layer_input.shape
    group_rows = segment.shape[0]
    sequences = group_rows // LENGTH
    tensor_index = lax.axis_index("tensor")
    heads_local = w_decay.shape[1]
    query_cols = w_query.shape[1]
    value_cols = w_value.shape[1]
    input_float = layer_input.astype(jnp.float32)
    normed_own, norm1_pull = jax.vjp(rms_scale, input_float, norm1_gain)
    normed = lax.all_gather(normed_own.astype(jnp.bfloat16), "tensor", axis=0, tiled=True)
    full_query, full_key, full_value, full_gate, full_decay, full_beta, full_out = (
        lax.all_gather(w_query, "dp", axis=0, tiled=True),
        lax.all_gather(w_key, "dp", axis=0, tiled=True),
        lax.all_gather(w_value, "dp", axis=0, tiled=True),
        lax.all_gather(w_gate_out, "dp", axis=0, tiled=True),
        lax.all_gather(w_decay, "dp", axis=0, tiled=True),
        lax.all_gather(w_beta, "dp", axis=0, tiled=True),
        lax.all_gather(w_out, "dp", axis=0, tiled=True),
    )
    proj_weights = (full_query, full_key, full_value, full_gate, full_decay, full_beta)
    projected = [
        jnp.dot(normed, weight, preferred_element_type=jnp.float32) for weight in proj_weights
    ]
    conv_q_local = lax.dynamic_slice_in_dim(conv_query, tensor_index * query_cols, query_cols, 1)
    conv_k_local = lax.dynamic_slice_in_dim(conv_key, tensor_index * query_cols, query_cols, 1)
    conv_v_local = lax.dynamic_slice_in_dim(conv_value, tensor_index * value_cols, value_cols, 1)
    scale_local = lax.dynamic_slice_in_dim(decay_scale, tensor_index * heads_local, heads_local, 0)
    bias_local = lax.dynamic_slice_in_dim(decay_bias, tensor_index * heads_local, heads_local, 0)
    seg_rows = segment.reshape(sequences, LENGTH)

    def mixer_local(
        q_pre,
        k_pre,
        v_pre,
        g_pre,
        a_pre,
        b_pre,
        conv_q,
        conv_k,
        conv_v,
        scale_rate,
        bias_rate,
        out_gain,
    ):
        shaped = [
            item.reshape(sequences, LENGTH, item.shape[1])
            for item in (q_pre, k_pre, v_pre, g_pre, a_pre, b_pre)
        ]
        mixed_rows = jax.vmap(
            mixer_sequence, in_axes=(0, 0, 0, 0, 0, 0, 0, None, None, None, None, None, None)
        )(*shaped, seg_rows, conv_q, conv_k, conv_v, scale_rate, bias_rate, out_gain)
        return mixed_rows.reshape(group_rows, mixed_rows.shape[2])

    mixed, mixer_pull = jax.vjp(
        mixer_local,
        *projected,
        conv_q_local,
        conv_k_local,
        conv_v_local,
        scale_local,
        bias_local,
        out_norm_gain
    )
    mixed_low = mixed.astype(jnp.bfloat16)
    attention = lax.psum_scatter(
        contract_cols(mixed_low, full_out), "tensor", scatter_dimension=0, tiled=True
    )
    residual = input_float + attention
    normed2_own, norm2_pull = jax.vjp(rms_scale, residual, norm2_gain)
    normed2 = lax.all_gather(normed2_own.astype(jnp.bfloat16), "tensor", axis=0, tiled=True)
    ffn_gate_w, ffn_up_w, ffn_down_w = (
        lax.all_gather(w_ffn_gate, "dp", axis=0, tiled=True),
        lax.all_gather(w_ffn_up, "dp", axis=0, tiled=True),
        lax.all_gather(w_ffn_down, "dp", axis=0, tiled=True),
    )
    gate_pre, up_pre = feed_inputs(normed2, ffn_gate_w, ffn_up_w)
    hidden = (jax.nn.silu(gate_pre) * up_pre).astype(jnp.bfloat16)
    ffn_out = lax.psum_scatter(
        contract_cols(hidden, ffn_down_w).astype(jnp.bfloat16),
        "tensor",
        scatter_dimension=0,
        tiled=True,
    ).astype(jnp.float32)
    output = residual + ffn_out
    live = pad_mask.astype(jnp.float32)
    error = output - target.astype(jnp.float32)
    loss_sum, count = lax.psum(
        (jnp.sum(live[:, None] * error * error), jnp.sum(live)), ("dp", "tensor")
    )
    loss = loss_sum / (count * width)
    all_tokens = own_rows * lax.axis_size("dp") * lax.axis_size("tensor")
    grad_output = error * live[:, None] * (all_tokens / count)
    grad_ffn = lax.all_gather(grad_output.astype(jnp.bfloat16), "tensor", axis=0, tiled=True)
    grad_hidden = jnp.dot(grad_ffn, ffn_down_w, preferred_element_type=jnp.float32)
    sigmoid_gate = jax.nn.sigmoid(gate_pre)
    grad_gate = (
        grad_hidden * up_pre * sigmoid_gate * (1.0 + gate_pre * (1.0 - sigmoid_gate))
    ).astype(jnp.bfloat16)
    grad_up = (grad_hidden * gate_pre * sigmoid_gate).astype(jnp.bfloat16)
    grad_down_local = contract_rows(grad_ffn, hidden)
    grad_gate_local = contract_rows(normed2, grad_gate)
    grad_up_local = contract_rows(normed2, grad_up)
    normed2_part = contract_cols(grad_gate, ffn_gate_w) + contract_cols(grad_up, ffn_up_w)
    grad_normed2 = lax.psum_scatter(
        normed2_part.astype(jnp.bfloat16), "tensor", scatter_dimension=0, tiled=True
    ).astype(jnp.float32)
    grad_residual_norm, grad_gain_two = norm2_pull(grad_normed2)
    grad_residual = grad_output + grad_residual_norm
    grad_attention = lax.all_gather(
        grad_residual.astype(jnp.bfloat16), "tensor", axis=0, tiled=True
    )
    grad_mixed = jnp.dot(grad_attention, full_out, preferred_element_type=jnp.float32)
    grad_out_local = contract_rows(grad_attention, mixed_low)
    mixer_grads = mixer_pull(grad_mixed)
    pre_grads = [item.astype(jnp.bfloat16) for item in mixer_grads[:6]]
    normed_part = contract_cols(pre_grads[0], full_query)
    for grad_item, weight in zip(pre_grads[1:], proj_weights[1:]):
        normed_part = normed_part + contract_cols(grad_item, weight)
    weight_locals = [contract_rows(normed, grad_item) for grad_item in pre_grads]
    grad_normed = lax.psum_scatter(
        normed_part.astype(jnp.bfloat16), "tensor", scatter_dimension=0, tiled=True
    ).astype(jnp.float32)
    grad_input_norm, grad_gain_one = norm1_pull(grad_normed)
    grad_input = grad_residual + grad_input_norm
    owned = (
        lax.psum_scatter(
            grad_gate_local.astype(jnp.bfloat16), "dp", scatter_dimension=0, tiled=True
        ).astype(jnp.float32),
        lax.psum_scatter(
            grad_up_local.astype(jnp.bfloat16), "dp", scatter_dimension=0, tiled=True
        ).astype(jnp.float32),
        lax.psum_scatter(
            grad_down_local.astype(jnp.bfloat16), "dp", scatter_dimension=0, tiled=True
        ).astype(jnp.float32),
        lax.psum_scatter(
            weight_locals[0].astype(jnp.bfloat16), "dp", scatter_dimension=0, tiled=True
        ).astype(jnp.float32),
        lax.psum_scatter(
            weight_locals[1].astype(jnp.bfloat16), "dp", scatter_dimension=0, tiled=True
        ).astype(jnp.float32),
        lax.psum_scatter(
            weight_locals[2].astype(jnp.bfloat16), "dp", scatter_dimension=0, tiled=True
        ).astype(jnp.float32),
        lax.psum_scatter(
            weight_locals[3].astype(jnp.bfloat16), "dp", scatter_dimension=0, tiled=True
        ).astype(jnp.float32),
        lax.psum_scatter(
            weight_locals[4].astype(jnp.bfloat16), "dp", scatter_dimension=0, tiled=True
        ).astype(jnp.float32),
        lax.psum_scatter(
            weight_locals[5].astype(jnp.bfloat16), "dp", scatter_dimension=0, tiled=True
        ).astype(jnp.float32),
        lax.psum_scatter(
            grad_out_local.astype(jnp.bfloat16), "dp", scatter_dimension=0, tiled=True
        ).astype(jnp.float32),
    )
    conv_q_full = lax.dynamic_update_slice_in_dim(
        jnp.zeros_like(conv_query), mixer_grads[6], tensor_index * query_cols, 1
    )
    conv_k_full = lax.dynamic_update_slice_in_dim(
        jnp.zeros_like(conv_key), mixer_grads[7], tensor_index * query_cols, 1
    )
    conv_v_full = lax.dynamic_update_slice_in_dim(
        jnp.zeros_like(conv_value), mixer_grads[8], tensor_index * value_cols, 1
    )
    scale_full = lax.dynamic_update_slice_in_dim(
        jnp.zeros_like(decay_scale), mixer_grads[9], tensor_index * heads_local, 0
    )
    bias_full = lax.dynamic_update_slice_in_dim(
        jnp.zeros_like(decay_bias), mixer_grads[10], tensor_index * heads_local, 0
    )
    summed = lax.psum(
        (
            grad_gain_one,
            grad_gain_two,
            conv_q_full,
            conv_k_full,
            conv_v_full,
            scale_full,
            bias_full,
            mixer_grads[11],
        ),
        ("dp", "tensor"),
    )
    return (
        output,
        loss,
        grad_input,
        summed[0],
        owned[3],
        owned[4],
        owned[5],
        owned[6],
        owned[7],
        owned[8],
        summed[2],
        summed[3],
        summed[4],
        summed[5],
        summed[6],
        summed[7],
        owned[9],
        summed[1],
        owned[0],
        owned[1],
        owned[2],
    )


def gather_all(local):
    rows = lax.all_gather(local, ("tensor", "dp"), axis=0, tiled=True)
    shares = lax.axis_size("tensor")
    return rows.reshape(shares, rows.shape[0] // shares, rows.shape[1])


def scatter_all(parts):
    shares, rows, cols = parts.shape
    return lax.psum_scatter(
        parts.reshape(shares * rows, cols), ("tensor", "dp"), scatter_dimension=0, tiled=True
    ).astype(jnp.float32)


def columns(array, sizes):
    pieces, start = [], 0
    for size in sizes:
        pieces.append(array[..., start : start + size])
        start += size
    return pieces


def on_device_whole(
    layer_input,
    target,
    segment,
    pad_mask,
    norm1_gain,
    w_query,
    w_key,
    w_value,
    w_gate_out,
    w_decay,
    w_beta,
    conv_query,
    conv_key,
    conv_value,
    decay_scale,
    decay_bias,
    out_norm_gain,
    w_out,
    norm2_gain,
    w_ffn_gate,
    w_ffn_up,
    w_ffn_down,
):
    own_rows, width = layer_input.shape
    shares = lax.axis_size("tensor")
    sequences = own_rows // LENGTH
    tensor_index = lax.axis_index("tensor")
    low = jnp.bfloat16
    proj_local = (w_query, w_key, w_value, w_gate_out, w_decay, w_beta)
    proj_sizes = [item.shape[1] for item in proj_local]
    used = sum(proj_sizes)
    padded = -(-used // 128) * 128
    proj_all = gather_all(
        jnp.concatenate(proj_local + (jnp.zeros((w_query.shape[0], padded - used), low),), axis=1)
    )
    rest_local = (w_out, w_ffn_gate, w_ffn_up, w_ffn_down)
    rest_sizes = [item.shape[1] for item in rest_local]
    rest_all = gather_all(jnp.concatenate(rest_local, axis=1))
    out_all, gate_all, up_all, down_all = columns(rest_all, rest_sizes)
    live = pad_mask.astype(jnp.float32)
    count = lax.psum(jnp.sum(live), ("dp", "tensor"))
    input_float = layer_input.astype(jnp.float32)
    normed_float, norm1_pull = jax.vjp(rms_scale, input_float, norm1_gain)
    normed = normed_float.astype(low)
    seg_rows = lax.dynamic_slice_in_dim(segment, tensor_index * own_rows, own_rows, 0).reshape(
        sequences, LENGTH
    )
    projected = [
        columns(jnp.dot(normed, proj_all[part], preferred_element_type=jnp.float32), proj_sizes)
        for part in range(shares)
    ]
    pre = [
        jnp.concatenate([projected[part][item] for part in range(shares)], axis=1)
        for item in range(6)
    ]

    def mixer_local(
        q_pre, k_pre, v_pre, g_pre, a_pre, b_pre, conv_q, conv_k, conv_v, rate, bias, out_gain
    ):
        shaped = [
            item.reshape(sequences, LENGTH, item.shape[1])
            for item in (q_pre, k_pre, v_pre, g_pre, a_pre, b_pre)
        ]
        mixed_rows = jax.vmap(
            mixer_sequence, in_axes=(0, 0, 0, 0, 0, 0, 0, None, None, None, None, None, None)
        )(*shaped, seg_rows, conv_q, conv_k, conv_v, rate, bias, out_gain)
        return mixed_rows.reshape(own_rows, mixed_rows.shape[2])

    mixed, mixer_pull = jax.vjp(
        mixer_local,
        *pre,
        conv_query,
        conv_key,
        conv_value,
        decay_scale,
        decay_bias,
        out_norm_gain
    )
    mixed_low = mixed.astype(low)
    value_cols = w_value.shape[1]
    residual = input_float
    for part in range(shares):
        residual = residual + contract_cols(
            mixed_low[:, part * value_cols : (part + 1) * value_cols], out_all[part]
        )
    normed2_float, norm2_pull = jax.vjp(rms_scale, residual, norm2_gain)
    normed2 = normed2_float.astype(low)
    output = residual
    kept = []
    for part in range(shares):
        gate_pre, up_pre = feed_inputs(normed2, gate_all[part], up_all[part])
        hidden = (jax.nn.silu(gate_pre) * up_pre).astype(low)
        output = output + contract_cols(hidden, down_all[part])
        kept.append((gate_pre, up_pre, hidden))
    error = output - target.astype(jnp.float32)
    loss_sum = jnp.sum(live[:, None] * error * error)
    all_tokens = own_rows * lax.axis_size("dp") * lax.axis_size("tensor")
    grad_output = error * live[:, None] * (all_tokens / count)
    grad_ffn = grad_output.astype(low)
    grad_normed2 = jnp.zeros_like(residual)
    ffn_grads = []
    for part in range(shares):
        gate_pre, up_pre, hidden = kept[part]
        grad_hidden = jnp.dot(grad_ffn, down_all[part], preferred_element_type=jnp.float32)
        sigmoid_gate = jax.nn.sigmoid(gate_pre)
        grad_gate = (
            grad_hidden * up_pre * sigmoid_gate * (1.0 + gate_pre * (1.0 - sigmoid_gate))
        ).astype(low)
        grad_up = (grad_hidden * gate_pre * sigmoid_gate).astype(low)
        grad_normed2 = (
            grad_normed2
            + contract_cols(grad_gate, gate_all[part])
            + contract_cols(grad_up, up_all[part])
        )
        ffn_grads.append(
            (
                contract_rows(normed2, grad_gate),
                contract_rows(normed2, grad_up),
                contract_rows(grad_ffn, hidden),
            )
        )
    grad_residual_norm, grad_gain_two = norm2_pull(grad_normed2)
    grad_residual = grad_output + grad_residual_norm
    grad_attention = grad_residual.astype(low)
    grad_mixed = jnp.concatenate(
        [
            jnp.dot(grad_attention, out_all[part], preferred_element_type=jnp.float32)
            for part in range(shares)
        ],
        axis=1,
    )
    rest_grads = jnp.stack(
        [
            jnp.concatenate(
                [
                    item.astype(low)
                    for item in (
                        contract_rows(
                            grad_attention,
                            mixed_low[:, part * value_cols : (part + 1) * value_cols],
                        ),
                    )
                    + ffn_grads[part]
                ],
                axis=1,
            )
            for part in range(shares)
        ]
    )
    own_out, own_gate, own_up, own_down = columns(scatter_all(rest_grads), rest_sizes)
    mixer_grads = mixer_pull(grad_mixed)
    grad_normed = jnp.zeros_like(residual)
    proj_grads = []
    for part in range(shares):
        grad_part = jnp.concatenate(
            [
                item[:, part * size : (part + 1) * size].astype(low)
                for item, size in zip(mixer_grads[:6], proj_sizes)
            ]
            + [jnp.zeros((own_rows, padded - used), low)],
            axis=1,
        )
        grad_normed = grad_normed + contract_cols(grad_part, proj_all[part])
        proj_grads.append(contract_rows(normed, grad_part).astype(low))
    own_proj = columns(scatter_all(jnp.stack(proj_grads)), proj_sizes)
    grad_input_norm, grad_gain_one = norm1_pull(grad_normed)
    grad_input = grad_residual + grad_input_norm
    summed = lax.psum(
        (grad_gain_one, grad_gain_two) + tuple(mixer_grads[6:12]) + (loss_sum,), ("dp", "tensor")
    )
    loss = summed[8] / (count * width)
    return (
        output,
        loss,
        grad_input,
        summed[0],
        *own_proj,
        summed[2],
        summed[3],
        summed[4],
        summed[5],
        summed[6],
        summed[7],
        own_out,
        summed[1],
        own_gate,
        own_up,
        own_down,
    )


def on_device(layer_input, *others):
    whole = layer_input.shape[0] % LENGTH == 0
    return (on_device_whole if whole else on_device_split)(layer_input, *others)


def solution(mesh):
    return jax.shard_map(
        on_device,
        mesh=mesh,
        in_specs=(
            P(("dp", "tensor"), None),
            P(("dp", "tensor"), None),
            P("dp"),
            P(("dp", "tensor")),
            P(),
            P("dp", "tensor"),
            P("dp", "tensor"),
            P("dp", "tensor"),
            P("dp", "tensor"),
            P("dp", "tensor"),
            P("dp", "tensor"),
            P(),
            P(),
            P(),
            P(),
            P(),
            P(),
            P("dp", "tensor"),
            P(),
            P("dp", "tensor"),
            P("dp", "tensor"),
            P("dp", "tensor"),
        ),
        out_specs=(
            P(("dp", "tensor"), None),
            P(),
            P(("dp", "tensor"), None),
            P(),
            P("dp", "tensor"),
            P("dp", "tensor"),
            P("dp", "tensor"),
            P("dp", "tensor"),
            P("dp", "tensor"),
            P("dp", "tensor"),
            P(),
            P(),
            P(),
            P(),
            P(),
            P(),
            P("dp", "tensor"),
            P(),
            P("dp", "tensor"),
            P("dp", "tensor"),
            P("dp", "tensor"),
        ),
        check_vma=False,
    )
```

```python
import functools

import jax
import jax.numpy as jnp
from jax import lax
from jax.experimental import pallas as pl
from jax.experimental.pallas import tpu as pltpu
from jax.sharding import PartitionSpec as P

CH = 64
LENGTH = 1024


exact_precision = lax.Precision.HIGHEST


def rms_scale(values, gain):
    return values * lax.rsqrt(jnp.mean(values * values, axis=-1, keepdims=True) + 1e-06) * gain


def shift_masks(segment_ids, taps):
    masks = [jnp.ones(segment_ids.shape, jnp.float32)]
    for offset in range(1, taps):
        earlier = jnp.concatenate([jnp.full((offset,), -1, jnp.int32), segment_ids[:-offset]])
        masks.append((segment_ids == earlier).astype(jnp.float32))
    return masks


def short_conv(values, kernel, masks):
    result = values * kernel[0]
    for offset in range(1, len(masks)):
        shifted = jnp.concatenate(
            [jnp.zeros((offset, values.shape[1]), jnp.float32), values[:-offset]]
        )
        result = result + shifted * masks[offset][:, None] * kernel[offset]
    return result


def unit_rows(values):
    return values * lax.rsqrt(jnp.sum(values * values, axis=-1, keepdims=True) + 1e-06)


def lower_inverse(lower_part, length):
    negative = -lower_part
    inverse = jnp.eye(length, dtype=jnp.float32) + negative
    power = negative
    covered = 2
    while covered < length:
        power = jnp.einsum("hij,hjk->hik", power, power, precision=exact_precision)
        inverse = inverse + jnp.einsum("hij,hjk->hik", inverse, power, precision=exact_precision)
        covered = covered * 2
    return inverse


def block_update(state, inputs):
    queries, keys, values, betas, log_decay, seg_block, previous = inputs
    length = queries.shape[0]
    cumulative = jnp.cumsum(log_decay, axis=0)
    order = jnp.arange(length)
    causal = order[:, None] >= order[None, :]
    strict = order[:, None] > order[None, :]
    same_doc = seg_block[:, None] == seg_block[None, :]
    visible = (same_doc & causal)[:, :, None]
    spread = cumulative[:, None, :] - cumulative[None, :, :]
    weights = jnp.where(visible, jnp.exp(jnp.where(visible, spread, 0.0)), 0.0)
    carried = (seg_block == previous).astype(jnp.float32)
    carry_decay = jnp.exp(cumulative) * carried[:, None]
    key_gram = jnp.einsum("ihd,jhd->ijh", keys, keys, precision=exact_precision)
    lower_part = jnp.where(strict[:, :, None], betas[:, None, :] * weights * key_gram, 0.0)
    inverse = lower_inverse(jnp.transpose(lower_part, (2, 0, 1)), length)
    key_state = jnp.einsum("ihd,hde->ihe", keys, state, precision=exact_precision)
    target_rows = betas[:, :, None] * (values - carry_decay[:, :, None] * key_state)
    pseudo = jnp.einsum("hij,jhe->hie", inverse, target_rows, precision=exact_precision)
    scores = jnp.einsum("ihd,jhd->hij", queries, keys, precision=exact_precision) * jnp.transpose(
        weights, (2, 0, 1)
    )
    query_state = jnp.einsum("ihd,hde->ihe", queries, state, precision=exact_precision)
    outputs = carry_decay[:, :, None] * query_state + jnp.einsum(
        "hij,hje->ihe", scores, pseudo, precision=exact_precision
    )
    last_weights = weights[-1]
    new_state = (carried[-1] * jnp.exp(cumulative[-1]))[:, None, None] * state + jnp.einsum(
        "jh,jhd,hje->hde", last_weights, keys, pseudo, precision=exact_precision
    )
    return (new_state, outputs)


def mixer_sequence(
    q_pre,
    k_pre,
    v_pre,
    g_pre,
    a_pre,
    b_pre,
    segment_ids,
    conv_q,
    conv_k,
    conv_v,
    scale_rate,
    bias_rate,
    out_gain,
):
    length = q_pre.shape[0]
    heads = a_pre.shape[1]
    key_size = q_pre.shape[1] // heads
    value_size = v_pre.shape[1] // heads
    masks = shift_masks(segment_ids, conv_q.shape[0])
    queries = unit_rows(
        jax.nn.silu(short_conv(q_pre, conv_q, masks)).reshape(length, heads, key_size)
    ) * key_size ** (-0.5)
    keys = unit_rows(jax.nn.silu(short_conv(k_pre, conv_k, masks)).reshape(length, heads, key_size))
    values = jax.nn.silu(short_conv(v_pre, conv_v, masks)).reshape(length, heads, value_size)
    betas = jax.nn.sigmoid(b_pre)
    log_decay = -scale_rate * jax.nn.softplus(a_pre + bias_rate)
    blocks = length // CH
    seg_blocks = segment_ids.reshape(blocks, CH)
    previous = jnp.concatenate([jnp.full((1,), -1, jnp.int32), seg_blocks[:-1, -1]])
    state = jnp.zeros((heads, key_size, value_size), jnp.float32)
    carried_in = (
        queries.reshape(blocks, CH, heads, key_size),
        keys.reshape(blocks, CH, heads, key_size),
        values.reshape(blocks, CH, heads, value_size),
        betas.reshape(blocks, CH, heads),
        log_decay.reshape(blocks, CH, heads),
        seg_blocks,
        previous,
    )
    final_state, outputs = lax.scan(jax.checkpoint(block_update), state, carried_in)
    outputs = outputs.reshape(length, heads, value_size)
    gated = rms_scale(outputs, out_gain) * jax.nn.silu(g_pre.reshape(length, heads, value_size))
    return gated.reshape(length, heads * value_size)


def contract_rows(left, right):
    return lax.dot_general(
        left, right, (((0,), (0,)), ((), ())), preferred_element_type=jnp.float32
    )


def contract_cols(left, right):
    return lax.dot_general(
        left, right, (((1,), (1,)), ((), ())), preferred_element_type=jnp.float32
    )


def feed_inputs(normed_rows, gate_weight, up_weight):
    gate_pre = jnp.dot(normed_rows, gate_weight, preferred_element_type=jnp.float32)
    up_pre = jnp.dot(normed_rows, up_weight, preferred_element_type=jnp.float32)
    return (gate_pre, up_pre)


def on_device_split(
    layer_input,
    target,
    segment,
    pad_mask,
    norm1_gain,
    w_query,
    w_key,
    w_value,
    w_gate_out,
    w_decay,
    w_beta,
    conv_query,
    conv_key,
    conv_value,
    decay_scale,
    decay_bias,
    out_norm_gain,
    w_out,
    norm2_gain,
    w_ffn_gate,
    w_ffn_up,
    w_ffn_down,
):
    own_rows, width = layer_input.shape
    group_rows = segment.shape[0]
    sequences = group_rows // LENGTH
    tensor_index = lax.axis_index("tensor")
    heads_local = w_decay.shape[1]
    query_cols = w_query.shape[1]
    value_cols = w_value.shape[1]
    input_float = layer_input.astype(jnp.float32)
    normed_own, norm1_pull = jax.vjp(rms_scale, input_float, norm1_gain)
    normed = lax.all_gather(normed_own.astype(jnp.bfloat16), "tensor", axis=0, tiled=True)
    full_query, full_key, full_value, full_gate, full_decay, full_beta, full_out = (
        lax.all_gather(w_query, "dp", axis=0, tiled=True),
        lax.all_gather(w_key, "dp", axis=0, tiled=True),
        lax.all_gather(w_value, "dp", axis=0, tiled=True),
        lax.all_gather(w_gate_out, "dp", axis=0, tiled=True),
        lax.all_gather(w_decay, "dp", axis=0, tiled=True),
        lax.all_gather(w_beta, "dp", axis=0, tiled=True),
        lax.all_gather(w_out, "dp", axis=0, tiled=True),
    )
    proj_weights = (full_query, full_key, full_value, full_gate, full_decay, full_beta)
    projected = [
        jnp.dot(normed, weight, preferred_element_type=jnp.float32) for weight in proj_weights
    ]
    conv_q_local = lax.dynamic_slice_in_dim(conv_query, tensor_index * query_cols, query_cols, 1)
    conv_k_local = lax.dynamic_slice_in_dim(conv_key, tensor_index * query_cols, query_cols, 1)
    conv_v_local = lax.dynamic_slice_in_dim(conv_value, tensor_index * value_cols, value_cols, 1)
    scale_local = lax.dynamic_slice_in_dim(decay_scale, tensor_index * heads_local, heads_local, 0)
    bias_local = lax.dynamic_slice_in_dim(decay_bias, tensor_index * heads_local, heads_local, 0)
    seg_rows = segment.reshape(sequences, LENGTH)

    def mixer_local(
        q_pre,
        k_pre,
        v_pre,
        g_pre,
        a_pre,
        b_pre,
        conv_q,
        conv_k,
        conv_v,
        scale_rate,
        bias_rate,
        out_gain,
    ):
        shaped = [
            item.reshape(sequences, LENGTH, item.shape[1])
            for item in (q_pre, k_pre, v_pre, g_pre, a_pre, b_pre)
        ]
        mixed_rows = jax.vmap(
            mixer_sequence, in_axes=(0, 0, 0, 0, 0, 0, 0, None, None, None, None, None, None)
        )(*shaped, seg_rows, conv_q, conv_k, conv_v, scale_rate, bias_rate, out_gain)
        return mixed_rows.reshape(group_rows, mixed_rows.shape[2])

    mixed, mixer_pull = jax.vjp(
        mixer_local,
        *projected,
        conv_q_local,
        conv_k_local,
        conv_v_local,
        scale_local,
        bias_local,
        out_norm_gain
    )
    mixed_low = mixed.astype(jnp.bfloat16)
    attention = lax.psum_scatter(
        contract_cols(mixed_low, full_out), "tensor", scatter_dimension=0, tiled=True
    )
    residual = input_float + attention
    normed2_own, norm2_pull = jax.vjp(rms_scale, residual, norm2_gain)
    normed2 = lax.all_gather(normed2_own.astype(jnp.bfloat16), "tensor", axis=0, tiled=True)
    ffn_gate_w, ffn_up_w, ffn_down_w = (
        lax.all_gather(w_ffn_gate, "dp", axis=0, tiled=True),
        lax.all_gather(w_ffn_up, "dp", axis=0, tiled=True),
        lax.all_gather(w_ffn_down, "dp", axis=0, tiled=True),
    )
    gate_pre, up_pre = feed_inputs(normed2, ffn_gate_w, ffn_up_w)
    hidden = (jax.nn.silu(gate_pre) * up_pre).astype(jnp.bfloat16)
    ffn_out = lax.psum_scatter(
        contract_cols(hidden, ffn_down_w).astype(jnp.bfloat16),
        "tensor",
        scatter_dimension=0,
        tiled=True,
    ).astype(jnp.float32)
    output = residual + ffn_out
    live = pad_mask.astype(jnp.float32)
    error = output - target.astype(jnp.float32)
    loss_sum, count = lax.psum(
        (jnp.sum(live[:, None] * error * error), jnp.sum(live)), ("dp", "tensor")
    )
    loss = loss_sum / (count * width)
    all_tokens = own_rows * lax.axis_size("dp") * lax.axis_size("tensor")
    grad_output = error * live[:, None] * (all_tokens / count)
    grad_ffn = lax.all_gather(grad_output.astype(jnp.bfloat16), "tensor", axis=0, tiled=True)
    grad_hidden = jnp.dot(grad_ffn, ffn_down_w, preferred_element_type=jnp.float32)
    sigmoid_gate = jax.nn.sigmoid(gate_pre)
    grad_gate = (
        grad_hidden * up_pre * sigmoid_gate * (1.0 + gate_pre * (1.0 - sigmoid_gate))
    ).astype(jnp.bfloat16)
    grad_up = (grad_hidden * gate_pre * sigmoid_gate).astype(jnp.bfloat16)
    grad_down_local = contract_rows(grad_ffn, hidden)
    grad_gate_local = contract_rows(normed2, grad_gate)
    grad_up_local = contract_rows(normed2, grad_up)
    normed2_part = contract_cols(grad_gate, ffn_gate_w) + contract_cols(grad_up, ffn_up_w)
    grad_normed2 = lax.psum_scatter(
        normed2_part.astype(jnp.bfloat16), "tensor", scatter_dimension=0, tiled=True
    ).astype(jnp.float32)
    grad_residual_norm, grad_gain_two = norm2_pull(grad_normed2)
    grad_residual = grad_output + grad_residual_norm
    grad_attention = lax.all_gather(
        grad_residual.astype(jnp.bfloat16), "tensor", axis=0, tiled=True
    )
    grad_mixed = jnp.dot(grad_attention, full_out, preferred_element_type=jnp.float32)
    grad_out_local = contract_rows(grad_attention, mixed_low)
    mixer_grads = mixer_pull(grad_mixed)
    pre_grads = [item.astype(jnp.bfloat16) for item in mixer_grads[:6]]
    normed_part = contract_cols(pre_grads[0], full_query)
    for grad_item, weight in zip(pre_grads[1:], proj_weights[1:]):
        normed_part = normed_part + contract_cols(grad_item, weight)
    weight_locals = [contract_rows(normed, grad_item) for grad_item in pre_grads]
    grad_normed = lax.psum_scatter(
        normed_part.astype(jnp.bfloat16), "tensor", scatter_dimension=0, tiled=True
    ).astype(jnp.float32)
    grad_input_norm, grad_gain_one = norm1_pull(grad_normed)
    grad_input = grad_residual + grad_input_norm
    owned = (
        lax.psum_scatter(
            grad_gate_local.astype(jnp.bfloat16), "dp", scatter_dimension=0, tiled=True
        ).astype(jnp.float32),
        lax.psum_scatter(
            grad_up_local.astype(jnp.bfloat16), "dp", scatter_dimension=0, tiled=True
        ).astype(jnp.float32),
        lax.psum_scatter(
            grad_down_local.astype(jnp.bfloat16), "dp", scatter_dimension=0, tiled=True
        ).astype(jnp.float32),
        lax.psum_scatter(
            weight_locals[0].astype(jnp.bfloat16), "dp", scatter_dimension=0, tiled=True
        ).astype(jnp.float32),
        lax.psum_scatter(
            weight_locals[1].astype(jnp.bfloat16), "dp", scatter_dimension=0, tiled=True
        ).astype(jnp.float32),
        lax.psum_scatter(
            weight_locals[2].astype(jnp.bfloat16), "dp", scatter_dimension=0, tiled=True
        ).astype(jnp.float32),
        lax.psum_scatter(
            weight_locals[3].astype(jnp.bfloat16), "dp", scatter_dimension=0, tiled=True
        ).astype(jnp.float32),
        lax.psum_scatter(
            weight_locals[4].astype(jnp.bfloat16), "dp", scatter_dimension=0, tiled=True
        ).astype(jnp.float32),
        lax.psum_scatter(
            weight_locals[5].astype(jnp.bfloat16), "dp", scatter_dimension=0, tiled=True
        ).astype(jnp.float32),
        lax.psum_scatter(
            grad_out_local.astype(jnp.bfloat16), "dp", scatter_dimension=0, tiled=True
        ).astype(jnp.float32),
    )
    conv_q_full = lax.dynamic_update_slice_in_dim(
        jnp.zeros_like(conv_query), mixer_grads[6], tensor_index * query_cols, 1
    )
    conv_k_full = lax.dynamic_update_slice_in_dim(
        jnp.zeros_like(conv_key), mixer_grads[7], tensor_index * query_cols, 1
    )
    conv_v_full = lax.dynamic_update_slice_in_dim(
        jnp.zeros_like(conv_value), mixer_grads[8], tensor_index * value_cols, 1
    )
    scale_full = lax.dynamic_update_slice_in_dim(
        jnp.zeros_like(decay_scale), mixer_grads[9], tensor_index * heads_local, 0
    )
    bias_full = lax.dynamic_update_slice_in_dim(
        jnp.zeros_like(decay_bias), mixer_grads[10], tensor_index * heads_local, 0
    )
    summed = lax.psum(
        (
            grad_gain_one,
            grad_gain_two,
            conv_q_full,
            conv_k_full,
            conv_v_full,
            scale_full,
            bias_full,
            mixer_grads[11],
        ),
        ("dp", "tensor"),
    )
    return (
        output,
        loss,
        grad_input,
        summed[0],
        owned[3],
        owned[4],
        owned[5],
        owned[6],
        owned[7],
        owned[8],
        summed[2],
        summed[3],
        summed[4],
        summed[5],
        summed[6],
        summed[7],
        owned[9],
        summed[1],
        owned[0],
        owned[1],
        owned[2],
    )


TILE = 128


def mm(left, right, dims=((1,), (0,))):
    return lax.dot_general(
        left.astype(jnp.bfloat16),
        right.astype(jnp.bfloat16),
        (dims, ((), ())),
        preferred_element_type=jnp.float32,
    )


def mm_nt(left, right):
    return mm(left, right, ((1,), (1,)))


def mm_tn(left, right):
    return mm(left, right, ((0,), (0,)))


def mm_fine(left, right):
    left_high, right_high = left.astype(jnp.bfloat16), right.astype(jnp.bfloat16)
    left_rest = left - left_high.astype(jnp.float32)
    right_rest = right - right_high.astype(jnp.float32)
    return mm(left_high, right_high) + (mm(left_high, right_rest) + mm(left_rest, right_high))


def ones_mm(ones, right):
    high = right.astype(jnp.bfloat16)
    rest = right - high.astype(jnp.float32)
    middle = rest.astype(jnp.bfloat16)
    return mm(ones, high) + (mm(ones, middle) + mm(ones, rest - middle.astype(jnp.float32)))


def unit_lower_inverse(part, row, col):
    size = part.shape[0]
    eye = (row == col).astype(jnp.float32)
    block = 16
    power = jnp.where((row // block) == (col // block), -part, 0.0)
    inverse = eye + power
    covered = 2
    while covered < block:
        power = mm_fine(power, power)
        inverse = inverse + mm_fine(inverse, power)
        covered *= 2
    while block < size:
        pair = (row // (2 * block)) == (col // (2 * block))
        cross = jnp.where(pair & ((row // block) != (col // block)), part, 0.0)
        inverse = inverse - mm(mm(inverse, cross), inverse)
        block *= 2
    return inverse


def stable_softplus(values):
    return jnp.maximum(values, 0.0) + jnp.log1p(jnp.exp(-jnp.abs(values)))


def decay_tiles(raw, rate, bias):
    shifted = raw + bias
    soft = stable_softplus(shifted)
    return shifted, soft, -rate * soft


def grids():
    row = lax.broadcasted_iota(jnp.int32, (TILE, TILE), 0)
    col = lax.broadcasted_iota(jnp.int32, (TILE, TILE), 1)
    return row, col


def forward_body(
    heads,
    proj_ref,
    info_ref,
    conv_ref,
    rates_ref,
    gain_ref,
    mixed_ref,
    conv_out_ref,
    rows_out_ref,
    state_out_ref,
    inverse_out_ref,
    pseudo_out_ref,
    earlier_ref,
    state_ref,
):
    first = pl.program_id(2) == 0
    blocks = 4 * heads

    @pl.when(first)
    def _():
        earlier_ref[:, 0:8, :] = jnp.zeros((blocks, 8, TILE), jnp.float32)
        state_ref[...] = jnp.zeros(state_ref.shape, jnp.float32)

    row, col = grids()
    info = info_ref[...]
    info_rows = info.T
    masks = [jnp.broadcast_to(info[:, j : j + 1], (TILE, TILE)) for j in range(3)]
    visible = (row >= col) & (info[:, 4:5] == info_rows[4:5, :])
    raw = proj_ref[0, :, 6 * heads * TILE : 6 * heads * TILE + TILE]
    _, _, log_decay = decay_tiles(raw, rates_ref[0, 0:1, :], rates_ref[0, 1:2, :])
    total = ones_mm((row >= col).astype(jnp.float32), log_decay)
    total_rows = total.T
    carry = jnp.exp(total) * info[:, 3:4]
    beta_tile = jax.nn.sigmoid(raw)
    for block in range(blocks):
        earlier_ref[block, 8 : 8 + TILE, :] = proj_ref[0, :, block * TILE : (block + 1) * TILE]

    def conv_block(block):
        lanes = slice(block * TILE, (block + 1) * TILE)
        result = earlier_ref[block, 8 : 8 + TILE, :] * conv_ref[0, 0:1, lanes]
        for j in range(1, 4):
            result = result + masks[j - 1] * (
                earlier_ref[block, 8 - j : 8 - j + TILE, :] * conv_ref[0, j : j + 1, lanes]
            )
        conv_out_ref[0, :, lanes] = result
        return result * jax.nn.sigmoid(result)

    for head in range(heads):
        query, key = conv_block(head), conv_block(heads + head)
        query = query * (
            lax.rsqrt(jnp.sum(query * query, axis=1, keepdims=True) + 1e-06) * TILE ** (-0.5)
        )
        key = key * lax.rsqrt(jnp.sum(key * key, axis=1, keepdims=True) + 1e-06)
        value = jnp.concatenate(
            [conv_block(2 * heads + 2 * head), conv_block(2 * heads + 2 * head + 1)], axis=1
        )
        spread = total[:, head : head + 1] - total_rows[head : head + 1, :]
        weights = jnp.exp(jnp.where(visible, spread, -1e30))
        beta = beta_tile[:, heads + head : heads + head + 1]
        carried = carry[:, head : head + 1]
        key_low, query_low = key.astype(jnp.bfloat16), query.astype(jnp.bfloat16)
        both = jnp.concatenate([key_low, query_low], axis=0)
        grams = mm_nt(both, key_low)
        part = jnp.where(row > col, beta * weights * grams[:TILE], 0.0)
        inverse = unit_lower_inverse(part, row, col).astype(jnp.bfloat16)
        state = state_ref[head]
        state_low = state.astype(jnp.bfloat16)
        from_state = mm(both, state_low)
        pseudo = mm(inverse, beta * (value - carried * from_state[:TILE])).astype(jnp.bfloat16)
        rows = carried * from_state[TILE:] + mm(grams[TILE:] * weights, pseudo)
        weighted = key.T * weights[TILE - 1 : TILE, :]
        state_ref[head] = carried[TILE - 1 : TILE, :] * state + mm(weighted, pseudo)
        lanes = slice(2 * head * TILE, 2 * (head + 1) * TILE)
        state_out_ref[0, 0, head] = state_low
        inverse_out_ref[0, 0, head] = inverse
        pseudo_out_ref[0, :, lanes] = pseudo
        rows_out_ref[0, :, lanes] = rows
        gate = proj_ref[
            0, :, (4 * heads + 2 * head) * TILE : (4 * heads + 2 * (head + 1)) * TILE
        ]
        scale = lax.rsqrt(jnp.mean(rows * rows, axis=1, keepdims=True) + 1e-06)
        mixed_ref[:, lanes] = (
            rows * scale * gain_ref[...] * (gate * jax.nn.sigmoid(gate))
        ).astype(jnp.bfloat16)
    for block in range(blocks):
        earlier_ref[block, 0:8, :] = earlier_ref[block, TILE : TILE + 8, :]


def backward_body(
    heads,
    proj_ref,
    info_ref,
    conv_ref,
    rates_ref,
    gain_ref,
    conv_out_ref,
    rows_ref,
    state_in_ref,
    inverse_ref,
    pseudo_ref,
    grad_ref,
    grad_proj_ref,
    grad_conv_ref,
    grad_rates_ref,
    grad_gain_ref,
    later_ref,
    grad_state_ref,
):
    step = pl.program_id(2)
    blocks = 4 * heads

    @pl.when(step == 0)
    def _():
        later_ref[:, TILE : TILE + 8, :] = jnp.zeros((blocks, 8, TILE), jnp.float32)
        grad_state_ref[...] = jnp.zeros(grad_state_ref.shape, jnp.float32)

    @pl.when((step == 0) & (pl.program_id(1) == 0))
    def _():
        grad_conv_ref[...] = jnp.zeros(grad_conv_ref.shape, jnp.float32)
        grad_rates_ref[...] = jnp.zeros(grad_rates_ref.shape, jnp.float32)
        grad_gain_ref[...] = jnp.zeros(grad_gain_ref.shape, jnp.float32)

    row, col = grids()
    info = info_ref[...]
    info_rows = info.T
    masks = [jnp.broadcast_to(info[:, 4 + j : 5 + j], (TILE, TILE)) for j in range(1, 4)]
    visible = (row >= col) & (info[:, 4:5] == info_rows[4:5, :])
    raw = proj_ref[0, :, 6 * heads * TILE : 6 * heads * TILE + TILE]
    rate = rates_ref[0, 0:1, :]
    shifted, soft, log_decay = decay_tiles(raw, rate, rates_ref[0, 1:2, :])
    total = ones_mm((row >= col).astype(jnp.float32), log_decay)
    total_rows = total.T
    carry = jnp.exp(total) * info[:, 3:4]
    beta_tile = jax.nn.sigmoid(raw)
    grad_total = jnp.zeros((TILE, TILE), jnp.float32)
    grad_beta = jnp.zeros((TILE, TILE), jnp.float32)
    gain = gain_ref[...]
    gain_sum = jnp.zeros((1, 2 * TILE), jnp.float32)

    def activation(block):
        value = conv_out_ref[0, :, block * TILE : (block + 1) * TILE]
        gate = jax.nn.sigmoid(value)
        return value * gate, gate * (1.0 + value * (1.0 - gate))

    def close_block(block, grad):
        later_ref[block, 0:TILE, :] = grad
        lanes = slice(block * TILE, (block + 1) * TILE)
        own = proj_ref[0, :, lanes]
        result = grad * conv_ref[0, 0:1, lanes]
        sums = [jnp.sum(grad * own, axis=0, keepdims=True)]
        for j in range(1, 4):
            moved = masks[j - 1] * later_ref[block, j : j + TILE, :]
            result = result + moved * conv_ref[0, j : j + 1, lanes]
            sums.append(jnp.sum(moved * own, axis=0, keepdims=True))
        grad_proj_ref[0, :, lanes] = result.astype(jnp.bfloat16)
        for j in range(4):
            grad_conv_ref[0, j : j + 1, lanes] += sums[j]

    for head in range(heads):
        lanes = slice(2 * head * TILE, 2 * (head + 1) * TILE)
        gate_lanes = slice((4 * heads + 2 * head) * TILE, (4 * heads + 2 * (head + 1)) * TILE)
        rows = rows_ref[0, :, lanes]
        gate = proj_ref[0, :, gate_lanes]
        grad = grad_ref[:, lanes]
        scale = lax.rsqrt(jnp.mean(rows * rows, axis=1, keepdims=True) + 1e-06)
        level = rows * scale
        sigmoid = jax.nn.sigmoid(gate)
        through = grad * (gate * sigmoid)
        gain_sum = gain_sum + jnp.sum(through * level, axis=0, keepdims=True)
        grad_proj_ref[0, :, gate_lanes] = (
            grad * level * gain * (sigmoid * (1.0 + gate * (1.0 - sigmoid)))
        ).astype(jnp.bfloat16)
        through = through * gain
        grad_rows = scale * (
            through - level * jnp.mean(through * level, axis=1, keepdims=True)
        )

        query_act, query_slope = activation(head)
        query_scale = lax.rsqrt(jnp.sum(query_act * query_act, axis=1, keepdims=True) + 1e-06)
        query_unit = query_act * query_scale
        query = query_unit * TILE ** (-0.5)
        key_act, key_slope = activation(heads + head)
        key_scale = lax.rsqrt(jnp.sum(key_act * key_act, axis=1, keepdims=True) + 1e-06)
        key = key_act * key_scale
        value_parts = [activation(2 * heads + 2 * head), activation(2 * heads + 2 * head + 1)]
        value = jnp.concatenate([value_parts[0][0], value_parts[1][0]], axis=1)

        spread = total[:, head : head + 1] - total_rows[head : head + 1, :]
        weights = jnp.exp(jnp.where(visible, spread, -1e30))
        beta = beta_tile[:, heads + head : heads + head + 1]
        carried = carry[:, head : head + 1]
        key_low, query_low = key.astype(jnp.bfloat16), query.astype(jnp.bfloat16)
        both = jnp.concatenate([key_low, query_low], axis=0)
        grams = mm_nt(both, key_low)
        state_low = state_in_ref[0, 0, head]
        inverse = inverse_ref[0, 0, head]
        pseudo = pseudo_ref[0, :, lanes]
        grad_state = grad_state_ref[head]
        grad_state_low = grad_state.astype(jnp.bfloat16)
        last_row = weights[TILE - 1 : TILE, :]
        last_col = jnp.sum(jnp.where(row == col, last_row, 0.0), axis=1, keepdims=True)
        grad_rows_low = grad_rows.astype(jnp.bfloat16)
        grad_pseudo = mm_tn(grams[TILE:] * weights, grad_rows_low) + mm(
            last_col * key, grad_state_low
        )
        solved = mm_tn(inverse, grad_pseudo)
        crossed = mm_nt(
            jnp.concatenate([grad_rows_low, solved.astype(jnp.bfloat16)], axis=0), pseudo
        )
        grad_scores = crossed[:TILE] * weights
        below = jnp.where(row > col, crossed[TILE:] * weights, 0.0)
        grad_gram = (-beta) * below
        grad_value = beta * solved
        from_state = mm(key_low, state_low)
        grad_beta_col = jnp.sum(
            solved * (value - carried * from_state), axis=1, keepdims=True
        ) - jnp.sum(below * grams[:TILE], axis=1, keepdims=True)
        out_part = (carried * grad_rows).astype(jnp.bfloat16)
        key_part = ((-carried) * grad_value).astype(jnp.bfloat16)
        stacked = jnp.concatenate([out_part, key_part], axis=0)
        to_inputs = mm_nt(stacked, state_low)
        scores_low, gram_low = grad_scores.astype(jnp.bfloat16), grad_gram.astype(jnp.bfloat16)
        grad_query = mm(scores_low, key_low) + to_inputs[:TILE]
        key_own = mm(gram_low, key_low) + to_inputs[TILE:]
        key_rest = mm_tn(
            jnp.concatenate([gram_low, scores_low], axis=0), both
        )
        key_state = last_col * mm_nt(pseudo, grad_state_low)
        grad_key = key_own + key_rest + key_state
        grad_state_ref[head] = carried[TILE - 1 : TILE, :] * grad_state + mm_tn(
            jnp.concatenate([query_low, key_low], axis=0), stacked
        )
        key_exact, query_exact = key_low.astype(jnp.float32), query_low.astype(jnp.float32)
        state_dot = jnp.sum(key_state * key_exact, axis=1, keepdims=True)
        tail = jnp.sum(state_dot, axis=0, keepdims=True) + carried[TILE - 1 : TILE, :] * jnp.sum(
            jnp.sum(grad_state * state_low.astype(jnp.float32), axis=1, keepdims=True),
            axis=0,
            keepdims=True,
        )
        grad_total_col = (
            jnp.sum(
                grad_query * query_exact + (key_own - key_rest) * key_exact, axis=1, keepdims=True
            )
            - state_dot
            + jnp.where(row[:, 0:1] == TILE - 1, tail, 0.0)
        )
        grad_total = jnp.where(col == head, grad_total_col, grad_total)
        grad_beta = jnp.where(col == heads + head, grad_beta_col, grad_beta)

        grad_query = grad_query * TILE ** (-0.5)
        close_block(
            head,
            query_scale
            * (
                grad_query
                - query_unit * jnp.sum(grad_query * query_unit, axis=1, keepdims=True)
            )
            * query_slope,
        )
        close_block(
            heads + head,
            key_scale
            * (grad_key - key * jnp.sum(grad_key * key, axis=1, keepdims=True))
            * key_slope,
        )
        close_block(2 * heads + 2 * head, grad_value[:, :TILE] * value_parts[0][1])
        close_block(2 * heads + 2 * head + 1, grad_value[:, TILE:] * value_parts[1][1])

    grad_log = ones_mm((row <= col).astype(jnp.float32), grad_total)
    grad_raw = -rate * grad_log * jax.nn.sigmoid(shifted)
    grad_rates_ref[0, 0:1, :] += -jnp.sum(grad_log * soft, axis=0, keepdims=True)
    grad_rates_ref[0, 1:2, :] += jnp.sum(grad_raw, axis=0, keepdims=True)
    grad_gain_ref[0, 0:1, :] += gain_sum
    grad_proj_ref[0, :, 6 * heads * TILE : 6 * heads * TILE + TILE] = jnp.where(
        col < heads, grad_raw, grad_beta * beta_tile * (1.0 - beta_tile)
    ).astype(jnp.bfloat16)
    for block in range(blocks):
        later_ref[block, TILE : TILE + 8, :] = later_ref[block, 0:8, :]


def mixer_specs(parts, rows, wide, heads, blocks, backward):
    conv_cols, value_cols = 4 * heads * TILE, 2 * heads * TILE

    def place(s, c):
        return s * blocks + ((blocks - 1 - c) if backward else c)

    return dict(
        proj=pl.BlockSpec((1, TILE, wide), lambda p, s, c: (p, place(s, c), 0)),
        info=pl.BlockSpec((TILE, TILE), lambda p, s, c: (place(s, c), 0)),
        conv=pl.BlockSpec((1, 8, conv_cols), lambda p, s, c: (p, 0, 0)),
        rates=pl.BlockSpec((1, 8, TILE), lambda p, s, c: (p, 0, 0)),
        gain=pl.BlockSpec((1, 2 * TILE), lambda p, s, c: (0, 0)),
        flat=pl.BlockSpec((TILE, value_cols), lambda p, s, c: (place(s, c), p)),
        conv_out=pl.BlockSpec((1, TILE, conv_cols), lambda p, s, c: (p, place(s, c), 0)),
        value=pl.BlockSpec((1, TILE, value_cols), lambda p, s, c: (p, place(s, c), 0)),
        state=pl.BlockSpec(
            (1, 1, heads, TILE, 2 * TILE), lambda p, s, c: (p, place(s, c), 0, 0, 0)
        ),
        inverse=pl.BlockSpec(
            (1, 1, heads, TILE, TILE), lambda p, s, c: (p, place(s, c), 0, 0, 0)
        ),
        gain_sum=pl.BlockSpec((1, 8, 2 * TILE), lambda p, s, c: (p, 0, 0)),
    )


def mixer_forward(proj, info, conv, rates, gain, heads):
    parts, rows, wide = proj.shape
    blocks = LENGTH // TILE
    spec = mixer_specs(parts, rows, wide, heads, blocks, False)
    conv_cols, value_cols = 4 * heads * TILE, 2 * heads * TILE
    low, full = jnp.bfloat16, jnp.float32
    return pl.pallas_call(
        functools.partial(forward_body, heads),
        grid=(parts, rows // LENGTH, blocks),
        in_specs=[spec[n] for n in ("proj", "info", "conv", "rates", "gain")],
        out_specs=[
            spec[n] for n in ("flat", "conv_out", "value", "state", "inverse", "value")
        ],
        out_shape=[
            jax.ShapeDtypeStruct((rows, parts * value_cols), low),
            jax.ShapeDtypeStruct((parts, rows, conv_cols), full),
            jax.ShapeDtypeStruct((parts, rows, value_cols), full),
            jax.ShapeDtypeStruct((parts, rows // TILE, heads, TILE, 2 * TILE), low),
            jax.ShapeDtypeStruct((parts, rows // TILE, heads, TILE, TILE), low),
            jax.ShapeDtypeStruct((parts, rows, value_cols), low),
        ],
        scratch_shapes=[
            pltpu.VMEM((4 * heads, TILE + 8, TILE), full),
            pltpu.VMEM((heads, TILE, 2 * TILE), full),
        ],
        compiler_params=pltpu.CompilerParams(
            dimension_semantics=("arbitrary", "arbitrary", "arbitrary"),
            vmem_limit_bytes=48 * 1024 * 1024,
        ),
        name="mixer_forward",
    )(proj, info, conv, rates, gain)


def mixer_backward(proj, info, conv, rates, gain, saved, grad, heads):
    parts, rows, wide = proj.shape
    blocks = LENGTH // TILE
    spec = mixer_specs(parts, rows, wide, heads, blocks, True)
    conv_cols = 4 * heads * TILE
    low, full = jnp.bfloat16, jnp.float32
    return pl.pallas_call(
        functools.partial(backward_body, heads),
        grid=(parts, rows // LENGTH, blocks),
        in_specs=[
            spec[n]
            for n in (
                "proj", "info", "conv", "rates", "gain",
                "conv_out", "value", "state", "inverse", "value", "flat",
            )
        ],
        out_specs=[spec[n] for n in ("proj", "conv", "rates", "gain_sum")],
        out_shape=[
            jax.ShapeDtypeStruct((parts, rows, wide), low),
            jax.ShapeDtypeStruct((parts, 8, conv_cols), full),
            jax.ShapeDtypeStruct((parts, 8, TILE), full),
            jax.ShapeDtypeStruct((parts, 8, 2 * TILE), full),
        ],
        scratch_shapes=[
            pltpu.VMEM((4 * heads, TILE + 8, TILE), full),
            pltpu.VMEM((heads, TILE, 2 * TILE), full),
        ],
        compiler_params=pltpu.CompilerParams(
            dimension_semantics=("arbitrary", "arbitrary", "arbitrary"),
            vmem_limit_bytes=48 * 1024 * 1024,
        ),
        name="mixer_backward",
    )(proj, info, conv, rates, gain, *saved, grad)


def token_info(seg):
    sequences, length = seg.shape
    lanes = []
    for j in range(1, 4):
        lanes.append(jnp.pad(seg[:, j:] == seg[:, :-j], ((0, 0), (j, 0))))
    ends = seg.reshape(sequences, length // TILE, TILE)
    before = jnp.pad(ends[:, :-1, -1], ((0, 0), (1, 0)), constant_values=-1)
    lanes.append((ends == before[:, :, None]).reshape(sequences, length))
    lanes.append(seg)
    for j in range(1, 4):
        lanes.append(jnp.pad(seg[:, j:] == seg[:, :-j], ((0, 0), (0, j))))
    table = jnp.stack([item.astype(jnp.float32).reshape(-1) for item in lanes], axis=1)
    return jnp.pad(table, ((0, 0), (0, TILE - table.shape[1])))


def gather_all(local):
    rows = lax.all_gather(local, ("tensor", "dp"), axis=0, tiled=True)
    shares = lax.axis_size("tensor")
    return rows.reshape(shares, rows.shape[0] // shares, rows.shape[1])


def scatter_all(parts):
    shares, rows, cols = parts.shape
    return lax.psum_scatter(
        parts.reshape(shares * rows, cols), ("tensor", "dp"), scatter_dimension=0, tiled=True
    ).astype(jnp.float32)


def columns(array, sizes):
    pieces, start = [], 0
    for size in sizes:
        pieces.append(array[..., start : start + size])
        start += size
    return pieces


def on_device_whole(
    layer_input,
    target,
    segment,
    pad_mask,
    norm1_gain,
    w_query,
    w_key,
    w_value,
    w_gate_out,
    w_decay,
    w_beta,
    conv_query,
    conv_key,
    conv_value,
    decay_scale,
    decay_bias,
    out_norm_gain,
    w_out,
    norm2_gain,
    w_ffn_gate,
    w_ffn_up,
    w_ffn_down,
):
    own_rows, width = layer_input.shape
    shares = lax.axis_size("tensor")
    sequences = own_rows // LENGTH
    tensor_index = lax.axis_index("tensor")
    low = jnp.bfloat16
    proj_local = (w_query, w_key, w_value, w_gate_out, w_decay, w_beta)
    proj_sizes = [item.shape[1] for item in proj_local]
    used = sum(proj_sizes)
    padded = -(-used // 128) * 128
    proj_all = gather_all(
        jnp.concatenate(proj_local + (jnp.zeros((w_query.shape[0], padded - used), low),), axis=1)
    )
    rest_local = (w_out, w_ffn_gate, w_ffn_up, w_ffn_down)
    rest_sizes = [item.shape[1] for item in rest_local]
    rest_all = gather_all(jnp.concatenate(rest_local, axis=1))
    out_all, gate_all, up_all, down_all = columns(rest_all, rest_sizes)
    live = pad_mask.astype(jnp.float32)
    count = lax.psum(jnp.sum(live), ("dp", "tensor"))
    input_float = layer_input.astype(jnp.float32)
    normed_float, norm1_pull = jax.vjp(rms_scale, input_float, norm1_gain)
    normed = normed_float.astype(low)
    seg_rows = lax.dynamic_slice_in_dim(segment, tensor_index * own_rows, own_rows, 0).reshape(
        sequences, LENGTH
    )
    proj = jnp.stack(
        [
            jnp.dot(normed, proj_all[part], preferred_element_type=jnp.float32)
            for part in range(shares)
        ]
    )
    heads = w_decay.shape[1]
    info = token_info(seg_rows)

    def by_part(item):
        return item.reshape(item.shape[0], shares, item.shape[1] // shares).transpose(1, 0, 2)

    conv = jnp.pad(
        jnp.concatenate([by_part(c) for c in (conv_query, conv_key, conv_value)], axis=2),
        ((0, 0), (0, 4), (0, 0)),
    )
    rates = jnp.pad(
        by_part(jnp.stack([decay_scale, decay_bias])), ((0, 0), (0, 6), (0, TILE - heads))
    )
    gain = out_norm_gain.reshape(1, -1)
    mixed_low, *saved = mixer_forward(proj, info, conv, rates, gain, heads)
    value_cols = w_value.shape[1]
    residual = input_float
    for part in range(shares):
        residual = residual + contract_cols(
            mixed_low[:, part * value_cols : (part + 1) * value_cols], out_all[part]
        )
    normed2_float, norm2_pull = jax.vjp(rms_scale, residual, norm2_gain)
    normed2 = normed2_float.astype(low)
    output = residual
    kept = []
    for part in range(shares):
        gate_pre, up_pre = feed_inputs(normed2, gate_all[part], up_all[part])
        hidden = (jax.nn.silu(gate_pre) * up_pre).astype(low)
        output = output + contract_cols(hidden, down_all[part])
        kept.append((gate_pre, up_pre, hidden))
    error = output - target.astype(jnp.float32)
    loss_sum = jnp.sum(live[:, None] * error * error)
    all_tokens = own_rows * lax.axis_size("dp") * lax.axis_size("tensor")
    grad_output = error * live[:, None] * (all_tokens / count)
    grad_ffn = grad_output.astype(low)
    grad_normed2 = jnp.zeros_like(residual)
    ffn_grads = []
    for part in range(shares):
        gate_pre, up_pre, hidden = kept[part]
        grad_hidden = jnp.dot(grad_ffn, down_all[part], preferred_element_type=jnp.float32)
        sigmoid_gate = jax.nn.sigmoid(gate_pre)
        grad_gate = (
            grad_hidden * up_pre * sigmoid_gate * (1.0 + gate_pre * (1.0 - sigmoid_gate))
        ).astype(low)
        grad_up = (grad_hidden * gate_pre * sigmoid_gate).astype(low)
        grad_normed2 = (
            grad_normed2
            + contract_cols(grad_gate, gate_all[part])
            + contract_cols(grad_up, up_all[part])
        )
        ffn_grads.append(
            (
                contract_rows(normed2, grad_gate),
                contract_rows(normed2, grad_up),
                contract_rows(grad_ffn, hidden),
            )
        )
    grad_residual_norm, grad_gain_two = norm2_pull(grad_normed2)
    grad_residual = grad_output + grad_residual_norm
    grad_attention = grad_residual.astype(low)
    grad_mixed = jnp.concatenate(
        [
            jnp.dot(grad_attention, out_all[part], preferred_element_type=jnp.float32)
            for part in range(shares)
        ],
        axis=1,
    )
    rest_grads = jnp.stack(
        [
            jnp.concatenate(
                [
                    item.astype(low)
                    for item in (
                        contract_rows(
                            grad_attention,
                            mixed_low[:, part * value_cols : (part + 1) * value_cols],
                        ),
                    )
                    + ffn_grads[part]
                ],
                axis=1,
            )
            for part in range(shares)
        ]
    )
    own_out, own_gate, own_up, own_down = columns(scatter_all(rest_grads), rest_sizes)
    grad_proj, grad_conv, grad_rates, grad_gain = mixer_backward(
        proj, info, conv, rates, gain, saved, grad_mixed, heads
    )
    grad_normed = jnp.zeros_like(residual)
    proj_grads = []
    for part in range(shares):
        grad_normed = grad_normed + contract_cols(grad_proj[part], proj_all[part])
        proj_grads.append(contract_rows(normed, grad_proj[part]).astype(low))

    def from_part(item):
        return item.transpose(1, 0, 2).reshape(item.shape[1], -1)

    query_cols = w_query.shape[1]
    mixer_grads = [
        from_part(item)
        for item in columns(grad_conv[:, :4], (query_cols, query_cols, value_cols))
    ] + [
        grad_rates[:, 0, :heads].reshape(-1),
        grad_rates[:, 1, :heads].reshape(-1),
        jnp.sum(grad_gain[:, 0], axis=0),
    ]
    own_proj = columns(scatter_all(jnp.stack(proj_grads)), proj_sizes)
    grad_input_norm, grad_gain_one = norm1_pull(grad_normed)
    grad_input = grad_residual + grad_input_norm
    summed = lax.psum(
        (grad_gain_one, grad_gain_two) + tuple(mixer_grads) + (loss_sum,), ("dp", "tensor")
    )
    loss = summed[8] / (count * width)
    return (
        output,
        loss,
        grad_input,
        summed[0],
        *own_proj,
        summed[2],
        summed[3],
        summed[4],
        summed[5],
        summed[6],
        summed[7],
        own_out,
        summed[1],
        own_gate,
        own_up,
        own_down,
    )


def on_device(layer_input, *others):
    whole = layer_input.shape[0] % LENGTH == 0
    return (on_device_whole if whole else on_device_split)(layer_input, *others)


def solution(mesh):
    return jax.shard_map(
        on_device,
        mesh=mesh,
        in_specs=(
            P(("dp", "tensor"), None),
            P(("dp", "tensor"), None),
            P("dp"),
            P(("dp", "tensor")),
            P(),
            P("dp", "tensor"),
            P("dp", "tensor"),
            P("dp", "tensor"),
            P("dp", "tensor"),
            P("dp", "tensor"),
            P("dp", "tensor"),
            P(),
            P(),
            P(),
            P(),
            P(),
            P(),
            P("dp", "tensor"),
            P(),
            P("dp", "tensor"),
            P("dp", "tensor"),
            P("dp", "tensor"),
        ),
        out_specs=(
            P(("dp", "tensor"), None),
            P(),
            P(("dp", "tensor"), None),
            P(),
            P("dp", "tensor"),
            P("dp", "tensor"),
            P("dp", "tensor"),
            P("dp", "tensor"),
            P("dp", "tensor"),
            P("dp", "tensor"),
            P(),
            P(),
            P(),
            P(),
            P(),
            P(),
            P("dp", "tensor"),
            P(),
            P("dp", "tensor"),
            P("dp", "tensor"),
            P("dp", "tensor"),
        ),
        check_vma=False,
    )
```

```python
import functools
from types import SimpleNamespace

import jax
import jax.numpy as jnp
from jax import lax
from jax.experimental import pallas as pl
from jax.experimental.pallas import tpu as pltpu
from jax.sharding import PartitionSpec as P

CH = 64
LENGTH = 1024


DP, TP = "dp", "tensor"
exact_precision = lax.Precision.HIGHEST


def rms_scale(values, gain):
    return values * lax.rsqrt(jnp.mean(values * values, axis=-1, keepdims=True) + 1e-06) * gain


def shift_masks(segment_ids, taps):
    masks = [jnp.ones(segment_ids.shape, jnp.float32)]
    for offset in range(1, taps):
        earlier = jnp.concatenate([jnp.full((offset,), -1, jnp.int32), segment_ids[:-offset]])
        masks.append((segment_ids == earlier).astype(jnp.float32))
    return masks


def short_conv(values, kernel, masks):
    result = values * kernel[0]
    for offset in range(1, len(masks)):
        shifted = jnp.concatenate(
            [jnp.zeros((offset, values.shape[1]), jnp.float32), values[:-offset]]
        )
        result = result + shifted * masks[offset][:, None] * kernel[offset]
    return result


def unit_rows(values):
    return values * lax.rsqrt(jnp.sum(values * values, axis=-1, keepdims=True) + 1e-06)


def lower_inverse(lower_part, length):
    negative = -lower_part
    inverse = jnp.eye(length, dtype=jnp.float32) + negative
    power = negative
    covered = 2
    while covered < length:
        power = jnp.einsum("hij,hjk->hik", power, power, precision=exact_precision)
        inverse = inverse + jnp.einsum("hij,hjk->hik", inverse, power, precision=exact_precision)
        covered = covered * 2
    return inverse


def block_update(state, inputs):
    queries, keys, values, betas, log_decay, seg_block, previous = inputs
    length = queries.shape[0]
    cumulative = jnp.cumsum(log_decay, axis=0)
    order = jnp.arange(length)
    causal = order[:, None] >= order[None, :]
    strict = order[:, None] > order[None, :]
    same_doc = seg_block[:, None] == seg_block[None, :]
    visible = (same_doc & causal)[:, :, None]
    spread = cumulative[:, None, :] - cumulative[None, :, :]
    weights = jnp.where(visible, jnp.exp(jnp.where(visible, spread, 0.0)), 0.0)
    carried = (seg_block == previous).astype(jnp.float32)
    carry_decay = jnp.exp(cumulative) * carried[:, None]
    key_gram = jnp.einsum("ihd,jhd->ijh", keys, keys, precision=exact_precision)
    lower_part = jnp.where(strict[:, :, None], betas[:, None, :] * weights * key_gram, 0.0)
    inverse = lower_inverse(jnp.transpose(lower_part, (2, 0, 1)), length)
    key_state = jnp.einsum("ihd,hde->ihe", keys, state, precision=exact_precision)
    target_rows = betas[:, :, None] * (values - carry_decay[:, :, None] * key_state)
    pseudo = jnp.einsum("hij,jhe->hie", inverse, target_rows, precision=exact_precision)
    scores = jnp.einsum("ihd,jhd->hij", queries, keys, precision=exact_precision) * jnp.transpose(
        weights, (2, 0, 1)
    )
    query_state = jnp.einsum("ihd,hde->ihe", queries, state, precision=exact_precision)
    outputs = carry_decay[:, :, None] * query_state + jnp.einsum(
        "hij,hje->ihe", scores, pseudo, precision=exact_precision
    )
    last_weights = weights[-1]
    new_state = (carried[-1] * jnp.exp(cumulative[-1]))[:, None, None] * state + jnp.einsum(
        "jh,jhd,hje->hde", last_weights, keys, pseudo, precision=exact_precision
    )
    return (new_state, outputs)


def mixer_sequence(
    q_pre,
    k_pre,
    v_pre,
    g_pre,
    a_pre,
    b_pre,
    segment_ids,
    conv_q,
    conv_k,
    conv_v,
    scale_rate,
    bias_rate,
    out_gain,
):
    length = q_pre.shape[0]
    heads = a_pre.shape[1]
    key_size = q_pre.shape[1] // heads
    value_size = v_pre.shape[1] // heads
    masks = shift_masks(segment_ids, conv_q.shape[0])
    queries = unit_rows(
        jax.nn.silu(short_conv(q_pre, conv_q, masks)).reshape(length, heads, key_size)
    ) * key_size ** (-0.5)
    keys = unit_rows(jax.nn.silu(short_conv(k_pre, conv_k, masks)).reshape(length, heads, key_size))
    values = jax.nn.silu(short_conv(v_pre, conv_v, masks)).reshape(length, heads, value_size)
    betas = jax.nn.sigmoid(b_pre)
    log_decay = -scale_rate * jax.nn.softplus(a_pre + bias_rate)
    blocks = length // CH
    seg_blocks = segment_ids.reshape(blocks, CH)
    previous = jnp.concatenate([jnp.full((1,), -1, jnp.int32), seg_blocks[:-1, -1]])
    state = jnp.zeros((heads, key_size, value_size), jnp.float32)
    carried_in = (
        queries.reshape(blocks, CH, heads, key_size),
        keys.reshape(blocks, CH, heads, key_size),
        values.reshape(blocks, CH, heads, value_size),
        betas.reshape(blocks, CH, heads),
        log_decay.reshape(blocks, CH, heads),
        seg_blocks,
        previous,
    )
    final_state, outputs = lax.scan(jax.checkpoint(block_update), state, carried_in)
    outputs = outputs.reshape(length, heads, value_size)
    gated = rms_scale(outputs, out_gain) * jax.nn.silu(g_pre.reshape(length, heads, value_size))
    return gated.reshape(length, heads * value_size)


def contract_rows(left, right):
    return lax.dot_general(
        left, right, (((0,), (0,)), ((), ())), preferred_element_type=jnp.float32
    )


def contract_cols(left, right):
    return lax.dot_general(
        left, right, (((1,), (1,)), ((), ())), preferred_element_type=jnp.float32
    )


def feed_inputs(normed_rows, gate_weight, up_weight):
    gate_pre = jnp.dot(normed_rows, gate_weight, preferred_element_type=jnp.float32)
    up_pre = jnp.dot(normed_rows, up_weight, preferred_element_type=jnp.float32)
    return (gate_pre, up_pre)


def on_device_split(
    layer_input,
    target,
    segment,
    pad_mask,
    norm1_gain,
    w_query,
    w_key,
    w_value,
    w_gate_out,
    w_decay,
    w_beta,
    conv_query,
    conv_key,
    conv_value,
    decay_scale,
    decay_bias,
    out_norm_gain,
    w_out,
    norm2_gain,
    w_ffn_gate,
    w_ffn_up,
    w_ffn_down,
):
    own_rows, width = layer_input.shape
    group_rows = segment.shape[0]
    sequences = group_rows // LENGTH
    tensor_index = lax.axis_index(TP)
    heads_local = w_decay.shape[1]
    query_cols = w_query.shape[1]
    value_cols = w_value.shape[1]
    input_float = layer_input.astype(jnp.float32)
    normed_own, norm1_pull = jax.vjp(rms_scale, input_float, norm1_gain)
    normed = lax.all_gather(normed_own.astype(jnp.bfloat16), TP, axis=0, tiled=True)
    full_query, full_key, full_value, full_gate, full_decay, full_beta, full_out = (
        lax.all_gather(w_query, DP, axis=0, tiled=True),
        lax.all_gather(w_key, DP, axis=0, tiled=True),
        lax.all_gather(w_value, DP, axis=0, tiled=True),
        lax.all_gather(w_gate_out, DP, axis=0, tiled=True),
        lax.all_gather(w_decay, DP, axis=0, tiled=True),
        lax.all_gather(w_beta, DP, axis=0, tiled=True),
        lax.all_gather(w_out, DP, axis=0, tiled=True),
    )
    proj_weights = (full_query, full_key, full_value, full_gate, full_decay, full_beta)
    projected = [
        jnp.dot(normed, weight, preferred_element_type=jnp.float32) for weight in proj_weights
    ]
    conv_q_local = lax.dynamic_slice_in_dim(conv_query, tensor_index * query_cols, query_cols, 1)
    conv_k_local = lax.dynamic_slice_in_dim(conv_key, tensor_index * query_cols, query_cols, 1)
    conv_v_local = lax.dynamic_slice_in_dim(conv_value, tensor_index * value_cols, value_cols, 1)
    scale_local = lax.dynamic_slice_in_dim(decay_scale, tensor_index * heads_local, heads_local, 0)
    bias_local = lax.dynamic_slice_in_dim(decay_bias, tensor_index * heads_local, heads_local, 0)
    seg_rows = segment.reshape(sequences, LENGTH)

    def mixer_local(
        q_pre,
        k_pre,
        v_pre,
        g_pre,
        a_pre,
        b_pre,
        conv_q,
        conv_k,
        conv_v,
        scale_rate,
        bias_rate,
        out_gain,
    ):
        shaped = [
            item.reshape(sequences, LENGTH, item.shape[1])
            for item in (q_pre, k_pre, v_pre, g_pre, a_pre, b_pre)
        ]
        mixed_rows = jax.vmap(
            mixer_sequence, in_axes=(0, 0, 0, 0, 0, 0, 0, None, None, None, None, None, None)
        )(*shaped, seg_rows, conv_q, conv_k, conv_v, scale_rate, bias_rate, out_gain)
        return mixed_rows.reshape(group_rows, mixed_rows.shape[2])

    mixed, mixer_pull = jax.vjp(
        mixer_local,
        *projected,
        conv_q_local,
        conv_k_local,
        conv_v_local,
        scale_local,
        bias_local,
        out_norm_gain
    )
    mixed_low = mixed.astype(jnp.bfloat16)
    attention = lax.psum_scatter(
        contract_cols(mixed_low, full_out), TP, scatter_dimension=0, tiled=True
    )
    residual = input_float + attention
    normed2_own, norm2_pull = jax.vjp(rms_scale, residual, norm2_gain)
    normed2 = lax.all_gather(normed2_own.astype(jnp.bfloat16), TP, axis=0, tiled=True)
    ffn_gate_w, ffn_up_w, ffn_down_w = (
        lax.all_gather(w_ffn_gate, DP, axis=0, tiled=True),
        lax.all_gather(w_ffn_up, DP, axis=0, tiled=True),
        lax.all_gather(w_ffn_down, DP, axis=0, tiled=True),
    )
    gate_pre, up_pre = feed_inputs(normed2, ffn_gate_w, ffn_up_w)
    hidden = (jax.nn.silu(gate_pre) * up_pre).astype(jnp.bfloat16)
    ffn_out = lax.psum_scatter(
        contract_cols(hidden, ffn_down_w).astype(jnp.bfloat16),
        TP,
        scatter_dimension=0,
        tiled=True,
    ).astype(jnp.float32)
    output = residual + ffn_out
    live = pad_mask.astype(jnp.float32)
    error = output - target.astype(jnp.float32)
    loss_sum, count = lax.psum(
        (jnp.sum(live[:, None] * error * error), jnp.sum(live)), (DP, TP)
    )
    loss = loss_sum / (count * width)
    all_tokens = own_rows * lax.axis_size(DP) * lax.axis_size(TP)
    grad_output = error * live[:, None] * (all_tokens / count)
    grad_ffn = lax.all_gather(grad_output.astype(jnp.bfloat16), TP, axis=0, tiled=True)
    grad_hidden = jnp.dot(grad_ffn, ffn_down_w, preferred_element_type=jnp.float32)
    sigmoid_gate = jax.nn.sigmoid(gate_pre)
    grad_gate = (
        grad_hidden * up_pre * sigmoid_gate * (1.0 + gate_pre * (1.0 - sigmoid_gate))
    ).astype(jnp.bfloat16)
    grad_up = (grad_hidden * gate_pre * sigmoid_gate).astype(jnp.bfloat16)
    grad_down_local = contract_rows(grad_ffn, hidden)
    grad_gate_local = contract_rows(normed2, grad_gate)
    grad_up_local = contract_rows(normed2, grad_up)
    normed2_part = contract_cols(grad_gate, ffn_gate_w) + contract_cols(grad_up, ffn_up_w)
    grad_normed2 = lax.psum_scatter(
        normed2_part.astype(jnp.bfloat16), TP, scatter_dimension=0, tiled=True
    ).astype(jnp.float32)
    grad_residual_norm, grad_gain_two = norm2_pull(grad_normed2)
    grad_residual = grad_output + grad_residual_norm
    grad_attention = lax.all_gather(
        grad_residual.astype(jnp.bfloat16), TP, axis=0, tiled=True
    )
    grad_mixed = jnp.dot(grad_attention, full_out, preferred_element_type=jnp.float32)
    grad_out_local = contract_rows(grad_attention, mixed_low)
    mixer_grads = mixer_pull(grad_mixed)
    pre_grads = [item.astype(jnp.bfloat16) for item in mixer_grads[:6]]
    normed_part = contract_cols(pre_grads[0], full_query)
    for grad_item, weight in zip(pre_grads[1:], proj_weights[1:]):
        normed_part = normed_part + contract_cols(grad_item, weight)
    weight_locals = [contract_rows(normed, grad_item) for grad_item in pre_grads]
    grad_normed = lax.psum_scatter(
        normed_part.astype(jnp.bfloat16), TP, scatter_dimension=0, tiled=True
    ).astype(jnp.float32)
    grad_input_norm, grad_gain_one = norm1_pull(grad_normed)
    grad_input = grad_residual + grad_input_norm
    owned = (
        lax.psum_scatter(
            grad_gate_local.astype(jnp.bfloat16), DP, scatter_dimension=0, tiled=True
        ).astype(jnp.float32),
        lax.psum_scatter(
            grad_up_local.astype(jnp.bfloat16), DP, scatter_dimension=0, tiled=True
        ).astype(jnp.float32),
        lax.psum_scatter(
            grad_down_local.astype(jnp.bfloat16), DP, scatter_dimension=0, tiled=True
        ).astype(jnp.float32),
        lax.psum_scatter(
            weight_locals[0].astype(jnp.bfloat16), DP, scatter_dimension=0, tiled=True
        ).astype(jnp.float32),
        lax.psum_scatter(
            weight_locals[1].astype(jnp.bfloat16), DP, scatter_dimension=0, tiled=True
        ).astype(jnp.float32),
        lax.psum_scatter(
            weight_locals[2].astype(jnp.bfloat16), DP, scatter_dimension=0, tiled=True
        ).astype(jnp.float32),
        lax.psum_scatter(
            weight_locals[3].astype(jnp.bfloat16), DP, scatter_dimension=0, tiled=True
        ).astype(jnp.float32),
        lax.psum_scatter(
            weight_locals[4].astype(jnp.bfloat16), DP, scatter_dimension=0, tiled=True
        ).astype(jnp.float32),
        lax.psum_scatter(
            weight_locals[5].astype(jnp.bfloat16), DP, scatter_dimension=0, tiled=True
        ).astype(jnp.float32),
        lax.psum_scatter(
            grad_out_local.astype(jnp.bfloat16), DP, scatter_dimension=0, tiled=True
        ).astype(jnp.float32),
    )
    conv_q_full = lax.dynamic_update_slice_in_dim(
        jnp.zeros_like(conv_query), mixer_grads[6], tensor_index * query_cols, 1
    )
    conv_k_full = lax.dynamic_update_slice_in_dim(
        jnp.zeros_like(conv_key), mixer_grads[7], tensor_index * query_cols, 1
    )
    conv_v_full = lax.dynamic_update_slice_in_dim(
        jnp.zeros_like(conv_value), mixer_grads[8], tensor_index * value_cols, 1
    )
    scale_full = lax.dynamic_update_slice_in_dim(
        jnp.zeros_like(decay_scale), mixer_grads[9], tensor_index * heads_local, 0
    )
    bias_full = lax.dynamic_update_slice_in_dim(
        jnp.zeros_like(decay_bias), mixer_grads[10], tensor_index * heads_local, 0
    )
    summed = lax.psum(
        (
            grad_gain_one,
            grad_gain_two,
            conv_q_full,
            conv_k_full,
            conv_v_full,
            scale_full,
            bias_full,
            mixer_grads[11],
        ),
        (DP, TP),
    )
    return (
        output,
        loss,
        grad_input,
        summed[0],
        owned[3],
        owned[4],
        owned[5],
        owned[6],
        owned[7],
        owned[8],
        summed[2],
        summed[3],
        summed[4],
        summed[5],
        summed[6],
        summed[7],
        owned[9],
        summed[1],
        owned[0],
        owned[1],
        owned[2],
    )


CORE, SIDE, TENSOR, PLACE = 1, 2, 3, 0
TENSOR_FIRST = (CORE, TENSOR, SIDE, PLACE)
SIDE_FIRST = (CORE, SIDE, TENSOR, PLACE)
TILE = 128
COST = 4 * 10**10


def mm(left, right, dims=((1,), (0,))):
    return lax.dot_general(
        left.astype(jnp.bfloat16),
        right.astype(jnp.bfloat16),
        (dims, ((), ())),
        preferred_element_type=jnp.float32,
    )


def mm_nt(left, right):
    return mm(left, right, ((1,), (1,)))


def mm_tn(left, right):
    return mm(left, right, ((0,), (0,)))


def mm_fine(left, right):
    left_high, right_high = left.astype(jnp.bfloat16), right.astype(jnp.bfloat16)
    left_rest = left - left_high.astype(jnp.float32)
    right_rest = right - right_high.astype(jnp.float32)
    return mm(left_high, right_high) + (mm(left_high, right_rest) + mm(left_rest, right_high))


def ones_mm(ones, right):
    high = right.astype(jnp.bfloat16)
    rest = right - high.astype(jnp.float32)
    middle = rest.astype(jnp.bfloat16)
    return mm(ones, high) + (mm(ones, middle) + mm(ones, rest - middle.astype(jnp.float32)))


def unit_lower_inverses(parts, row, col):
    size = parts[0].shape[0]
    eye = (row == col).astype(jnp.float32)
    block = 16
    inside = (row // block) == (col // block)
    powers = [jnp.where(inside, -part, 0.0) for part in parts]
    inverses = [eye + power for power in powers]
    covered = 2
    while covered < block:
        powers = [mm_fine(power, power) for power in powers]
        moves = [mm_fine(inverse, power) for inverse, power in zip(inverses, powers)]
        inverses = [inverse + move for inverse, move in zip(inverses, moves)]
        covered *= 2
    while block < size:
        cross = ((row // (2 * block)) == (col // (2 * block))) & (
            (row // block) != (col // block)
        )
        lows = [inverse.astype(jnp.bfloat16) for inverse in inverses]
        moves = [mm(low, jnp.where(cross, part, 0.0)) for low, part in zip(lows, parts)]
        moves = [mm(move, low) for move, low in zip(moves, lows)]
        inverses = [inverse - move for inverse, move in zip(inverses, moves)]
        block *= 2
    return inverses


def stable_softplus(values):
    return jnp.maximum(values, 0.0) + jnp.log1p(jnp.exp(-jnp.abs(values)))


def decay_tiles(raw, rate, bias):
    shifted = raw + bias
    soft = stable_softplus(shifted)
    return shifted, soft, -rate * soft


def grids():
    row = lax.broadcasted_iota(jnp.int32, (TILE, TILE), 0)
    col = lax.broadcasted_iota(jnp.int32, (TILE, TILE), 1)
    return row, col


def forward_body(
    heads,
    proj_ref,
    info_ref,
    conv_ref,
    rates_ref,
    gain_ref,
    mixed_ref,
    conv_out_ref,
    rows_out_ref,
    state_out_ref,
    inverse_out_ref,
    pseudo_out_ref,
    earlier_ref,
    state_ref,
):
    first = pl.program_id(2) == 0
    blocks = 4 * heads

    @pl.when(first)
    def _():
        earlier_ref[:, 0:8, :] = jnp.zeros((blocks, 8, TILE), jnp.float32)
        state_ref[...] = jnp.zeros(state_ref.shape, jnp.float32)

    row, col = grids()
    info = info_ref[...]
    info_rows = info.T
    masks = [jnp.broadcast_to(info[:, j : j + 1], (TILE, TILE)) for j in range(3)]
    visible = (row >= col) & (info[:, 4:5] == info_rows[4:5, :])
    raw = proj_ref[0, :, 6 * heads * TILE : 6 * heads * TILE + TILE]
    _, _, log_decay = decay_tiles(raw, rates_ref[0, 0:1, :], rates_ref[0, 1:2, :])
    total = ones_mm((row >= col).astype(jnp.float32), log_decay)
    total_rows = total.T
    carry = jnp.exp(total) * info[:, 3:4]
    beta_tile = jax.nn.sigmoid(raw)
    for block in range(blocks):
        earlier_ref[block, 8 : 8 + TILE, :] = proj_ref[0, :, block * TILE : (block + 1) * TILE]

    def conv_block(block):
        lanes = slice(block * TILE, (block + 1) * TILE)
        result = earlier_ref[block, 8 : 8 + TILE, :] * conv_ref[0, 0:1, lanes]
        for j in range(1, 4):
            result = result + masks[j - 1] * (
                earlier_ref[block, 8 - j : 8 - j + TILE, :] * conv_ref[0, j : j + 1, lanes]
            )
        conv_out_ref[0, :, lanes] = result
        return result * jax.nn.sigmoid(result)

    every = range(heads)
    queries, keys, values, parts, scores = [], [], [], [], []
    for head in every:
        query, key = conv_block(head), conv_block(heads + head)
        query = query * (
            lax.rsqrt(jnp.sum(query * query, axis=1, keepdims=True) + 1e-06) * TILE ** (-0.5)
        )
        key = key * lax.rsqrt(jnp.sum(key * key, axis=1, keepdims=True) + 1e-06)
        spread = total[:, head : head + 1] - total_rows[head : head + 1, :]
        weights = jnp.exp(jnp.where(visible, spread, -1e30))
        key_low, query_low = key.astype(jnp.bfloat16), query.astype(jnp.bfloat16)
        grams = mm_nt(jnp.concatenate([key_low, query_low], axis=0), key_low)
        beta = beta_tile[:, heads + head : heads + head + 1]
        parts.append(jnp.where(row > col, beta * weights * grams[:TILE], 0.0))
        scores.append((grams[TILE:] * weights).astype(jnp.bfloat16))
        queries.append(query_low)
        keys.append((key_low, (key.T * weights[TILE - 1 : TILE, :]).astype(jnp.bfloat16)))
    for head in every:
        values.append(
            jnp.concatenate(
                [conv_block(2 * heads + 2 * head), conv_block(2 * heads + 2 * head + 1)], axis=1
            )
        )
    inverses = [item.astype(jnp.bfloat16) for item in unit_lower_inverses(parts, row, col)]
    states = [state_ref[head] for head in every]
    lows = [state.astype(jnp.bfloat16) for state in states]
    from_states = [
        mm(jnp.concatenate([keys[head][0], queries[head]], axis=0), lows[head]) for head in every
    ]
    carries = [carry[:, head : head + 1] for head in every]
    pseudos = [
        mm(
            inverses[head],
            beta_tile[:, heads + head : heads + head + 1]
            * (values[head] - carries[head] * from_states[head][:TILE]),
        ).astype(jnp.bfloat16)
        for head in every
    ]
    for head in every:
        lanes = slice(2 * head * TILE, 2 * (head + 1) * TILE)
        carried, pseudo = carries[head], pseudos[head]
        state_ref[head] = carried[TILE - 1 : TILE, :] * states[head] + mm(keys[head][1], pseudo)
        rows = carried * from_states[head][TILE:] + mm(scores[head], pseudo)
        state_out_ref[0, 0, head] = lows[head]
        inverse_out_ref[0, 0, head] = inverses[head]
        pseudo_out_ref[0, :, lanes] = pseudo
        rows_out_ref[0, :, lanes] = rows
        gate = proj_ref[
            0, :, (4 * heads + 2 * head) * TILE : (4 * heads + 2 * (head + 1)) * TILE
        ]
        scale = lax.rsqrt(jnp.mean(rows * rows, axis=1, keepdims=True) + 1e-06)
        mixed_ref[:, lanes] = (
            rows * scale * gain_ref[...] * (gate * jax.nn.sigmoid(gate))
        ).astype(jnp.bfloat16)
    for block in range(blocks):
        earlier_ref[block, 0:8, :] = earlier_ref[block, TILE : TILE + 8, :]


def backward_body(
    heads,
    proj_ref,
    info_ref,
    conv_ref,
    rates_ref,
    gain_ref,
    conv_out_ref,
    rows_ref,
    state_in_ref,
    inverse_ref,
    pseudo_ref,
    grad_ref,
    grad_proj_ref,
    grad_conv_ref,
    grad_rates_ref,
    grad_gain_ref,
    later_ref,
    grad_state_ref,
):
    step = pl.program_id(2)
    blocks = 4 * heads

    @pl.when(step == 0)
    def _():
        later_ref[:, TILE : TILE + 8, :] = jnp.zeros((blocks, 8, TILE), jnp.float32)
        grad_state_ref[...] = jnp.zeros(grad_state_ref.shape, jnp.float32)

    @pl.when((step == 0) & (pl.program_id(1) == 0))
    def _():
        grad_conv_ref[...] = jnp.zeros(grad_conv_ref.shape, jnp.float32)
        grad_rates_ref[...] = jnp.zeros(grad_rates_ref.shape, jnp.float32)
        grad_gain_ref[...] = jnp.zeros(grad_gain_ref.shape, jnp.float32)

    row, col = grids()
    info = info_ref[...]
    info_rows = info.T
    masks = [jnp.broadcast_to(info[:, 4 + j : 5 + j], (TILE, TILE)) for j in range(1, 4)]
    visible = (row >= col) & (info[:, 4:5] == info_rows[4:5, :])
    raw = proj_ref[0, :, 6 * heads * TILE : 6 * heads * TILE + TILE]
    rate = rates_ref[0, 0:1, :]
    shifted, soft, log_decay = decay_tiles(raw, rate, rates_ref[0, 1:2, :])
    total = ones_mm((row >= col).astype(jnp.float32), log_decay)
    total_rows = total.T
    carry = jnp.exp(total) * info[:, 3:4]
    beta_tile = jax.nn.sigmoid(raw)
    grad_total = jnp.zeros((TILE, TILE), jnp.float32)
    grad_beta = jnp.zeros((TILE, TILE), jnp.float32)
    gain = gain_ref[...]
    gain_sum = jnp.zeros((1, 2 * TILE), jnp.float32)

    def activation(block):
        value = conv_out_ref[0, :, block * TILE : (block + 1) * TILE]
        gate = jax.nn.sigmoid(value)
        return value * gate, gate * (1.0 + value * (1.0 - gate))

    def close_block(block, grad):
        later_ref[block, 0:TILE, :] = grad
        lanes = slice(block * TILE, (block + 1) * TILE)
        own = proj_ref[0, :, lanes]
        result = grad * conv_ref[0, 0:1, lanes]
        sums = [jnp.sum(grad * own, axis=0, keepdims=True)]
        for j in range(1, 4):
            moved = masks[j - 1] * later_ref[block, j : j + TILE, :]
            result = result + moved * conv_ref[0, j : j + 1, lanes]
            sums.append(jnp.sum(moved * own, axis=0, keepdims=True))
        grad_proj_ref[0, :, lanes] = result.astype(jnp.bfloat16)
        for j in range(4):
            grad_conv_ref[0, j : j + 1, lanes] += sums[j]

    for head in range(heads):
        lanes = slice(2 * head * TILE, 2 * (head + 1) * TILE)
        gate_lanes = slice((4 * heads + 2 * head) * TILE, (4 * heads + 2 * (head + 1)) * TILE)
        rows = rows_ref[0, :, lanes]
        gate = proj_ref[0, :, gate_lanes]
        grad = grad_ref[:, lanes]
        scale = lax.rsqrt(jnp.mean(rows * rows, axis=1, keepdims=True) + 1e-06)
        level = rows * scale
        sigmoid = jax.nn.sigmoid(gate)
        through = grad * (gate * sigmoid)
        gain_sum = gain_sum + jnp.sum(through * level, axis=0, keepdims=True)
        grad_proj_ref[0, :, gate_lanes] = (
            grad * level * gain * (sigmoid * (1.0 + gate * (1.0 - sigmoid)))
        ).astype(jnp.bfloat16)
        through = through * gain
        grad_rows = scale * (
            through - level * jnp.mean(through * level, axis=1, keepdims=True)
        )

        query_act, query_slope = activation(head)
        query_scale = lax.rsqrt(jnp.sum(query_act * query_act, axis=1, keepdims=True) + 1e-06)
        query_unit = query_act * query_scale
        query = query_unit * TILE ** (-0.5)
        key_act, key_slope = activation(heads + head)
        key_scale = lax.rsqrt(jnp.sum(key_act * key_act, axis=1, keepdims=True) + 1e-06)
        key = key_act * key_scale
        value_parts = [activation(2 * heads + 2 * head), activation(2 * heads + 2 * head + 1)]
        value = jnp.concatenate([value_parts[0][0], value_parts[1][0]], axis=1)

        spread = total[:, head : head + 1] - total_rows[head : head + 1, :]
        weights = jnp.exp(jnp.where(visible, spread, -1e30))
        beta = beta_tile[:, heads + head : heads + head + 1]
        carried = carry[:, head : head + 1]
        key_low, query_low = key.astype(jnp.bfloat16), query.astype(jnp.bfloat16)
        both = jnp.concatenate([key_low, query_low], axis=0)
        grams = mm_nt(both, key_low)
        state_low = state_in_ref[0, 0, head]
        inverse = inverse_ref[0, 0, head]
        pseudo = pseudo_ref[0, :, lanes]
        grad_state = grad_state_ref[head]
        grad_state_low = grad_state.astype(jnp.bfloat16)
        last_row = weights[TILE - 1 : TILE, :]
        last_col = jnp.sum(jnp.where(row == col, last_row, 0.0), axis=1, keepdims=True)
        grad_rows_low = grad_rows.astype(jnp.bfloat16)
        grad_pseudo = mm_tn(grams[TILE:] * weights, grad_rows_low) + mm(
            last_col * key, grad_state_low
        )
        solved = mm_tn(inverse, grad_pseudo)
        crossed = mm_nt(
            jnp.concatenate([grad_rows_low, solved.astype(jnp.bfloat16)], axis=0), pseudo
        )
        grad_scores = crossed[:TILE] * weights
        below = jnp.where(row > col, crossed[TILE:] * weights, 0.0)
        grad_gram = (-beta) * below
        grad_value = beta * solved
        from_state = mm(key_low, state_low)
        grad_beta_col = jnp.sum(
            solved * (value - carried * from_state), axis=1, keepdims=True
        ) - jnp.sum(below * grams[:TILE], axis=1, keepdims=True)
        out_part = (carried * grad_rows).astype(jnp.bfloat16)
        key_part = ((-carried) * grad_value).astype(jnp.bfloat16)
        stacked = jnp.concatenate([out_part, key_part], axis=0)
        to_inputs = mm_nt(stacked, state_low)
        scores_low, gram_low = grad_scores.astype(jnp.bfloat16), grad_gram.astype(jnp.bfloat16)
        grad_query = mm(scores_low, key_low) + to_inputs[:TILE]
        key_own = mm(gram_low, key_low) + to_inputs[TILE:]
        key_rest = mm_tn(
            jnp.concatenate([gram_low, scores_low], axis=0), both
        )
        key_state = last_col * mm_nt(pseudo, grad_state_low)
        grad_key = key_own + key_rest + key_state
        grad_state_ref[head] = carried[TILE - 1 : TILE, :] * grad_state + mm_tn(
            jnp.concatenate([query_low, key_low], axis=0), stacked
        )
        key_exact, query_exact = key_low.astype(jnp.float32), query_low.astype(jnp.float32)
        state_dot = jnp.sum(key_state * key_exact, axis=1, keepdims=True)
        tail = jnp.sum(state_dot, axis=0, keepdims=True) + carried[TILE - 1 : TILE, :] * jnp.sum(
            jnp.sum(grad_state * state_low.astype(jnp.float32), axis=1, keepdims=True),
            axis=0,
            keepdims=True,
        )
        grad_total_col = (
            jnp.sum(
                grad_query * query_exact + (key_own - key_rest) * key_exact, axis=1, keepdims=True
            )
            - state_dot
            + jnp.where(row[:, 0:1] == TILE - 1, tail, 0.0)
        )
        grad_total = jnp.where(col == head, grad_total_col, grad_total)
        grad_beta = jnp.where(col == heads + head, grad_beta_col, grad_beta)

        grad_query = grad_query * TILE ** (-0.5)
        close_block(
            head,
            query_scale
            * (
                grad_query
                - query_unit * jnp.sum(grad_query * query_unit, axis=1, keepdims=True)
            )
            * query_slope,
        )
        close_block(
            heads + head,
            key_scale
            * (grad_key - key * jnp.sum(grad_key * key, axis=1, keepdims=True))
            * key_slope,
        )
        close_block(2 * heads + 2 * head, grad_value[:, :TILE] * value_parts[0][1])
        close_block(2 * heads + 2 * head + 1, grad_value[:, TILE:] * value_parts[1][1])

    grad_log = ones_mm((row <= col).astype(jnp.float32), grad_total)
    grad_raw = -rate * grad_log * jax.nn.sigmoid(shifted)
    grad_rates_ref[0, 0:1, :] += -jnp.sum(grad_log * soft, axis=0, keepdims=True)
    grad_rates_ref[0, 1:2, :] += jnp.sum(grad_raw, axis=0, keepdims=True)
    grad_gain_ref[0, 0:1, :] += gain_sum
    grad_proj_ref[0, :, 6 * heads * TILE : 6 * heads * TILE + TILE] = jnp.where(
        col < heads, grad_raw, grad_beta * beta_tile * (1.0 - beta_tile)
    ).astype(jnp.bfloat16)
    for block in range(blocks):
        later_ref[block, TILE : TILE + 8, :] = later_ref[block, 0:8, :]


def mixer_specs(parts, rows, wide, heads, blocks, backward):
    conv_cols, value_cols = 4 * heads * TILE, 2 * heads * TILE

    def place(s, c):
        return s * blocks + ((blocks - 1 - c) if backward else c)

    return SimpleNamespace(
        proj=pl.BlockSpec((1, TILE, wide), lambda p, s, c: (p, place(s, c), 0)),
        info=pl.BlockSpec((TILE, TILE), lambda p, s, c: (place(s, c), 0)),
        conv=pl.BlockSpec((1, 8, conv_cols), lambda p, s, c: (p, 0, 0)),
        rates=pl.BlockSpec((1, 8, TILE), lambda p, s, c: (p, 0, 0)),
        gain=pl.BlockSpec((1, 2 * TILE), lambda p, s, c: (0, 0)),
        flat=pl.BlockSpec((TILE, value_cols), lambda p, s, c: (place(s, c), p)),
        conv_out=pl.BlockSpec((1, TILE, conv_cols), lambda p, s, c: (p, place(s, c), 0)),
        value=pl.BlockSpec((1, TILE, value_cols), lambda p, s, c: (p, place(s, c), 0)),
        state=pl.BlockSpec(
            (1, 1, heads, TILE, 2 * TILE), lambda p, s, c: (p, place(s, c), 0, 0, 0)
        ),
        inverse=pl.BlockSpec(
            (1, 1, heads, TILE, TILE), lambda p, s, c: (p, place(s, c), 0, 0, 0)
        ),
        gain_sum=pl.BlockSpec((1, 8, 2 * TILE), lambda p, s, c: (p, 0, 0)),
    )


def mixer_forward(proj, info, conv, rates, gain, heads):
    parts, rows, wide = proj.shape
    blocks = LENGTH // TILE
    spec = mixer_specs(parts, rows, wide, heads, blocks, False)
    conv_cols, value_cols = 4 * heads * TILE, 2 * heads * TILE
    low, full = jnp.bfloat16, jnp.float32
    return pl.pallas_call(
        functools.partial(forward_body, heads),
        grid=(parts, rows // LENGTH, blocks),
        in_specs=[spec.proj, spec.info, spec.conv, spec.rates, spec.gain],
        out_specs=[
            spec.flat, spec.conv_out, spec.value, spec.state, spec.inverse, spec.value
        ],
        out_shape=[
            jax.ShapeDtypeStruct((rows, parts * value_cols), low),
            jax.ShapeDtypeStruct((parts, rows, conv_cols), full),
            jax.ShapeDtypeStruct((parts, rows, value_cols), full),
            jax.ShapeDtypeStruct((parts, rows // TILE, heads, TILE, 2 * TILE), low),
            jax.ShapeDtypeStruct((parts, rows // TILE, heads, TILE, TILE), low),
            jax.ShapeDtypeStruct((parts, rows, value_cols), low),
        ],
        scratch_shapes=[
            pltpu.VMEM((4 * heads, TILE + 8, TILE), full),
            pltpu.VMEM((heads, TILE, 2 * TILE), full),
        ],
        compiler_params=pltpu.CompilerParams(
            vmem_limit_bytes=48 * 1024 * 1024,
        ),
        cost_estimate=pl.CostEstimate(flops=COST, transcendentals=0, bytes_accessed=10**8),
        name="mixer_forward",
    )(proj, info, conv, rates, gain)


def mixer_backward(proj, info, conv, rates, gain, saved, grad, heads):
    parts, rows, wide = proj.shape
    blocks = LENGTH // TILE
    spec = mixer_specs(parts, rows, wide, heads, blocks, True)
    conv_cols = 4 * heads * TILE
    low, full = jnp.bfloat16, jnp.float32
    return pl.pallas_call(
        functools.partial(backward_body, heads),
        grid=(parts, rows // LENGTH, blocks),
        in_specs=[
            spec.proj, spec.info, spec.conv, spec.rates, spec.gain,
            spec.conv_out, spec.value, spec.state, spec.inverse, spec.value, spec.flat,
        ],
        out_specs=[spec.proj, spec.conv, spec.rates, spec.gain_sum],
        out_shape=[
            jax.ShapeDtypeStruct((parts, rows, wide), low),
            jax.ShapeDtypeStruct((parts, 8, conv_cols), full),
            jax.ShapeDtypeStruct((parts, 8, TILE), full),
            jax.ShapeDtypeStruct((parts, 8, 2 * TILE), full),
        ],
        scratch_shapes=[
            pltpu.VMEM((4 * heads, TILE + 8, TILE), full),
            pltpu.VMEM((heads, TILE, 2 * TILE), full),
        ],
        compiler_params=pltpu.CompilerParams(
            vmem_limit_bytes=48 * 1024 * 1024,
        ),
        cost_estimate=pl.CostEstimate(flops=COST, transcendentals=0, bytes_accessed=10**8),
        name="mixer_backward",
    )(proj, info, conv, rates, gain, *saved, grad)


BLOCK = 256


def rms_backward(values, gain, grad):
    scale = lax.rsqrt(jnp.mean(values * values, axis=1, keepdims=True) + 1e-06)
    level = values * scale
    through = grad * gain
    back = scale * (through - level * jnp.mean(through * level, axis=1, keepdims=True))
    return back, jnp.sum(grad * level, axis=0, keepdims=True)


def dense_forward_body(
    normed_ref,
    gate_w_ref,
    up_w_ref,
    down_w_ref,
    residual_ref,
    target_ref,
    live_ref,
    level_ref,
    gate_ref,
    up_ref,
    hidden_ref,
    output_ref,
    grad_ref,
    grad_turned_ref,
    loss_ref,
    total_ref,
):
    part, step = pl.program_id(0), pl.program_id(1)
    normed = normed_ref[...]
    gate = mm(normed, gate_w_ref[0])
    up = mm(normed, up_w_ref[0])
    hidden = (gate * jax.nn.sigmoid(gate) * up).astype(jnp.bfloat16)
    gate_ref[0] = gate.astype(jnp.bfloat16)
    up_ref[0] = up.astype(jnp.bfloat16)
    hidden_ref[0] = hidden
    share = mm_nt(hidden, down_w_ref[0])
    rows = pl.ds(pl.multiple_of(step * BLOCK, BLOCK), BLOCK)

    @pl.when(part == 0)
    def _():
        total_ref[rows, :] = share

    @pl.when(part == pl.num_programs(0) - 1)
    def _():
        output = residual_ref[...] + (total_ref[rows, :] + share)
        output_ref[...] = output
        error = output - target_ref[...].astype(jnp.float32)
        live = live_ref[:, 0:1]
        grad = error * live * level_ref[0:1, 0:1]
        grad_ref[...] = grad.astype(jnp.bfloat16)
        grad_turned_ref[...] = grad.T.astype(jnp.bfloat16)
        squares = jnp.sum(live * error * error, axis=0, keepdims=True)

        @pl.when(step == 0)
        def _():
            loss_ref[...] = jnp.zeros(loss_ref.shape, jnp.float32)

        loss_ref[0:1, :] += squares


def dense_backward_body(
    grad_ref,
    gate_w_ref,
    up_w_ref,
    down_w_ref,
    gate_ref,
    up_ref,
    residual_ref,
    output_ref,
    target_ref,
    live_ref,
    level_ref,
    gain_ref,
    grad_gate_ref,
    grad_up_ref,
    back_ref,
    back_low_ref,
    back_turned_ref,
    gain_sum_ref,
    total_ref,
):
    part, step = pl.program_id(0), pl.program_id(1)
    grad_hidden = mm(grad_ref[...], down_w_ref[0])
    gate = gate_ref[0].astype(jnp.float32)
    up = up_ref[0].astype(jnp.float32)
    sigmoid = jax.nn.sigmoid(gate)
    grad_gate = (grad_hidden * up * sigmoid * (1.0 + gate * (1.0 - sigmoid))).astype(jnp.bfloat16)
    grad_up = (grad_hidden * gate * sigmoid).astype(jnp.bfloat16)
    grad_gate_ref[0] = grad_gate
    grad_up_ref[0] = grad_up
    share = mm_nt(grad_gate, gate_w_ref[0]) + mm_nt(grad_up, up_w_ref[0])
    rows = pl.ds(pl.multiple_of(step * BLOCK, BLOCK), BLOCK)

    @pl.when(part == 0)
    def _():
        total_ref[rows, :] = share

    @pl.when(part == pl.num_programs(0) - 1)
    def _():
        error = output_ref[...] - target_ref[...].astype(jnp.float32)
        back, gain_sum = rms_backward(
            residual_ref[...], gain_ref[...], total_ref[rows, :] + share
        )
        back = error * live_ref[:, 0:1] * level_ref[0:1, 0:1] + back
        back_ref[...] = back
        back_low_ref[...] = back.astype(jnp.bfloat16)
        back_turned_ref[...] = back.T.astype(jnp.bfloat16)

        @pl.when(step == 0)
        def _():
            gain_sum_ref[...] = jnp.zeros(gain_sum_ref.shape, jnp.float32)

        gain_sum_ref[0:1, :] += gain_sum


def input_backward_body(
    first_ref, second_ref, weight_ref, input_ref, residual_ref, gain_ref, back_ref, gain_sum_ref, total_ref
):
    part, step = pl.program_id(0), pl.program_id(1)
    grad = jnp.where(part == 0, first_ref[0], second_ref[0])
    share = mm_nt(grad, weight_ref[0])
    rows = pl.ds(pl.multiple_of(step * BLOCK, BLOCK), BLOCK)

    @pl.when(part == 0)
    def _():
        total_ref[rows, :] = share

    @pl.when(part == pl.num_programs(0) - 1)
    def _():
        back, gain_sum = rms_backward(
            input_ref[...].astype(jnp.float32), gain_ref[...], total_ref[rows, :] + share
        )
        back_ref[...] = residual_ref[...] + back

        @pl.when(step == 0)
        def _():
            gain_sum_ref[...] = jnp.zeros(gain_sum_ref.shape, jnp.float32)

        gain_sum_ref[0:1, :] += gain_sum


def dense_call(body, flags, arrays, choose, width, units):
    rows = arrays[0].shape[-2]
    full, low = jnp.float32, jnp.bfloat16

    def cut(block, place, shape=None, kind=full):
        return (pl.BlockSpec(block, place), jax.ShapeDtypeStruct(shape or block, kind))

    late = (lambda p, i, flags: (i * p, 0), (rows, width))
    spec = SimpleNamespace(
        row=cut((BLOCK, width), lambda p, i, flags: (i, 0)),
        late=cut((BLOCK, width), *late),
        late_low=cut((BLOCK, width), *late, low),
        turned=cut((width, BLOCK), lambda p, i, flags: (0, i * p), (width, rows), low),
        unit=cut((1, BLOCK, units), lambda p, i, flags: (p, i, 0), (2, rows, units), low),
        first=cut((1, BLOCK, units), lambda p, i, flags: (0, i * (1 - p), 0)),
        second=cut((1, BLOCK, units), lambda p, i, flags: (0, i * p, 0)),
        lane=cut((BLOCK, TILE), lambda p, i, flags: (i * p, 0)),
        level=cut((8, TILE), lambda p, i, flags: (0, 0)),
        gain=cut((1, width), lambda p, i, flags: (0, 0)),
        own=cut((1, width, units), lambda p, i, flags: (lax.rem(p + 1 + flags[1], 2), 0, 0)),
        sums=cut((8, width), lambda p, i, flags: (0, 0)),
        weights=[
            cut((1, width, units), lambda p, i, flags, index=index: (p, 0, index)) for index in range(3)
        ],
    )
    taken, given = choose(spec)
    return pl.pallas_call(
        lambda flags_ref, *refs: body(*refs),
        grid_spec=pltpu.PrefetchScalarGridSpec(
            num_scalar_prefetch=1,
            grid=(2, rows // BLOCK),
            in_specs=[item[0] for item in taken],
            out_specs=[item[0] for item in given],
            scratch_shapes=[pltpu.VMEM((rows, width), full)],
        ),
        out_shape=[item[1] for item in given],
        compiler_params=pltpu.CompilerParams(vmem_limit_bytes=56 * 1024 * 1024),
        cost_estimate=pl.CostEstimate(flops=COST, transcendentals=0, bytes_accessed=10**8),
        name=body.__name__[:-5],
    )(flags, *arrays)


def product_body(own, side_first, flags_ref, left_ref, first_ref, second_ref, *refs):
    part = pl.program_id(0)
    shape = left_ref.shape
    left = left_ref[...].reshape(shape[0] * shape[2], shape[3])

    def finish(right_ref):
        result = mm(left, right_ref[...].reshape(right_ref.shape[-2:]))
        if own:
            result = result + refs[0][0].astype(jnp.float32)
        result = result.astype(jnp.bfloat16)
        if not side_first:
            refs[-1][0] = result
            return
        split = result.reshape(shape[0] // 2, 2, shape[2], result.shape[1])
        count = shape[0] * shape[2] // 2
        low = split[:, 0].reshape(count, -1)
        high = split[:, 1].reshape(count, -1)
        here = flags_ref[2] == 0
        refs[-2][0] = jnp.where(here, low, high)
        refs[-1][0] = jnp.where(here, high, low)

    @pl.when(part == 0)
    def _():
        finish(first_ref)

    @pl.when(part == 1)
    def _():
        finish(second_ref)


def product(flags, left, rights, received=None, side_first=False, relative=False):
    own = received is not None
    side_first = side_first and own
    groups, _, rows, tokens = left.shape
    cols, count = rights[0].shape[-1], len(rights)
    block = cols if count == 2 else -(-cols // (2 * TILE)) * TILE
    last = -(-cols // block) - 1

    def slot(p, flags):
        return 0 if count == 1 else 1 - p if relative else lax.rem(p + flags[1], 2)

    def right_spec(array, index, which):
        def place(p, j, flags):
            return j * (1 - p) + last * p if which == 0 else j * p

        if array.ndim == 3:
            return pl.BlockSpec(
                (1, tokens, block), lambda p, j, flags: (index, 0, place(p, j, flags))
            )
        return pl.BlockSpec((tokens, block), lambda p, j, flags: (0, place(p, j, flags)))

    result_rows = groups * rows // (2 if side_first else 1)
    result = pl.BlockSpec((1, result_rows, block), lambda p, j, flags: (slot(p, flags), 0, j))
    kept = jax.ShapeDtypeStruct((count, result_rows, cols), jnp.bfloat16)
    in_specs = [
        pl.BlockSpec(
            (groups, 1, rows, tokens),
            lambda p, j, flags: (0, flags[0] if own else 1 - flags[0], 0, 0),
        ),
        right_spec(rights[0], 0, 0),
        right_spec(rights[-1], rights[-1].shape[0] - 1, count - 1),
    ]
    arrays = [left, rights[0], rights[-1]]
    if own:
        in_specs.append(
            pl.BlockSpec((1, groups * rows, block), lambda p, j, flags: (slot(p, flags), 0, j))
        )
        arrays.append(received)
    many = 2 if side_first else 1
    results = pl.pallas_call(
        functools.partial(product_body, own, side_first),
        grid_spec=pltpu.PrefetchScalarGridSpec(
            num_scalar_prefetch=1,
            grid=(count, last + 1),
            in_specs=in_specs,
            out_specs=[result] * many,
        ),
        out_shape=[kept] * many,
        compiler_params=pltpu.CompilerParams(vmem_limit_bytes=56 * 1024 * 1024),
        cost_estimate=pl.CostEstimate(
            flops=2 * groups * rows * tokens * cols * count, transcendentals=0, bytes_accessed=10**7
        ),
        name="product",
    )(flags, *arrays)
    return results if side_first else results[0]


def token_info(seg):
    sequences, length = seg.shape
    lanes = []
    for j in range(1, 4):
        lanes.append(jnp.pad(seg[:, j:] == seg[:, :-j], ((0, 0), (j, 0))))
    ends = seg.reshape(sequences, length // TILE, TILE)
    before = jnp.pad(ends[:, :-1, -1], ((0, 0), (1, 0)), constant_values=-1)
    lanes.append((ends == before[:, :, None]).reshape(sequences, length))
    lanes.append(seg)
    for j in range(1, 4):
        lanes.append(jnp.pad(seg[:, j:] == seg[:, :-j], ((0, 0), (0, j))))
    table = jnp.stack([item.astype(jnp.float32).reshape(-1) for item in lanes], axis=1)
    return jnp.pad(table, ((0, 0), (0, TILE - table.shape[1])))


def gather_all(local):
    rows = lax.all_gather(local, (TP, DP), axis=0, tiled=True)
    shares = lax.axis_size(TP)
    return rows.reshape(shares, rows.shape[0] // shares, rows.shape[1])


def scatter_all(parts):
    shares, rows, cols = parts.shape
    return lax.psum_scatter(
        parts.reshape(shares * rows, cols), (TP, DP), scatter_dimension=0, tiled=True
    ).astype(jnp.float32)


def exchange(array, axis, bit):
    size = lax.axis_size(axis)
    return lax.ppermute(array, axis, [(i, i ^ bit) for i in range(size)])


def shift(array, step):
    size = lax.axis_size(DP)
    return lax.ppermute(array, DP, [(i, (i + step) % size) for i in range(size)])


def pick(array, index, axis):
    return lax.dynamic_index_in_dim(array, index, axis, keepdims=False)


def add_low(left, right):
    return (left.astype(jnp.float32) + right.astype(jnp.float32)).astype(jnp.bfloat16)


def after(value, *earlier):
    return lax.optimization_barrier((value, earlier))[0]


class Scatter:
    def __init__(self, flags, turned, rights, stages, relative=False):
        self.relative, self.stages = relative, list(stages)
        self.size = lax.axis_size(DP)
        self.flags, self.rights = flags, rights
        self.left = turned.reshape(self.size // 2, 2, -1, turned.shape[1])
        self.rows = self.left.shape[2]
        self.sent = [product(flags, self.left, rights, relative=relative)]

    joined = None

    def routes(self):
        flat = [item.reshape(-1, item.shape[-1]) for item in self.sent]
        stage = self.stages[0]
        return [
            ((stage, step if stage == PLACE else 0, item.shape[0]), item)
            for step, item in enumerate(flat)
        ]

    def take(self, moved):
        stage = self.stages.pop(0)
        if stage == PLACE:
            self.total = self.kept.astype(jnp.float32)
            for item in moved:
                self.total = self.total + item.astype(jnp.float32)
            return
        if stage == CORE:
            side_first = self.stages[0] == SIDE
            held = product(
                self.flags, self.left, self.rights, moved[0], side_first, self.relative
            )
            if side_first:
                self.kept, self.sent = [list(item) for item in held]
            else:
                self.kept, self.sent = [held[0]], [held[1]]
            return
        held = [add_low(kept, item) for kept, item in zip(self.kept, moved)]
        if not self.stages:
            self.held = held[0]
            return
        if self.joined is not None:
            held = [add_low(held[0], self.joined)]
        stage = self.stages[0]
        if stage == TENSOR:
            self.kept, self.sent = held[:1], held[1:]
        elif stage == SIDE:
            held = held[0].reshape(self.size // 4, 2, self.rows, -1)
            self.kept, self.sent = [
                [pick(held, index, 1).reshape(-1, held.shape[-1])]
                for index in (self.flags[2], 1 - self.flags[2])
            ]
        else:
            count = self.size // 4
            held = held[0].reshape(count, self.rows, -1)
            self.sent = [
                pick(held, (self.flags[3] + step) % count, 0) for step in range(1, count)
            ]
            self.kept = pick(held, self.flags[3], 0)


def send(route, array):
    stage, step, _ = route
    if stage == PLACE:
        return shift(array, 4 * (step + 1))
    if stage == TENSOR:
        return exchange(array, TP, 1)
    return exchange(array, DP, stage)


class Transfer:
    def __init__(self, *items):
        self.items, self.routes = items, {}
        for index, item in enumerate(items):
            for slot, (route, array) in enumerate(item.routes()):
                key = route + ((index, slot) if route[0] == CORE else ())
                self.routes.setdefault(key, []).append((index, slot, array))
        self.packed = [
            jnp.concatenate([entry[2] for entry in entries], axis=1)
            for entries in self.routes.values()
        ]

    def send(self):
        return [send(key[:3], array) for key, array in zip(self.routes, self.packed)]

    def land(self):
        self.accept(lax.optimization_barrier(self.send()))

    def accept(self, moved):
        got = [[None] * len(item.sent) for item in self.items]
        for entries, array in zip(self.routes.values(), moved):
            pieces = columns(array, [entry[2].shape[1] for entry in entries])
            for (index, slot, _), piece in zip(entries, pieces):
                got[index][slot] = piece
        for item, mine in zip(self.items, got):
            item.take([piece.reshape(sent.shape) for piece, sent in zip(mine, item.sent)])


class Shared:
    def __init__(self, flat, stages):
        self.flat, self.stages = flat.reshape(1, -1), list(stages)

    @property
    def sent(self):
        return [self.flat]

    def routes(self):
        return [((self.stages[0], 0, 1), self.flat)]

    def take(self, moved):
        self.stages.pop(0)
        self.flat = self.flat + moved[0]


def columns(array, sizes):
    pieces, start = [], 0
    for size in sizes:
        pieces.append(array[..., start : start + size])
        start += size
    return pieces


def on_device_whole(
    layer_input,
    target,
    segment,
    pad_mask,
    norm1_gain,
    w_query,
    w_key,
    w_value,
    w_gate_out,
    w_decay,
    w_beta,
    conv_query,
    conv_key,
    conv_value,
    decay_scale,
    decay_bias,
    out_norm_gain,
    w_out,
    norm2_gain,
    w_ffn_gate,
    w_ffn_up,
    w_ffn_down,
):
    own_rows, width = layer_input.shape
    shares = lax.axis_size(TP)
    sequences = own_rows // LENGTH
    tensor_index = lax.axis_index(TP)
    low = jnp.bfloat16
    proj_local = (w_query, w_key, w_value, w_gate_out, w_decay, w_beta)
    proj_sizes = [item.shape[1] for item in proj_local]
    used = sum(proj_sizes)
    padded = -(-used // 128) * 128
    proj_all = gather_all(
        jnp.concatenate(proj_local + (jnp.zeros((w_query.shape[0], padded - used), low),), axis=1)
    )
    rest_local = (w_ffn_gate, w_ffn_up, w_ffn_down, w_out)
    rest_sizes = [item.shape[1] for item in rest_local]
    rest_all = gather_all(jnp.concatenate(rest_local, axis=1))
    out_all = columns(rest_all, rest_sizes)[3]
    live = pad_mask.astype(jnp.float32)
    count = lax.psum(jnp.sum(live), (DP, TP))
    input_float = layer_input.astype(jnp.float32)
    normed = rms_scale(input_float, norm1_gain).astype(low)
    seg_rows = lax.dynamic_slice_in_dim(segment, tensor_index * own_rows, own_rows, 0).reshape(
        sequences, LENGTH
    )
    parts = (1 - tensor_index, tensor_index)
    proj = [
        jnp.dot(normed, pick(proj_all, part, 0), preferred_element_type=jnp.float32)[None]
        for part in parts
    ]
    heads = w_decay.shape[1]
    info = token_info(seg_rows)

    def by_part(item):
        return item.reshape(item.shape[0], shares, item.shape[1] // shares).transpose(1, 0, 2)

    conv = jnp.pad(
        jnp.concatenate([by_part(c) for c in (conv_query, conv_key, conv_value)], axis=2),
        ((0, 0), (0, 4), (0, 0)),
    )
    rates = jnp.pad(
        by_part(jnp.stack([decay_scale, decay_bias])), ((0, 0), (0, 6), (0, TILE - heads))
    )
    gain = out_norm_gain.reshape(1, -1)
    value_cols = w_value.shape[1]
    mixer_args = [
        (item, info, pick(conv, part, 0)[None], pick(rates, part, 0)[None], gain)
        for item, part in zip(proj, parts)
    ]
    out_parts = [pick(out_all, part, 0) for part in parts]
    saved, mixed, residual = [], [], input_float
    for arguments in mixer_args:
        mixed_low, *kept = mixer_forward(*arguments, heads)
        mixed.append(mixed_low)
        saved.append(kept)
    for item, weight in zip(mixed, out_parts):
        residual = residual + contract_cols(item, weight)
    normed2 = rms_scale(residual, norm2_gain).astype(low)
    units = w_ffn_gate.shape[1]
    all_tokens = own_rows * lax.axis_size(DP) * lax.axis_size(TP)
    level = jnp.full((8, TILE), all_tokens / count, jnp.float32)
    live_lanes = jnp.broadcast_to(live[:, None], (own_rows, TILE))
    mine = lax.axis_index(DP)
    flags = jnp.stack([mine % 2, tensor_index, (mine // 2) % 2, mine // 4]).astype(jnp.int32)
    weights = [rest_all] * 3
    gate_pre, up_pre, hidden, output, grad_ffn, grad_ffn_turned, loss_rows = dense_call(
        dense_forward_body,
        flags,
        [normed2, *weights, residual, target, live_lanes, level],
        lambda s: (
            [s.row, *s.weights, s.late, s.late, s.lane, s.level],
            [s.unit, s.unit, s.unit, s.late, s.late_low, s.turned, s.sums],
        ),
        width,
        units,
    )
    loss_sum = jnp.sum(loss_rows)
    down = Scatter(flags, grad_ffn_turned, [hidden, hidden], SIDE_FIRST)
    cores = Transfer(down)
    grad_gates, grad_ups, grad_residual, grad_attention, back_turned, gain_two_rows = dense_call(
        dense_backward_body,
        flags,
        [
            after(grad_ffn, cores.packed), *weights, gate_pre, up_pre,
            residual, output, target, live_lanes, level, norm2_gain.reshape(1, -1),
        ],
        lambda s: (
            [s.row, *s.weights, s.unit, s.unit, s.late, s.late, s.late, s.lane, s.level, s.gain],
            [s.unit, s.unit, s.late, s.late_low, s.turned, s.sums],
        ),
        width,
        units,
    )
    grad_gain_two = gain_two_rows[0]
    turned2 = normed2.T
    gate = Scatter(flags, turned2, [grad_gates, grad_gates], TENSOR_FIRST)
    up = Scatter(flags, turned2, [grad_ups, grad_ups], SIDE_FIRST)
    cores.land()
    first_down = Transfer(down)
    gate.sent = after(gate.sent, first_down.packed)
    cores = Transfer(gate, up)
    out = Scatter(flags, back_turned, mixed, SIDE_FIRST, True)
    out_cores = Transfer(out)
    later = after(grad_attention, out_cores.packed, cores.packed)
    grad_mixed = [
        jnp.dot(later, weight, preferred_element_type=jnp.float32) for weight in out_parts
    ]
    cores.land()
    out_cores.land()
    first_down.land()
    middle = Transfer(gate, up, out, down)
    ready = after(grad_mixed[0], middle.packed)
    per_part = [mixer_backward(*mixer_args[0], saved[0], ready, heads)]
    turned = normed.T
    theirs = Scatter(flags, turned, [per_part[0][0]], (CORE, SIDE))
    theirs_cores = Transfer(theirs)
    middle.land()
    middle = Transfer(gate, up, out)
    theirs.left = after(theirs.left, middle.packed)
    theirs_cores.land()
    theirs_side = Transfer(theirs)
    ready = after(grad_mixed[1], middle.packed, theirs_side.packed)
    per_part.append(mixer_backward(*mixer_args[1], saved[1], ready, heads))
    grad_conv, grad_rates, grad_gain = [
        jnp.roll(
            jnp.concatenate([item[i] for item in per_part], axis=0), tensor_index + 1, axis=0
        )
        for i in (1, 2, 3)
    ]

    def from_part(item):
        return item.transpose(1, 0, 2).reshape(item.shape[1], -1)

    query_cols = w_query.shape[1]
    small = [
        from_part(item)
        for item in columns(grad_conv[:, :4], (query_cols, query_cols, value_cols))
    ] + [
        grad_rates[:, 0, :heads].reshape(-1),
        grad_rates[:, 1, :heads].reshape(-1),
        jnp.sum(grad_gain[:, 0], axis=0),
        grad_gain_two,
        loss_sum,
    ]
    grad_proj = [item[0] for item in per_part]
    ours = Scatter(flags, turned, [grad_proj[1]], (CORE, SIDE, PLACE))
    ours_cores = Transfer(ours)
    theirs.sent = after(theirs.sent, ours_cores.packed)
    middle.land()
    theirs_side.land()
    middle = Transfer(gate, up, out, down)
    ours.left = after(ours.left, middle.packed, theirs.held)
    ours_cores.land()
    ending = Transfer(ours)
    grad_proj = after(grad_proj, ending.packed)
    grad_input, gain_one_rows = dense_call(
        input_backward_body,
        flags,
        [*grad_proj, proj_all, layer_input, grad_residual, norm1_gain.reshape(1, -1)],
        lambda s: ([s.first, s.second, s.own, s.late, s.late, s.gain], [s.late, s.sums]),
        width,
        padded,
    )
    joined = exchange(theirs.held, TP, 1)
    joined, gain_one_rows, *moved = lax.optimization_barrier(
        [joined, gain_one_rows] + middle.send() + ending.send()
    )
    ours.joined = joined
    middle.accept(moved[: len(middle.packed)])
    ending.accept(moved[len(middle.packed) :])
    size, places = lax.axis_size(DP), []
    while 4 << len(places) < size:
        places.append(4 << len(places))
    small.append(gain_one_rows[0])
    flat = jnp.concatenate([item.reshape(-1) for item in small])
    flat = jnp.pad(flat, (0, -flat.shape[0] % 1024))
    shared = Shared(flat, places + [CORE, SIDE, TENSOR])
    for _ in places:
        Transfer(shared).land()
    ours.sent = after(ours.sent, shared.flat)
    ending = Transfer(ours)
    shared.flat = after(shared.flat, ending.packed)
    while shared.stages:
        Transfer(shared).land()
    ending.land()
    own_gate, own_up, own_out, own_down = [item.total for item in (gate, up, out, down)]
    own_proj = columns(ours.total, proj_sizes)
    summed, start = [], 0
    for item in small:
        summed.append(shared.flat[0, start : start + item.size].reshape(item.shape))
        start += item.size
    loss = summed[7] / (count * width)
    return (
        output,
        loss,
        grad_input,
        summed[8],
        *own_proj,
        *summed[:6],
        own_out,
        summed[6],
        own_gate,
        own_up,
        own_down,
    )


def on_device(layer_input, *others):
    size = lax.axis_size(DP)
    whole = layer_input.shape[0] % LENGTH == 0 and lax.axis_size(TP) == 2
    whole = whole and size >= 4 and size & (size - 1) == 0
    return (on_device_whole if whole else on_device_split)(layer_input, *others)


def solution(mesh):
    return jax.shard_map(
        on_device,
        mesh=mesh,
        in_specs=(
            P((DP, TP), None),
            P((DP, TP), None),
            P(DP),
            P((DP, TP)),
            P(),
            P(DP, TP),
            P(DP, TP),
            P(DP, TP),
            P(DP, TP),
            P(DP, TP),
            P(DP, TP),
            P(),
            P(),
            P(),
            P(),
            P(),
            P(),
            P(DP, TP),
            P(),
            P(DP, TP),
            P(DP, TP),
            P(DP, TP),
        ),
        out_specs=(
            P((DP, TP), None),
            P(),
            P((DP, TP), None),
            P(),
            P(DP, TP),
            P(DP, TP),
            P(DP, TP),
            P(DP, TP),
            P(DP, TP),
            P(DP, TP),
            P(),
            P(),
            P(),
            P(),
            P(),
            P(),
            P(DP, TP),
            P(),
            P(DP, TP),
            P(DP, TP),
            P(DP, TP),
        ),
        check_vma=False,
    )
```

```python
import functools
from types import SimpleNamespace

import jax
import jax.numpy as jnp
from jax import lax
from jax.experimental import pallas as pl
from jax.experimental.pallas import tpu as pltpu
from jax.sharding import PartitionSpec as P

CH = 64
LENGTH = 1024


DP, TP = "dp", "tensor"
exact_precision = lax.Precision.HIGHEST


def rms_scale(values, gain):
    return values * lax.rsqrt(jnp.mean(values * values, axis=-1, keepdims=True) + 1e-06) * gain


def shift_masks(segment_ids, taps):
    masks = [jnp.ones(segment_ids.shape, jnp.float32)]
    for offset in range(1, taps):
        earlier = jnp.concatenate([jnp.full((offset,), -1, jnp.int32), segment_ids[:-offset]])
        masks.append((segment_ids == earlier).astype(jnp.float32))
    return masks


def short_conv(values, kernel, masks):
    result = values * kernel[0]
    for offset in range(1, len(masks)):
        shifted = jnp.concatenate(
            [jnp.zeros((offset, values.shape[1]), jnp.float32), values[:-offset]]
        )
        result = result + shifted * masks[offset][:, None] * kernel[offset]
    return result


def unit_rows(values):
    return values * lax.rsqrt(jnp.sum(values * values, axis=-1, keepdims=True) + 1e-06)


def lower_inverse(lower_part, length):
    negative = -lower_part
    inverse = jnp.eye(length, dtype=jnp.float32) + negative
    power = negative
    covered = 2
    while covered < length:
        power = jnp.einsum("hij,hjk->hik", power, power, precision=exact_precision)
        inverse = inverse + jnp.einsum("hij,hjk->hik", inverse, power, precision=exact_precision)
        covered = covered * 2
    return inverse


def block_update(state, inputs):
    queries, keys, values, betas, log_decay, seg_block, previous = inputs
    length = queries.shape[0]
    cumulative = jnp.cumsum(log_decay, axis=0)
    order = jnp.arange(length)
    causal = order[:, None] >= order[None, :]
    strict = order[:, None] > order[None, :]
    same_doc = seg_block[:, None] == seg_block[None, :]
    visible = (same_doc & causal)[:, :, None]
    spread = cumulative[:, None, :] - cumulative[None, :, :]
    weights = jnp.where(visible, jnp.exp(jnp.where(visible, spread, 0.0)), 0.0)
    carried = (seg_block == previous).astype(jnp.float32)
    carry_decay = jnp.exp(cumulative) * carried[:, None]
    key_gram = jnp.einsum("ihd,jhd->ijh", keys, keys, precision=exact_precision)
    lower_part = jnp.where(strict[:, :, None], betas[:, None, :] * weights * key_gram, 0.0)
    inverse = lower_inverse(jnp.transpose(lower_part, (2, 0, 1)), length)
    key_state = jnp.einsum("ihd,hde->ihe", keys, state, precision=exact_precision)
    target_rows = betas[:, :, None] * (values - carry_decay[:, :, None] * key_state)
    pseudo = jnp.einsum("hij,jhe->hie", inverse, target_rows, precision=exact_precision)
    scores = jnp.einsum("ihd,jhd->hij", queries, keys, precision=exact_precision) * jnp.transpose(
        weights, (2, 0, 1)
    )
    query_state = jnp.einsum("ihd,hde->ihe", queries, state, precision=exact_precision)
    outputs = carry_decay[:, :, None] * query_state + jnp.einsum(
        "hij,hje->ihe", scores, pseudo, precision=exact_precision
    )
    last_weights = weights[-1]
    new_state = (carried[-1] * jnp.exp(cumulative[-1]))[:, None, None] * state + jnp.einsum(
        "jh,jhd,hje->hde", last_weights, keys, pseudo, precision=exact_precision
    )
    return (new_state, outputs)


def mixer_sequence(
    q_pre,
    k_pre,
    v_pre,
    g_pre,
    a_pre,
    b_pre,
    segment_ids,
    conv_q,
    conv_k,
    conv_v,
    scale_rate,
    bias_rate,
    out_gain,
):
    length = q_pre.shape[0]
    heads = a_pre.shape[1]
    key_size = q_pre.shape[1] // heads
    value_size = v_pre.shape[1] // heads
    masks = shift_masks(segment_ids, conv_q.shape[0])
    queries = unit_rows(
        jax.nn.silu(short_conv(q_pre, conv_q, masks)).reshape(length, heads, key_size)
    ) * key_size ** (-0.5)
    keys = unit_rows(jax.nn.silu(short_conv(k_pre, conv_k, masks)).reshape(length, heads, key_size))
    values = jax.nn.silu(short_conv(v_pre, conv_v, masks)).reshape(length, heads, value_size)
    betas = jax.nn.sigmoid(b_pre)
    log_decay = -scale_rate * jax.nn.softplus(a_pre + bias_rate)
    blocks = length // CH
    seg_blocks = segment_ids.reshape(blocks, CH)
    previous = jnp.concatenate([jnp.full((1,), -1, jnp.int32), seg_blocks[:-1, -1]])
    state = jnp.zeros((heads, key_size, value_size), jnp.float32)
    carried_in = (
        queries.reshape(blocks, CH, heads, key_size),
        keys.reshape(blocks, CH, heads, key_size),
        values.reshape(blocks, CH, heads, value_size),
        betas.reshape(blocks, CH, heads),
        log_decay.reshape(blocks, CH, heads),
        seg_blocks,
        previous,
    )
    final_state, outputs = lax.scan(jax.checkpoint(block_update), state, carried_in)
    outputs = outputs.reshape(length, heads, value_size)
    gated = rms_scale(outputs, out_gain) * jax.nn.silu(g_pre.reshape(length, heads, value_size))
    return gated.reshape(length, heads * value_size)


def contract_rows(left, right):
    return lax.dot_general(
        left, right, (((0,), (0,)), ((), ())), preferred_element_type=jnp.float32
    )


def contract_cols(left, right):
    return lax.dot_general(
        left, right, (((1,), (1,)), ((), ())), preferred_element_type=jnp.float32
    )


def feed_inputs(normed_rows, gate_weight, up_weight):
    gate_pre = jnp.dot(normed_rows, gate_weight, preferred_element_type=jnp.float32)
    up_pre = jnp.dot(normed_rows, up_weight, preferred_element_type=jnp.float32)
    return (gate_pre, up_pre)


def on_device_split(
    layer_input,
    target,
    segment,
    pad_mask,
    norm1_gain,
    w_query,
    w_key,
    w_value,
    w_gate_out,
    w_decay,
    w_beta,
    conv_query,
    conv_key,
    conv_value,
    decay_scale,
    decay_bias,
    out_norm_gain,
    w_out,
    norm2_gain,
    w_ffn_gate,
    w_ffn_up,
    w_ffn_down,
):
    own_rows, width = layer_input.shape
    group_rows = segment.shape[0]
    sequences = group_rows // LENGTH
    tensor_index = lax.axis_index(TP)
    heads_local = w_decay.shape[1]
    query_cols = w_query.shape[1]
    value_cols = w_value.shape[1]
    input_float = layer_input.astype(jnp.float32)
    normed_own, norm1_pull = jax.vjp(rms_scale, input_float, norm1_gain)
    normed = lax.all_gather(normed_own.astype(jnp.bfloat16), TP, axis=0, tiled=True)
    full_query, full_key, full_value, full_gate, full_decay, full_beta, full_out = (
        lax.all_gather(w_query, DP, axis=0, tiled=True),
        lax.all_gather(w_key, DP, axis=0, tiled=True),
        lax.all_gather(w_value, DP, axis=0, tiled=True),
        lax.all_gather(w_gate_out, DP, axis=0, tiled=True),
        lax.all_gather(w_decay, DP, axis=0, tiled=True),
        lax.all_gather(w_beta, DP, axis=0, tiled=True),
        lax.all_gather(w_out, DP, axis=0, tiled=True),
    )
    proj_weights = (full_query, full_key, full_value, full_gate, full_decay, full_beta)
    projected = [
        jnp.dot(normed, weight, preferred_element_type=jnp.float32) for weight in proj_weights
    ]
    conv_q_local = lax.dynamic_slice_in_dim(conv_query, tensor_index * query_cols, query_cols, 1)
    conv_k_local = lax.dynamic_slice_in_dim(conv_key, tensor_index * query_cols, query_cols, 1)
    conv_v_local = lax.dynamic_slice_in_dim(conv_value, tensor_index * value_cols, value_cols, 1)
    scale_local = lax.dynamic_slice_in_dim(decay_scale, tensor_index * heads_local, heads_local, 0)
    bias_local = lax.dynamic_slice_in_dim(decay_bias, tensor_index * heads_local, heads_local, 0)
    seg_rows = segment.reshape(sequences, LENGTH)

    def mixer_local(
        q_pre,
        k_pre,
        v_pre,
        g_pre,
        a_pre,
        b_pre,
        conv_q,
        conv_k,
        conv_v,
        scale_rate,
        bias_rate,
        out_gain,
    ):
        shaped = [
            item.reshape(sequences, LENGTH, item.shape[1])
            for item in (q_pre, k_pre, v_pre, g_pre, a_pre, b_pre)
        ]
        mixed_rows = jax.vmap(
            mixer_sequence, in_axes=(0, 0, 0, 0, 0, 0, 0, None, None, None, None, None, None)
        )(*shaped, seg_rows, conv_q, conv_k, conv_v, scale_rate, bias_rate, out_gain)
        return mixed_rows.reshape(group_rows, mixed_rows.shape[2])

    mixed, mixer_pull = jax.vjp(
        mixer_local,
        *projected,
        conv_q_local,
        conv_k_local,
        conv_v_local,
        scale_local,
        bias_local,
        out_norm_gain
    )
    mixed_low = mixed.astype(jnp.bfloat16)
    attention = lax.psum_scatter(
        contract_cols(mixed_low, full_out), TP, scatter_dimension=0, tiled=True
    )
    residual = input_float + attention
    normed2_own, norm2_pull = jax.vjp(rms_scale, residual, norm2_gain)
    normed2 = lax.all_gather(normed2_own.astype(jnp.bfloat16), TP, axis=0, tiled=True)
    ffn_gate_w, ffn_up_w, ffn_down_w = (
        lax.all_gather(w_ffn_gate, DP, axis=0, tiled=True),
        lax.all_gather(w_ffn_up, DP, axis=0, tiled=True),
        lax.all_gather(w_ffn_down, DP, axis=0, tiled=True),
    )
    gate_pre, up_pre = feed_inputs(normed2, ffn_gate_w, ffn_up_w)
    hidden = (jax.nn.silu(gate_pre) * up_pre).astype(jnp.bfloat16)
    ffn_out = lax.psum_scatter(
        contract_cols(hidden, ffn_down_w).astype(jnp.bfloat16),
        TP,
        scatter_dimension=0,
        tiled=True,
    ).astype(jnp.float32)
    output = residual + ffn_out
    live = pad_mask.astype(jnp.float32)
    error = output - target.astype(jnp.float32)
    loss_sum, count = lax.psum(
        (jnp.sum(live[:, None] * error * error), jnp.sum(live)), (DP, TP)
    )
    loss = loss_sum / (count * width)
    all_tokens = own_rows * lax.axis_size(DP) * lax.axis_size(TP)
    grad_output = error * live[:, None] * (all_tokens / count)
    grad_ffn = lax.all_gather(grad_output.astype(jnp.bfloat16), TP, axis=0, tiled=True)
    grad_hidden = jnp.dot(grad_ffn, ffn_down_w, preferred_element_type=jnp.float32)
    sigmoid_gate = jax.nn.sigmoid(gate_pre)
    grad_gate = (
        grad_hidden * up_pre * sigmoid_gate * (1.0 + gate_pre * (1.0 - sigmoid_gate))
    ).astype(jnp.bfloat16)
    grad_up = (grad_hidden * gate_pre * sigmoid_gate).astype(jnp.bfloat16)
    grad_down_local = contract_rows(grad_ffn, hidden)
    grad_gate_local = contract_rows(normed2, grad_gate)
    grad_up_local = contract_rows(normed2, grad_up)
    normed2_part = contract_cols(grad_gate, ffn_gate_w) + contract_cols(grad_up, ffn_up_w)
    grad_normed2 = lax.psum_scatter(
        normed2_part.astype(jnp.bfloat16), TP, scatter_dimension=0, tiled=True
    ).astype(jnp.float32)
    grad_residual_norm, grad_gain_two = norm2_pull(grad_normed2)
    grad_residual = grad_output + grad_residual_norm
    grad_attention = lax.all_gather(
        grad_residual.astype(jnp.bfloat16), TP, axis=0, tiled=True
    )
    grad_mixed = jnp.dot(grad_attention, full_out, preferred_element_type=jnp.float32)
    grad_out_local = contract_rows(grad_attention, mixed_low)
    mixer_grads = mixer_pull(grad_mixed)
    pre_grads = [item.astype(jnp.bfloat16) for item in mixer_grads[:6]]
    normed_part = contract_cols(pre_grads[0], full_query)
    for grad_item, weight in zip(pre_grads[1:], proj_weights[1:]):
        normed_part = normed_part + contract_cols(grad_item, weight)
    weight_locals = [contract_rows(normed, grad_item) for grad_item in pre_grads]
    grad_normed = lax.psum_scatter(
        normed_part.astype(jnp.bfloat16), TP, scatter_dimension=0, tiled=True
    ).astype(jnp.float32)
    grad_input_norm, grad_gain_one = norm1_pull(grad_normed)
    grad_input = grad_residual + grad_input_norm
    owned = (
        lax.psum_scatter(
            grad_gate_local.astype(jnp.bfloat16), DP, scatter_dimension=0, tiled=True
        ).astype(jnp.float32),
        lax.psum_scatter(
            grad_up_local.astype(jnp.bfloat16), DP, scatter_dimension=0, tiled=True
        ).astype(jnp.float32),
        lax.psum_scatter(
            grad_down_local.astype(jnp.bfloat16), DP, scatter_dimension=0, tiled=True
        ).astype(jnp.float32),
        lax.psum_scatter(
            weight_locals[0].astype(jnp.bfloat16), DP, scatter_dimension=0, tiled=True
        ).astype(jnp.float32),
        lax.psum_scatter(
            weight_locals[1].astype(jnp.bfloat16), DP, scatter_dimension=0, tiled=True
        ).astype(jnp.float32),
        lax.psum_scatter(
            weight_locals[2].astype(jnp.bfloat16), DP, scatter_dimension=0, tiled=True
        ).astype(jnp.float32),
        lax.psum_scatter(
            weight_locals[3].astype(jnp.bfloat16), DP, scatter_dimension=0, tiled=True
        ).astype(jnp.float32),
        lax.psum_scatter(
            weight_locals[4].astype(jnp.bfloat16), DP, scatter_dimension=0, tiled=True
        ).astype(jnp.float32),
        lax.psum_scatter(
            weight_locals[5].astype(jnp.bfloat16), DP, scatter_dimension=0, tiled=True
        ).astype(jnp.float32),
        lax.psum_scatter(
            grad_out_local.astype(jnp.bfloat16), DP, scatter_dimension=0, tiled=True
        ).astype(jnp.float32),
    )
    conv_q_full = lax.dynamic_update_slice_in_dim(
        jnp.zeros_like(conv_query), mixer_grads[6], tensor_index * query_cols, 1
    )
    conv_k_full = lax.dynamic_update_slice_in_dim(
        jnp.zeros_like(conv_key), mixer_grads[7], tensor_index * query_cols, 1
    )
    conv_v_full = lax.dynamic_update_slice_in_dim(
        jnp.zeros_like(conv_value), mixer_grads[8], tensor_index * value_cols, 1
    )
    scale_full = lax.dynamic_update_slice_in_dim(
        jnp.zeros_like(decay_scale), mixer_grads[9], tensor_index * heads_local, 0
    )
    bias_full = lax.dynamic_update_slice_in_dim(
        jnp.zeros_like(decay_bias), mixer_grads[10], tensor_index * heads_local, 0
    )
    summed = lax.psum(
        (
            grad_gain_one,
            grad_gain_two,
            conv_q_full,
            conv_k_full,
            conv_v_full,
            scale_full,
            bias_full,
            mixer_grads[11],
        ),
        (DP, TP),
    )
    return (
        output,
        loss,
        grad_input,
        summed[0],
        owned[3],
        owned[4],
        owned[5],
        owned[6],
        owned[7],
        owned[8],
        summed[2],
        summed[3],
        summed[4],
        summed[5],
        summed[6],
        summed[7],
        owned[9],
        summed[1],
        owned[0],
        owned[1],
        owned[2],
    )


CORE, SIDE, TENSOR, PLACE = 1, 2, 3, 0
TENSOR_FIRST = (CORE, TENSOR, SIDE, PLACE)
SIDE_FIRST = (CORE, SIDE, TENSOR, PLACE)
TILE = 128
DONE = object()
COST = 4 * 10**10


def mm(left, right, dims=((1,), (0,))):
    return lax.dot_general(
        left.astype(jnp.bfloat16),
        right.astype(jnp.bfloat16),
        (dims, ((), ())),
        preferred_element_type=jnp.float32,
    )


def mm_nt(left, right):
    return mm(left, right, ((1,), (1,)))


def mm_tn(left, right):
    return mm(left, right, ((0,), (0,)))


def mm_fine(left, right):
    left_high, right_high = left.astype(jnp.bfloat16), right.astype(jnp.bfloat16)
    left_rest = left - left_high.astype(jnp.float32)
    right_rest = right - right_high.astype(jnp.float32)
    return mm(left_high, right_high) + (mm(left_high, right_rest) + mm(left_rest, right_high))


def ones_mm(ones, right):
    high = right.astype(jnp.bfloat16)
    rest = right - high.astype(jnp.float32)
    middle = rest.astype(jnp.bfloat16)
    return mm(ones, high) + (mm(ones, middle) + mm(ones, rest - middle.astype(jnp.float32)))


def unit_lower_inverses(parts, row, col):
    size = parts[0].shape[0]
    eye = (row == col).astype(jnp.float32)
    block = 16
    inside = (row // block) == (col // block)
    powers = [jnp.where(inside, -part, 0.0) for part in parts]
    inverses = [eye + power for power in powers]
    covered = 2
    while covered < block:
        powers = [mm_fine(power, power) for power in powers]
        moves = [mm_fine(inverse, power) for inverse, power in zip(inverses, powers)]
        inverses = [inverse + move for inverse, move in zip(inverses, moves)]
        covered *= 2
    while block < size:
        cross = ((row // (2 * block)) == (col // (2 * block))) & (
            (row // block) != (col // block)
        )
        lows = [inverse.astype(jnp.bfloat16) for inverse in inverses]
        moves = [mm(low, jnp.where(cross, part, 0.0)) for low, part in zip(lows, parts)]
        moves = [mm(move, low) for move, low in zip(moves, lows)]
        inverses = [inverse - move for inverse, move in zip(inverses, moves)]
        block *= 2
    return inverses


def stable_softplus(values):
    return jnp.maximum(values, 0.0) + jnp.log1p(jnp.exp(-jnp.abs(values)))


def decay_tiles(raw, rate, bias):
    shifted = raw + bias
    soft = stable_softplus(shifted)
    return shifted, soft, -rate * soft


def grids():
    row = lax.broadcasted_iota(jnp.int32, (TILE, TILE), 0)
    col = lax.broadcasted_iota(jnp.int32, (TILE, TILE), 1)
    return row, col


def forward_body(
    heads,
    proj_ref,
    info_ref,
    conv_ref,
    rates_ref,
    gain_ref,
    mixed_ref,
    conv_out_ref,
    rows_out_ref,
    state_out_ref,
    inverse_out_ref,
    pseudo_out_ref,
    earlier_ref,
    state_ref,
):
    first = pl.program_id(2) == 0
    blocks = 4 * heads

    @pl.when(first)
    def _():
        earlier_ref[:, 0:8, :] = jnp.zeros((blocks, 8, TILE), jnp.float32)
        state_ref[...] = jnp.zeros(state_ref.shape, jnp.float32)

    row, col = grids()
    info = info_ref[...]
    info_rows = info.T
    masks = [jnp.broadcast_to(info[:, j : j + 1], (TILE, TILE)) for j in range(3)]
    visible = (row >= col) & (info[:, 4:5] == info_rows[4:5, :])
    raw = proj_ref[0, :, 6 * heads * TILE : 6 * heads * TILE + TILE]
    _, _, log_decay = decay_tiles(raw, rates_ref[0, 0:1, :], rates_ref[0, 1:2, :])
    total = ones_mm((row >= col).astype(jnp.float32), log_decay)
    total_rows = total.T
    carry = jnp.exp(total) * info[:, 3:4]
    beta_tile = jax.nn.sigmoid(raw)
    for block in range(blocks):
        earlier_ref[block, 8 : 8 + TILE, :] = proj_ref[0, :, block * TILE : (block + 1) * TILE]

    def conv_block(block):
        lanes = slice(block * TILE, (block + 1) * TILE)
        result = earlier_ref[block, 8 : 8 + TILE, :] * conv_ref[0, 0:1, lanes]
        for j in range(1, 4):
            result = result + masks[j - 1] * (
                earlier_ref[block, 8 - j : 8 - j + TILE, :] * conv_ref[0, j : j + 1, lanes]
            )
        conv_out_ref[0, :, lanes] = result
        return result * jax.nn.sigmoid(result)

    every = range(heads)
    queries, keys, values, parts, scores = [], [], [], [], []
    for head in every:
        query, key = conv_block(head), conv_block(heads + head)
        query = query * (
            lax.rsqrt(jnp.sum(query * query, axis=1, keepdims=True) + 1e-06) * TILE ** (-0.5)
        )
        key = key * lax.rsqrt(jnp.sum(key * key, axis=1, keepdims=True) + 1e-06)
        spread = total[:, head : head + 1] - total_rows[head : head + 1, :]
        weights = jnp.exp(jnp.where(visible, spread, -1e30))
        key_low, query_low = key.astype(jnp.bfloat16), query.astype(jnp.bfloat16)
        grams = mm_nt(jnp.concatenate([key_low, query_low], axis=0), key_low)
        beta = beta_tile[:, heads + head : heads + head + 1]
        parts.append(jnp.where(row > col, beta * weights * grams[:TILE], 0.0))
        scores.append((grams[TILE:] * weights).astype(jnp.bfloat16))
        queries.append(query_low)
        keys.append((key_low, (key.T * weights[TILE - 1 : TILE, :]).astype(jnp.bfloat16)))
    for head in every:
        values.append(
            jnp.concatenate(
                [conv_block(2 * heads + 2 * head), conv_block(2 * heads + 2 * head + 1)], axis=1
            )
        )
    inverses = [item.astype(jnp.bfloat16) for item in unit_lower_inverses(parts, row, col)]
    states = [state_ref[head] for head in every]
    lows = [state.astype(jnp.bfloat16) for state in states]
    from_states = [
        mm(jnp.concatenate([keys[head][0], queries[head]], axis=0), lows[head]) for head in every
    ]
    carries = [carry[:, head : head + 1] for head in every]
    pseudos = [
        mm(
            inverses[head],
            beta_tile[:, heads + head : heads + head + 1]
            * (values[head] - carries[head] * from_states[head][:TILE]),
        ).astype(jnp.bfloat16)
        for head in every
    ]
    for head in every:
        lanes = slice(2 * head * TILE, 2 * (head + 1) * TILE)
        carried, pseudo = carries[head], pseudos[head]
        state_ref[head] = carried[TILE - 1 : TILE, :] * states[head] + mm(keys[head][1], pseudo)
        rows = carried * from_states[head][TILE:] + mm(scores[head], pseudo)
        state_out_ref[0, 0, head] = lows[head]
        inverse_out_ref[0, 0, head] = inverses[head]
        pseudo_out_ref[0, :, lanes] = pseudo
        rows_out_ref[0, :, lanes] = rows
        gate = proj_ref[
            0, :, (4 * heads + 2 * head) * TILE : (4 * heads + 2 * (head + 1)) * TILE
        ]
        scale = lax.rsqrt(jnp.mean(rows * rows, axis=1, keepdims=True) + 1e-06)
        mixed_ref[:, lanes] = (
            rows * scale * gain_ref[...] * (gate * jax.nn.sigmoid(gate))
        ).astype(jnp.bfloat16)
    for block in range(blocks):
        earlier_ref[block, 0:8, :] = earlier_ref[block, TILE : TILE + 8, :]


def backward_body(
    heads,
    proj_ref,
    info_ref,
    conv_ref,
    rates_ref,
    gain_ref,
    conv_out_ref,
    rows_ref,
    state_in_ref,
    inverse_ref,
    pseudo_ref,
    grad_ref,
    grad_proj_ref,
    grad_conv_ref,
    grad_rates_ref,
    grad_gain_ref,
    later_ref,
    grad_state_ref,
):
    step = pl.program_id(2)
    blocks = 4 * heads

    @pl.when(step == 0)
    def _():
        later_ref[:, TILE : TILE + 8, :] = jnp.zeros((blocks, 8, TILE), jnp.float32)
        grad_state_ref[...] = jnp.zeros(grad_state_ref.shape, jnp.float32)

    @pl.when((step == 0) & (pl.program_id(1) == 0))
    def _():
        grad_conv_ref[...] = jnp.zeros(grad_conv_ref.shape, jnp.float32)
        grad_rates_ref[...] = jnp.zeros(grad_rates_ref.shape, jnp.float32)
        grad_gain_ref[...] = jnp.zeros(grad_gain_ref.shape, jnp.float32)

    row, col = grids()
    info = info_ref[...]
    info_rows = info.T
    masks = [jnp.broadcast_to(info[:, 4 + j : 5 + j], (TILE, TILE)) for j in range(1, 4)]
    visible = (row >= col) & (info[:, 4:5] == info_rows[4:5, :])
    raw = proj_ref[0, :, 6 * heads * TILE : 6 * heads * TILE + TILE]
    rate = rates_ref[0, 0:1, :]
    shifted, soft, log_decay = decay_tiles(raw, rate, rates_ref[0, 1:2, :])
    total = ones_mm((row >= col).astype(jnp.float32), log_decay)
    total_rows = total.T
    carry = jnp.exp(total) * info[:, 3:4]
    beta_tile = jax.nn.sigmoid(raw)
    grad_total = jnp.zeros((TILE, TILE), jnp.float32)
    grad_beta = jnp.zeros((TILE, TILE), jnp.float32)
    gain = gain_ref[...]
    gain_sum = jnp.zeros((1, 2 * TILE), jnp.float32)

    def activation(block):
        value = conv_out_ref[0, :, block * TILE : (block + 1) * TILE]
        gate = jax.nn.sigmoid(value)
        return value * gate, gate * (1.0 + value * (1.0 - gate))

    def close_block(block, grad):
        later_ref[block, 0:TILE, :] = grad
        lanes = slice(block * TILE, (block + 1) * TILE)
        own = proj_ref[0, :, lanes]
        result = grad * conv_ref[0, 0:1, lanes]
        sums = [jnp.sum(grad * own, axis=0, keepdims=True)]
        for j in range(1, 4):
            moved = masks[j - 1] * later_ref[block, j : j + TILE, :]
            result = result + moved * conv_ref[0, j : j + 1, lanes]
            sums.append(jnp.sum(moved * own, axis=0, keepdims=True))
        grad_proj_ref[0, :, lanes] = result.astype(jnp.bfloat16)
        for j in range(4):
            grad_conv_ref[0, j : j + 1, lanes] += sums[j]

    def head_steps(head):
        lanes = slice(2 * head * TILE, 2 * (head + 1) * TILE)
        gate_lanes = slice((4 * heads + 2 * head) * TILE, (4 * heads + 2 * (head + 1)) * TILE)
        rows = rows_ref[0, :, lanes]
        gate = proj_ref[0, :, gate_lanes]
        grad = grad_ref[:, lanes]
        scale = lax.rsqrt(jnp.mean(rows * rows, axis=1, keepdims=True) + 1e-06)
        level = rows * scale
        sigmoid = jax.nn.sigmoid(gate)
        through = grad * (gate * sigmoid)
        gain_sums.append(jnp.sum(through * level, axis=0, keepdims=True))
        grad_proj_ref[0, :, gate_lanes] = (
            grad * level * gain * (sigmoid * (1.0 + gate * (1.0 - sigmoid)))
        ).astype(jnp.bfloat16)
        through = through * gain
        grad_rows = scale * (
            through - level * jnp.mean(through * level, axis=1, keepdims=True)
        )

        yield
        query_act, query_slope = activation(head)
        query_scale = lax.rsqrt(jnp.sum(query_act * query_act, axis=1, keepdims=True) + 1e-06)
        query_unit = query_act * query_scale
        query = query_unit * TILE ** (-0.5)
        key_act, key_slope = activation(heads + head)
        key_scale = lax.rsqrt(jnp.sum(key_act * key_act, axis=1, keepdims=True) + 1e-06)
        key = key_act * key_scale
        value_parts = [activation(2 * heads + 2 * head), activation(2 * heads + 2 * head + 1)]
        value = jnp.concatenate([value_parts[0][0], value_parts[1][0]], axis=1)

        yield
        spread = total[:, head : head + 1] - total_rows[head : head + 1, :]
        weights = jnp.exp(jnp.where(visible, spread, -1e30))
        beta = beta_tile[:, heads + head : heads + head + 1]
        carried = carry[:, head : head + 1]
        key_low, query_low = key.astype(jnp.bfloat16), query.astype(jnp.bfloat16)
        both = jnp.concatenate([key_low, query_low], axis=0)
        grams = mm_nt(both, key_low)
        yield
        state_low = state_in_ref[0, 0, head]
        inverse = inverse_ref[0, 0, head]
        pseudo = pseudo_ref[0, :, lanes]
        grad_state = grad_state_ref[head]
        grad_state_low = grad_state.astype(jnp.bfloat16)
        last_row = weights[TILE - 1 : TILE, :]
        last_col = jnp.sum(jnp.where(row == col, last_row, 0.0), axis=1, keepdims=True)
        grad_rows_low = grad_rows.astype(jnp.bfloat16)
        grad_pseudo = mm_tn(grams[TILE:] * weights, grad_rows_low) + mm(
            last_col * key, grad_state_low
        )
        yield
        solved = mm_tn(inverse, grad_pseudo)
        yield
        crossed = mm_nt(
            jnp.concatenate([grad_rows_low, solved.astype(jnp.bfloat16)], axis=0), pseudo
        )
        yield
        grad_scores = crossed[:TILE] * weights
        below = jnp.where(row > col, crossed[TILE:] * weights, 0.0)
        grad_gram = (-beta) * below
        grad_value = beta * solved
        from_state = mm(key_low, state_low)
        grad_beta_col = jnp.sum(
            solved * (value - carried * from_state), axis=1, keepdims=True
        ) - jnp.sum(below * grams[:TILE], axis=1, keepdims=True)
        yield
        out_part = (carried * grad_rows).astype(jnp.bfloat16)
        key_part = ((-carried) * grad_value).astype(jnp.bfloat16)
        stacked = jnp.concatenate([out_part, key_part], axis=0)
        to_inputs = mm_nt(stacked, state_low)
        yield
        scores_low, gram_low = grad_scores.astype(jnp.bfloat16), grad_gram.astype(jnp.bfloat16)
        grad_query = mm(scores_low, key_low) + to_inputs[:TILE]
        key_own = mm(gram_low, key_low) + to_inputs[TILE:]
        key_rest = mm_tn(
            jnp.concatenate([gram_low, scores_low], axis=0), both
        )
        key_state = last_col * mm_nt(pseudo, grad_state_low)
        grad_key = key_own + key_rest + key_state
        grad_state_ref[head] = carried[TILE - 1 : TILE, :] * grad_state + mm_tn(
            jnp.concatenate([query_low, key_low], axis=0), stacked
        )
        yield
        key_exact, query_exact = key_low.astype(jnp.float32), query_low.astype(jnp.float32)
        state_dot = jnp.sum(key_state * key_exact, axis=1, keepdims=True)
        tail = jnp.sum(state_dot, axis=0, keepdims=True) + carried[TILE - 1 : TILE, :] * jnp.sum(
            jnp.sum(grad_state * state_low.astype(jnp.float32), axis=1, keepdims=True),
            axis=0,
            keepdims=True,
        )
        grad_total_col = (
            jnp.sum(
                grad_query * query_exact + (key_own - key_rest) * key_exact, axis=1, keepdims=True
            )
            - state_dot
            + jnp.where(row[:, 0:1] == TILE - 1, tail, 0.0)
        )
        columns_of[head] = (grad_total_col, grad_beta_col)
        yield

        grad_query = grad_query * TILE ** (-0.5)
        close_block(
            head,
            query_scale
            * (
                grad_query
                - query_unit * jnp.sum(grad_query * query_unit, axis=1, keepdims=True)
            )
            * query_slope,
        )
        yield
        close_block(
            heads + head,
            key_scale
            * (grad_key - key * jnp.sum(grad_key * key, axis=1, keepdims=True))
            * key_slope,
        )
        yield
        close_block(2 * heads + 2 * head, grad_value[:, :TILE] * value_parts[0][1])
        close_block(2 * heads + 2 * head + 1, grad_value[:, TILE:] * value_parts[1][1])

    gain_sums, columns_of = [], {}
    waiting = [head_steps(head) for head in range(heads)]
    while waiting:
        waiting = [steps for steps in waiting if next(steps, DONE) is not DONE]
    for head in range(heads):
        grad_total = jnp.where(col == head, columns_of[head][0], grad_total)
        grad_beta = jnp.where(col == heads + head, columns_of[head][1], grad_beta)
        gain_sum = gain_sum + gain_sums[head]

    grad_log = ones_mm((row <= col).astype(jnp.float32), grad_total)
    grad_raw = -rate * grad_log * jax.nn.sigmoid(shifted)
    grad_rates_ref[0, 0:1, :] += -jnp.sum(grad_log * soft, axis=0, keepdims=True)
    grad_rates_ref[0, 1:2, :] += jnp.sum(grad_raw, axis=0, keepdims=True)
    grad_gain_ref[0, 0:1, :] += gain_sum
    grad_proj_ref[0, :, 6 * heads * TILE : 6 * heads * TILE + TILE] = jnp.where(
        col < heads, grad_raw, grad_beta * beta_tile * (1.0 - beta_tile)
    ).astype(jnp.bfloat16)
    for block in range(blocks):
        later_ref[block, TILE : TILE + 8, :] = later_ref[block, 0:8, :]


def mixer_specs(parts, rows, wide, heads, blocks, backward):
    conv_cols, value_cols = 4 * heads * TILE, 2 * heads * TILE

    def place(s, c):
        return s * blocks + ((blocks - 1 - c) if backward else c)

    return SimpleNamespace(
        proj=pl.BlockSpec((1, TILE, wide), lambda p, s, c: (p, place(s, c), 0)),
        info=pl.BlockSpec((TILE, TILE), lambda p, s, c: (place(s, c), 0)),
        conv=pl.BlockSpec((1, 8, conv_cols), lambda p, s, c: (p, 0, 0)),
        rates=pl.BlockSpec((1, 8, TILE), lambda p, s, c: (p, 0, 0)),
        gain=pl.BlockSpec((1, 2 * TILE), lambda p, s, c: (0, 0)),
        flat=pl.BlockSpec((TILE, value_cols), lambda p, s, c: (place(s, c), p)),
        conv_out=pl.BlockSpec((1, TILE, conv_cols), lambda p, s, c: (p, place(s, c), 0)),
        value=pl.BlockSpec((1, TILE, value_cols), lambda p, s, c: (p, place(s, c), 0)),
        state=pl.BlockSpec(
            (1, 1, heads, TILE, 2 * TILE), lambda p, s, c: (p, place(s, c), 0, 0, 0)
        ),
        inverse=pl.BlockSpec(
            (1, 1, heads, TILE, TILE), lambda p, s, c: (p, place(s, c), 0, 0, 0)
        ),
        gain_sum=pl.BlockSpec((1, 8, 2 * TILE), lambda p, s, c: (p, 0, 0)),
    )


def mixer_forward(proj, info, conv, rates, gain, heads):
    parts, rows, wide = proj.shape
    blocks = LENGTH // TILE
    spec = mixer_specs(parts, rows, wide, heads, blocks, False)
    conv_cols, value_cols = 4 * heads * TILE, 2 * heads * TILE
    low, full = jnp.bfloat16, jnp.float32
    return pl.pallas_call(
        functools.partial(forward_body, heads),
        grid=(parts, rows // LENGTH, blocks),
        in_specs=[spec.proj, spec.info, spec.conv, spec.rates, spec.gain],
        out_specs=[
            spec.flat, spec.conv_out, spec.value, spec.state, spec.inverse, spec.value
        ],
        out_shape=[
            jax.ShapeDtypeStruct((rows, parts * value_cols), low),
            jax.ShapeDtypeStruct((parts, rows, conv_cols), full),
            jax.ShapeDtypeStruct((parts, rows, value_cols), full),
            jax.ShapeDtypeStruct((parts, rows // TILE, heads, TILE, 2 * TILE), low),
            jax.ShapeDtypeStruct((parts, rows // TILE, heads, TILE, TILE), low),
            jax.ShapeDtypeStruct((parts, rows, value_cols), low),
        ],
        scratch_shapes=[
            pltpu.VMEM((4 * heads, TILE + 8, TILE), full),
            pltpu.VMEM((heads, TILE, 2 * TILE), full),
        ],
        compiler_params=pltpu.CompilerParams(
            vmem_limit_bytes=48 * 1024 * 1024,
        ),
        cost_estimate=pl.CostEstimate(flops=COST, transcendentals=0, bytes_accessed=10**8),
        name="mixer_forward",
    )(proj, info, conv, rates, gain)


def mixer_backward(proj, info, conv, rates, gain, saved, grad, heads):
    parts, rows, wide = proj.shape
    blocks = LENGTH // TILE
    spec = mixer_specs(parts, rows, wide, heads, blocks, True)
    conv_cols = 4 * heads * TILE
    low, full = jnp.bfloat16, jnp.float32
    return pl.pallas_call(
        functools.partial(backward_body, heads),
        grid=(parts, rows // LENGTH, blocks),
        in_specs=[
            spec.proj, spec.info, spec.conv, spec.rates, spec.gain,
            spec.conv_out, spec.value, spec.state, spec.inverse, spec.value, spec.flat,
        ],
        out_specs=[spec.proj, spec.conv, spec.rates, spec.gain_sum],
        out_shape=[
            jax.ShapeDtypeStruct((parts, rows, wide), low),
            jax.ShapeDtypeStruct((parts, 8, conv_cols), full),
            jax.ShapeDtypeStruct((parts, 8, TILE), full),
            jax.ShapeDtypeStruct((parts, 8, 2 * TILE), full),
        ],
        scratch_shapes=[
            pltpu.VMEM((4 * heads, TILE + 8, TILE), full),
            pltpu.VMEM((heads, TILE, 2 * TILE), full),
        ],
        compiler_params=pltpu.CompilerParams(
            vmem_limit_bytes=48 * 1024 * 1024,
        ),
        cost_estimate=pl.CostEstimate(flops=COST, transcendentals=0, bytes_accessed=10**8),
        name="mixer_backward",
    )(proj, info, conv, rates, gain, *saved, grad)


BLOCK = 256


def rms_backward(values, gain, grad):
    scale = lax.rsqrt(jnp.mean(values * values, axis=1, keepdims=True) + 1e-06)
    level = values * scale
    through = grad * gain
    back = scale * (through - level * jnp.mean(through * level, axis=1, keepdims=True))
    return back, jnp.sum(grad * level, axis=0, keepdims=True)


def dense_forward_body(
    normed_ref,
    gate_w_ref,
    up_w_ref,
    down_w_ref,
    residual_ref,
    target_ref,
    live_ref,
    level_ref,
    gate_ref,
    up_ref,
    hidden_ref,
    output_ref,
    grad_ref,
    grad_turned_ref,
    loss_ref,
    total_ref,
):
    part, step = pl.program_id(0), pl.program_id(1)
    normed = normed_ref[...]
    gate = mm(normed, gate_w_ref[0])
    up = mm(normed, up_w_ref[0])
    hidden = (gate * jax.nn.sigmoid(gate) * up).astype(jnp.bfloat16)
    gate_ref[0] = gate.astype(jnp.bfloat16)
    up_ref[0] = up.astype(jnp.bfloat16)
    hidden_ref[0] = hidden
    share = mm_nt(hidden, down_w_ref[0])
    rows = pl.ds(pl.multiple_of(step * BLOCK, BLOCK), BLOCK)

    @pl.when(part == 0)
    def _():
        total_ref[rows, :] = share

    @pl.when(part == pl.num_programs(0) - 1)
    def _():
        output = residual_ref[...] + (total_ref[rows, :] + share)
        output_ref[...] = output
        error = output - target_ref[...].astype(jnp.float32)
        live = live_ref[:, 0:1]
        grad = error * live * level_ref[0:1, 0:1]
        grad_ref[...] = grad.astype(jnp.bfloat16)
        grad_turned_ref[...] = grad.T.astype(jnp.bfloat16)
        squares = jnp.sum(live * error * error, axis=0, keepdims=True)

        @pl.when(step == 0)
        def _():
            loss_ref[...] = jnp.zeros(loss_ref.shape, jnp.float32)

        loss_ref[0:1, :] += squares


def dense_backward_body(
    grad_ref,
    gate_w_ref,
    up_w_ref,
    down_w_ref,
    gate_ref,
    up_ref,
    residual_ref,
    output_ref,
    target_ref,
    live_ref,
    level_ref,
    gain_ref,
    grad_gate_ref,
    grad_up_ref,
    back_ref,
    back_low_ref,
    back_turned_ref,
    gain_sum_ref,
    total_ref,
):
    part, step = pl.program_id(0), pl.program_id(1)
    grad_hidden = mm(grad_ref[...], down_w_ref[0])
    gate = gate_ref[0].astype(jnp.float32)
    up = up_ref[0].astype(jnp.float32)
    sigmoid = jax.nn.sigmoid(gate)
    grad_gate = (grad_hidden * up * sigmoid * (1.0 + gate * (1.0 - sigmoid))).astype(jnp.bfloat16)
    grad_up = (grad_hidden * gate * sigmoid).astype(jnp.bfloat16)
    grad_gate_ref[0] = grad_gate
    grad_up_ref[0] = grad_up
    share = mm_nt(grad_gate, gate_w_ref[0]) + mm_nt(grad_up, up_w_ref[0])
    rows = pl.ds(pl.multiple_of(step * BLOCK, BLOCK), BLOCK)

    @pl.when(part == 0)
    def _():
        total_ref[rows, :] = share

    @pl.when(part == pl.num_programs(0) - 1)
    def _():
        error = output_ref[...] - target_ref[...].astype(jnp.float32)
        back, gain_sum = rms_backward(
            residual_ref[...], gain_ref[...], total_ref[rows, :] + share
        )
        back = error * live_ref[:, 0:1] * level_ref[0:1, 0:1] + back
        back_ref[...] = back
        back_low_ref[...] = back.astype(jnp.bfloat16)
        back_turned_ref[...] = back.T.astype(jnp.bfloat16)

        @pl.when(step == 0)
        def _():
            gain_sum_ref[...] = jnp.zeros(gain_sum_ref.shape, jnp.float32)

        gain_sum_ref[0:1, :] += gain_sum


def input_backward_body(
    first_ref, second_ref, weight_ref, input_ref, residual_ref, gain_ref, back_ref, gain_sum_ref, total_ref
):
    part, step = pl.program_id(0), pl.program_id(1)
    grad = jnp.where(part == 0, first_ref[0], second_ref[0])
    share = mm_nt(grad, weight_ref[0])
    rows = pl.ds(pl.multiple_of(step * BLOCK, BLOCK), BLOCK)

    @pl.when(part == 0)
    def _():
        total_ref[rows, :] = share

    @pl.when(part == pl.num_programs(0) - 1)
    def _():
        back, gain_sum = rms_backward(
            input_ref[...].astype(jnp.float32), gain_ref[...], total_ref[rows, :] + share
        )
        back_ref[...] = residual_ref[...] + back

        @pl.when(step == 0)
        def _():
            gain_sum_ref[...] = jnp.zeros(gain_sum_ref.shape, jnp.float32)

        gain_sum_ref[0:1, :] += gain_sum


def dense_call(body, flags, arrays, choose, width, units):
    rows = arrays[0].shape[-2]
    full, low = jnp.float32, jnp.bfloat16

    def cut(block, place, shape=None, kind=full):
        return (pl.BlockSpec(block, place), jax.ShapeDtypeStruct(shape or block, kind))

    late = (lambda p, i, flags: (i * p, 0), (rows, width))
    spec = SimpleNamespace(
        row=cut((BLOCK, width), lambda p, i, flags: (i, 0)),
        late=cut((BLOCK, width), *late),
        late_low=cut((BLOCK, width), *late, low),
        turned=cut((width, BLOCK), lambda p, i, flags: (0, i * p), (width, rows), low),
        unit=cut((1, BLOCK, units), lambda p, i, flags: (p, i, 0), (2, rows, units), low),
        first=cut((1, BLOCK, units), lambda p, i, flags: (0, i * (1 - p), 0)),
        second=cut((1, BLOCK, units), lambda p, i, flags: (0, i * p, 0)),
        lane=cut((BLOCK, TILE), lambda p, i, flags: (i * p, 0)),
        level=cut((8, TILE), lambda p, i, flags: (0, 0)),
        gain=cut((1, width), lambda p, i, flags: (0, 0)),
        own=cut((1, width, units), lambda p, i, flags: (lax.rem(p + 1 + flags[1], 2), 0, 0)),
        sums=cut((8, width), lambda p, i, flags: (0, 0)),
        weights=[
            cut((1, width, units), lambda p, i, flags, index=index: (p, 0, index)) for index in range(3)
        ],
    )
    taken, given = choose(spec)
    return pl.pallas_call(
        lambda flags_ref, *refs: body(*refs),
        grid_spec=pltpu.PrefetchScalarGridSpec(
            num_scalar_prefetch=1,
            grid=(2, rows // BLOCK),
            in_specs=[item[0] for item in taken],
            out_specs=[item[0] for item in given],
            scratch_shapes=[pltpu.VMEM((rows, width), full)],
        ),
        out_shape=[item[1] for item in given],
        compiler_params=pltpu.CompilerParams(vmem_limit_bytes=56 * 1024 * 1024),
        cost_estimate=pl.CostEstimate(flops=COST, transcendentals=0, bytes_accessed=10**8),
        name=body.__name__[:-5],
    )(flags, *arrays)


def product_body(own, side_first, flags_ref, left_ref, first_ref, second_ref, *refs):
    part = pl.program_id(0)
    shape = left_ref.shape
    left = left_ref[...].reshape(shape[0] * shape[2], shape[3])

    def finish(right_ref):
        result = mm(left, right_ref[...].reshape(right_ref.shape[-2:]))
        if own:
            result = result + refs[0][0].astype(jnp.float32)
        result = result.astype(jnp.bfloat16)
        if not side_first:
            refs[-1][0] = result
            return
        split = result.reshape(shape[0] // 2, 2, shape[2], result.shape[1])
        count = shape[0] * shape[2] // 2
        low = split[:, 0].reshape(count, -1)
        high = split[:, 1].reshape(count, -1)
        here = flags_ref[2] == 0
        refs[-2][0] = jnp.where(here, low, high)
        refs[-1][0] = jnp.where(here, high, low)

    @pl.when(part == 0)
    def _():
        finish(first_ref)

    @pl.when(part == 1)
    def _():
        finish(second_ref)


def product(flags, left, rights, received=None, side_first=False, relative=False):
    own = received is not None
    side_first = side_first and own
    groups, _, rows, tokens = left.shape
    cols, count = rights[0].shape[-1], len(rights)
    block = cols if count == 2 else -(-cols // (2 * TILE)) * TILE
    last = -(-cols // block) - 1

    def slot(p, flags):
        return 0 if count == 1 else 1 - p if relative else lax.rem(p + flags[1], 2)

    def right_spec(array, index, which):
        def place(p, j, flags):
            return j * (1 - p) + last * p if which == 0 else j * p

        if array.ndim == 3:
            return pl.BlockSpec(
                (1, tokens, block), lambda p, j, flags: (index, 0, place(p, j, flags))
            )
        return pl.BlockSpec((tokens, block), lambda p, j, flags: (0, place(p, j, flags)))

    result_rows = groups * rows // (2 if side_first else 1)
    result = pl.BlockSpec((1, result_rows, block), lambda p, j, flags: (slot(p, flags), 0, j))
    kept = jax.ShapeDtypeStruct((count, result_rows, cols), jnp.bfloat16)
    in_specs = [
        pl.BlockSpec(
            (groups, 1, rows, tokens),
            lambda p, j, flags: (0, flags[0] if own else 1 - flags[0], 0, 0),
        ),
        right_spec(rights[0], 0, 0),
        right_spec(rights[-1], rights[-1].shape[0] - 1, count - 1),
    ]
    arrays = [left, rights[0], rights[-1]]
    if own:
        in_specs.append(
            pl.BlockSpec((1, groups * rows, block), lambda p, j, flags: (slot(p, flags), 0, j))
        )
        arrays.append(received)
    many = 2 if side_first else 1
    results = pl.pallas_call(
        functools.partial(product_body, own, side_first),
        grid_spec=pltpu.PrefetchScalarGridSpec(
            num_scalar_prefetch=1,
            grid=(count, last + 1),
            in_specs=in_specs,
            out_specs=[result] * many,
        ),
        out_shape=[kept] * many,
        compiler_params=pltpu.CompilerParams(vmem_limit_bytes=56 * 1024 * 1024),
        cost_estimate=pl.CostEstimate(
            flops=2 * groups * rows * tokens * cols * count, transcendentals=0, bytes_accessed=10**7
        ),
        name="product",
    )(flags, *arrays)
    return results if side_first else results[0]


def token_info(seg):
    sequences, length = seg.shape
    lanes = []
    for j in range(1, 4):
        lanes.append(jnp.pad(seg[:, j:] == seg[:, :-j], ((0, 0), (j, 0))))
    ends = seg.reshape(sequences, length // TILE, TILE)
    before = jnp.pad(ends[:, :-1, -1], ((0, 0), (1, 0)), constant_values=-1)
    lanes.append((ends == before[:, :, None]).reshape(sequences, length))
    lanes.append(seg)
    for j in range(1, 4):
        lanes.append(jnp.pad(seg[:, j:] == seg[:, :-j], ((0, 0), (0, j))))
    table = jnp.stack([item.astype(jnp.float32).reshape(-1) for item in lanes], axis=1)
    return jnp.pad(table, ((0, 0), (0, TILE - table.shape[1])))


def gather_all(local):
    rows = lax.all_gather(local, (TP, DP), axis=0, tiled=True)
    shares = lax.axis_size(TP)
    return rows.reshape(shares, rows.shape[0] // shares, rows.shape[1])


def scatter_all(parts):
    shares, rows, cols = parts.shape
    return lax.psum_scatter(
        parts.reshape(shares * rows, cols), (TP, DP), scatter_dimension=0, tiled=True
    ).astype(jnp.float32)


def exchange(array, axis, bit):
    size = lax.axis_size(axis)
    return lax.ppermute(array, axis, [(i, i ^ bit) for i in range(size)])


def shift(array, step):
    size = lax.axis_size(DP)
    return lax.ppermute(array, DP, [(i, (i + step) % size) for i in range(size)])


def pick(array, index, axis):
    return lax.dynamic_index_in_dim(array, index, axis, keepdims=False)


def add_low(left, right):
    return (left.astype(jnp.float32) + right.astype(jnp.float32)).astype(jnp.bfloat16)


def after(value, *earlier):
    return lax.optimization_barrier((value, earlier))[0]


class Scatter:
    def __init__(self, flags, turned, rights, stages, relative=False):
        self.relative, self.stages = relative, list(stages)
        self.size = lax.axis_size(DP)
        self.flags, self.rights = flags, rights
        self.left = turned.reshape(self.size // 2, 2, -1, turned.shape[1])
        self.rows = self.left.shape[2]
        self.sent = [product(flags, self.left, rights, relative=relative)]

    joined = None

    def routes(self):
        flat = [item.reshape(-1, item.shape[-1]) for item in self.sent]
        stage = self.stages[0]
        return [
            ((stage, step if stage == PLACE else 0, item.shape[0]), item)
            for step, item in enumerate(flat)
        ]

    def take(self, moved):
        stage = self.stages.pop(0)
        if stage == PLACE:
            self.total = self.kept.astype(jnp.float32)
            for item in moved:
                self.total = self.total + item.astype(jnp.float32)
            return
        if stage == CORE:
            side_first = self.stages[0] == SIDE
            held = product(
                self.flags, self.left, self.rights, moved[0], side_first, self.relative
            )
            if side_first:
                self.kept, self.sent = [list(item) for item in held]
            else:
                self.kept, self.sent = [held[0]], [held[1]]
            return
        held = [add_low(kept, item) for kept, item in zip(self.kept, moved)]
        if not self.stages:
            self.held = held[0]
            return
        if self.joined is not None:
            held = [add_low(held[0], self.joined)]
        stage = self.stages[0]
        if stage == TENSOR:
            self.kept, self.sent = held[:1], held[1:]
        elif stage == SIDE:
            held = held[0].reshape(self.size // 4, 2, self.rows, -1)
            self.kept, self.sent = [
                [pick(held, index, 1).reshape(-1, held.shape[-1])]
                for index in (self.flags[2], 1 - self.flags[2])
            ]
        else:
            count = self.size // 4
            held = held[0].reshape(count, self.rows, -1)
            self.sent = [
                pick(held, (self.flags[3] + step) % count, 0) for step in range(1, count)
            ]
            self.kept = pick(held, self.flags[3], 0)


def send(route, array):
    stage, step, _ = route
    if stage == PLACE:
        return shift(array, 4 * (step + 1))
    if stage == TENSOR:
        return exchange(array, TP, 1)
    return exchange(array, DP, stage)


class Transfer:
    def __init__(self, *items):
        self.items, self.routes = items, {}
        for index, item in enumerate(items):
            for slot, (route, array) in enumerate(item.routes()):
                key = route + ((index, slot) if route[0] == CORE else ())
                self.routes.setdefault(key, []).append((index, slot, array))
        self.packed = [
            jnp.concatenate([entry[2] for entry in entries], axis=1)
            for entries in self.routes.values()
        ]

    def send(self):
        return [send(key[:3], array) for key, array in zip(self.routes, self.packed)]

    def land(self):
        self.accept(lax.optimization_barrier(self.send()))

    def accept(self, moved):
        got = [[None] * len(item.sent) for item in self.items]
        for entries, array in zip(self.routes.values(), moved):
            pieces = columns(array, [entry[2].shape[1] for entry in entries])
            for (index, slot, _), piece in zip(entries, pieces):
                got[index][slot] = piece
        for item, mine in zip(self.items, got):
            item.take([piece.reshape(sent.shape) for piece, sent in zip(mine, item.sent)])


class Shared:
    def __init__(self, flat, stages):
        self.flat, self.stages = flat.reshape(1, -1), list(stages)

    @property
    def sent(self):
        return [self.flat]

    def routes(self):
        return [((self.stages[0], 0, 1), self.flat)]

    def take(self, moved):
        self.stages.pop(0)
        self.flat = self.flat + moved[0]


def columns(array, sizes):
    pieces, start = [], 0
    for size in sizes:
        pieces.append(array[..., start : start + size])
        start += size
    return pieces


def on_device_whole(
    layer_input,
    target,
    segment,
    pad_mask,
    norm1_gain,
    w_query,
    w_key,
    w_value,
    w_gate_out,
    w_decay,
    w_beta,
    conv_query,
    conv_key,
    conv_value,
    decay_scale,
    decay_bias,
    out_norm_gain,
    w_out,
    norm2_gain,
    w_ffn_gate,
    w_ffn_up,
    w_ffn_down,
):
    own_rows, width = layer_input.shape
    shares = lax.axis_size(TP)
    sequences = own_rows // LENGTH
    tensor_index = lax.axis_index(TP)
    low = jnp.bfloat16
    proj_local = (w_query, w_key, w_value, w_gate_out, w_decay, w_beta)
    proj_sizes = [item.shape[1] for item in proj_local]
    used = sum(proj_sizes)
    padded = -(-used // 128) * 128
    proj_all = gather_all(
        jnp.concatenate(proj_local + (jnp.zeros((w_query.shape[0], padded - used), low),), axis=1)
    )
    rest_local = (w_ffn_gate, w_ffn_up, w_ffn_down, w_out)
    rest_sizes = [item.shape[1] for item in rest_local]
    rest_all = gather_all(jnp.concatenate(rest_local, axis=1))
    out_all = columns(rest_all, rest_sizes)[3]
    live = pad_mask.astype(jnp.float32)
    count = lax.psum(jnp.sum(live), (DP, TP))
    input_float = layer_input.astype(jnp.float32)
    normed = rms_scale(input_float, norm1_gain).astype(low)
    seg_rows = lax.dynamic_slice_in_dim(segment, tensor_index * own_rows, own_rows, 0).reshape(
        sequences, LENGTH
    )
    parts = (1 - tensor_index, tensor_index)
    proj = [
        jnp.dot(normed, pick(proj_all, part, 0), preferred_element_type=jnp.float32)[None]
        for part in parts
    ]
    heads = w_decay.shape[1]
    info = token_info(seg_rows)

    def by_part(item):
        return item.reshape(item.shape[0], shares, item.shape[1] // shares).transpose(1, 0, 2)

    conv = jnp.pad(
        jnp.concatenate([by_part(c) for c in (conv_query, conv_key, conv_value)], axis=2),
        ((0, 0), (0, 4), (0, 0)),
    )
    rates = jnp.pad(
        by_part(jnp.stack([decay_scale, decay_bias])), ((0, 0), (0, 6), (0, TILE - heads))
    )
    gain = out_norm_gain.reshape(1, -1)
    value_cols = w_value.shape[1]
    mixer_args = [
        (item, info, pick(conv, part, 0)[None], pick(rates, part, 0)[None], gain)
        for item, part in zip(proj, parts)
    ]
    out_parts = [pick(out_all, part, 0) for part in parts]
    saved, mixed, residual = [], [], input_float
    for arguments in mixer_args:
        mixed_low, *kept = mixer_forward(*arguments, heads)
        mixed.append(mixed_low)
        saved.append(kept)
    for item, weight in zip(mixed, out_parts):
        residual = residual + contract_cols(item, weight)
    normed2 = rms_scale(residual, norm2_gain).astype(low)
    units = w_ffn_gate.shape[1]
    all_tokens = own_rows * lax.axis_size(DP) * lax.axis_size(TP)
    level = jnp.full((8, TILE), all_tokens / count, jnp.float32)
    live_lanes = jnp.broadcast_to(live[:, None], (own_rows, TILE))
    mine = lax.axis_index(DP)
    flags = jnp.stack([mine % 2, tensor_index, (mine // 2) % 2, mine // 4]).astype(jnp.int32)
    weights = [rest_all] * 3
    gate_pre, up_pre, hidden, output, grad_ffn, grad_ffn_turned, loss_rows = dense_call(
        dense_forward_body,
        flags,
        [normed2, *weights, residual, target, live_lanes, level],
        lambda s: (
            [s.row, *s.weights, s.late, s.late, s.lane, s.level],
            [s.unit, s.unit, s.unit, s.late, s.late_low, s.turned, s.sums],
        ),
        width,
        units,
    )
    loss_sum = jnp.sum(loss_rows)
    down = Scatter(flags, grad_ffn_turned, [hidden, hidden], SIDE_FIRST)
    cores = Transfer(down)
    grad_gates, grad_ups, grad_residual, grad_attention, back_turned, gain_two_rows = dense_call(
        dense_backward_body,
        flags,
        [
            after(grad_ffn, cores.packed), *weights, gate_pre, up_pre,
            residual, output, target, live_lanes, level, norm2_gain.reshape(1, -1),
        ],
        lambda s: (
            [s.row, *s.weights, s.unit, s.unit, s.late, s.late, s.late, s.lane, s.level, s.gain],
            [s.unit, s.unit, s.late, s.late_low, s.turned, s.sums],
        ),
        width,
        units,
    )
    grad_gain_two = gain_two_rows[0]
    turned2 = normed2.T
    gate = Scatter(flags, turned2, [grad_gates, grad_gates], TENSOR_FIRST)
    up = Scatter(flags, turned2, [grad_ups, grad_ups], SIDE_FIRST)
    cores.land()
    first_down = Transfer(down)
    gate.sent = after(gate.sent, first_down.packed)
    cores = Transfer(gate, up)
    out = Scatter(flags, back_turned, mixed, SIDE_FIRST, True)
    out_cores = Transfer(out)
    later = after(grad_attention, out_cores.packed, cores.packed)
    grad_mixed = [
        jnp.dot(later, weight, preferred_element_type=jnp.float32) for weight in out_parts
    ]
    cores.land()
    out_cores.land()
    middle = Transfer(gate, up, out)
    ready = after(grad_mixed[0], middle.packed)
    per_part = [mixer_backward(*mixer_args[0], saved[0], ready, heads)]
    turned = normed.T
    theirs = Scatter(flags, turned, [per_part[0][0]], (CORE, SIDE))
    theirs_cores = Transfer(theirs)
    middle.land()
    first_down.land()
    middle = Transfer(gate, up, out, down)
    theirs.left = after(theirs.left, middle.packed)
    theirs_cores.land()
    theirs_side = Transfer(theirs)
    ready = after(grad_mixed[1], middle.packed, theirs_side.packed)
    per_part.append(mixer_backward(*mixer_args[1], saved[1], ready, heads))
    grad_conv, grad_rates, grad_gain = [
        jnp.roll(
            jnp.concatenate([item[i] for item in per_part], axis=0), tensor_index + 1, axis=0
        )
        for i in (1, 2, 3)
    ]

    def from_part(item):
        return item.transpose(1, 0, 2).reshape(item.shape[1], -1)

    query_cols = w_query.shape[1]
    small = [
        from_part(item)
        for item in columns(grad_conv[:, :4], (query_cols, query_cols, value_cols))
    ] + [
        grad_rates[:, 0, :heads].reshape(-1),
        grad_rates[:, 1, :heads].reshape(-1),
        jnp.sum(grad_gain[:, 0], axis=0),
        grad_gain_two,
        loss_sum,
    ]
    grad_proj = [item[0] for item in per_part]
    ours = Scatter(flags, turned, [grad_proj[1]], (CORE, SIDE, PLACE))
    ours_cores = Transfer(ours)
    theirs.sent = after(theirs.sent, ours_cores.packed)
    middle.land()
    theirs_side.land()
    middle = Transfer(gate, up, out, down)
    ours.left = after(ours.left, middle.packed, theirs.held)
    ours_cores.land()
    ending = Transfer(ours)
    grad_proj = after(grad_proj, ending.packed)
    grad_input, gain_one_rows = dense_call(
        input_backward_body,
        flags,
        [*grad_proj, proj_all, layer_input, grad_residual, norm1_gain.reshape(1, -1)],
        lambda s: ([s.first, s.second, s.own, s.late, s.late, s.gain], [s.late, s.sums]),
        width,
        padded,
    )
    joined = exchange(theirs.held, TP, 1)
    joined, gain_one_rows, *moved = lax.optimization_barrier(
        [joined, gain_one_rows] + middle.send() + ending.send()
    )
    ours.joined = joined
    middle.accept(moved[: len(middle.packed)])
    ending.accept(moved[len(middle.packed) :])
    size, places = lax.axis_size(DP), []
    while 4 << len(places) < size:
        places.append(4 << len(places))
    small.append(gain_one_rows[0])
    flat = jnp.concatenate([item.reshape(-1) for item in small])
    flat = jnp.pad(flat, (0, -flat.shape[0] % 1024))
    shared = Shared(flat, places + [CORE, SIDE, TENSOR])
    for _ in places:
        Transfer(shared).land()
    ours.sent = after(ours.sent, shared.flat)
    ending = Transfer(ours)
    shared.flat = after(shared.flat, ending.packed)
    while shared.stages:
        Transfer(shared).land()
    ending.land()
    own_gate, own_up, own_out, own_down = [item.total for item in (gate, up, out, down)]
    own_proj = columns(ours.total, proj_sizes)
    summed, start = [], 0
    for item in small:
        summed.append(shared.flat[0, start : start + item.size].reshape(item.shape))
        start += item.size
    loss = summed[7] / (count * width)
    return (
        output,
        loss,
        grad_input,
        summed[8],
        *own_proj,
        *summed[:6],
        own_out,
        summed[6],
        own_gate,
        own_up,
        own_down,
    )


def on_device(layer_input, *others):
    size = lax.axis_size(DP)
    whole = layer_input.shape[0] % LENGTH == 0 and lax.axis_size(TP) == 2
    whole = whole and size >= 4 and size & (size - 1) == 0
    return (on_device_whole if whole else on_device_split)(layer_input, *others)


def solution(mesh):
    return jax.shard_map(
        on_device,
        mesh=mesh,
        in_specs=(
            P((DP, TP), None),
            P((DP, TP), None),
            P(DP),
            P((DP, TP)),
            P(),
            P(DP, TP),
            P(DP, TP),
            P(DP, TP),
            P(DP, TP),
            P(DP, TP),
            P(DP, TP),
            P(),
            P(),
            P(),
            P(),
            P(),
            P(),
            P(DP, TP),
            P(),
            P(DP, TP),
            P(DP, TP),
            P(DP, TP),
        ),
        out_specs=(
            P((DP, TP), None),
            P(),
            P((DP, TP), None),
            P(),
            P(DP, TP),
            P(DP, TP),
            P(DP, TP),
            P(DP, TP),
            P(DP, TP),
            P(DP, TP),
            P(),
            P(),
            P(),
            P(),
            P(),
            P(),
            P(DP, TP),
            P(),
            P(DP, TP),
            P(DP, TP),
            P(DP, TP),
        ),
        check_vma=False,
    )
```

```python
import functools
from types import SimpleNamespace

import jax
import jax.numpy as jnp
from jax import lax
from jax.experimental import pallas as pl
from jax.experimental.pallas import tpu as pltpu
from jax.sharding import PartitionSpec as P

CH = 64
LENGTH = 1024


DP, TP = "dp", "tensor"
exact_precision = lax.Precision.HIGHEST


def rms_scale(values, gain):
    return values * lax.rsqrt(jnp.mean(values * values, axis=-1, keepdims=True) + 1e-06) * gain


def shift_masks(segment_ids, taps):
    masks = [jnp.ones(segment_ids.shape, jnp.float32)]
    for offset in range(1, taps):
        earlier = jnp.concatenate([jnp.full((offset,), -1, jnp.int32), segment_ids[:-offset]])
        masks.append((segment_ids == earlier).astype(jnp.float32))
    return masks


def short_conv(values, kernel, masks):
    result = values * kernel[0]
    for offset in range(1, len(masks)):
        shifted = jnp.concatenate(
            [jnp.zeros((offset, values.shape[1]), jnp.float32), values[:-offset]]
        )
        result = result + shifted * masks[offset][:, None] * kernel[offset]
    return result


def unit_rows(values):
    return values * lax.rsqrt(jnp.sum(values * values, axis=-1, keepdims=True) + 1e-06)


def lower_inverse(lower_part, length):
    negative = -lower_part
    inverse = jnp.eye(length, dtype=jnp.float32) + negative
    power = negative
    covered = 2
    while covered < length:
        power = jnp.einsum("hij,hjk->hik", power, power, precision=exact_precision)
        inverse = inverse + jnp.einsum("hij,hjk->hik", inverse, power, precision=exact_precision)
        covered = covered * 2
    return inverse


def block_update(state, inputs):
    queries, keys, values, betas, log_decay, seg_block, previous = inputs
    length = queries.shape[0]
    cumulative = jnp.cumsum(log_decay, axis=0)
    order = jnp.arange(length)
    causal = order[:, None] >= order[None, :]
    strict = order[:, None] > order[None, :]
    same_doc = seg_block[:, None] == seg_block[None, :]
    visible = (same_doc & causal)[:, :, None]
    spread = cumulative[:, None, :] - cumulative[None, :, :]
    weights = jnp.where(visible, jnp.exp(jnp.where(visible, spread, 0.0)), 0.0)
    carried = (seg_block == previous).astype(jnp.float32)
    carry_decay = jnp.exp(cumulative) * carried[:, None]
    key_gram = jnp.einsum("ihd,jhd->ijh", keys, keys, precision=exact_precision)
    lower_part = jnp.where(strict[:, :, None], betas[:, None, :] * weights * key_gram, 0.0)
    inverse = lower_inverse(jnp.transpose(lower_part, (2, 0, 1)), length)
    key_state = jnp.einsum("ihd,hde->ihe", keys, state, precision=exact_precision)
    target_rows = betas[:, :, None] * (values - carry_decay[:, :, None] * key_state)
    pseudo = jnp.einsum("hij,jhe->hie", inverse, target_rows, precision=exact_precision)
    scores = jnp.einsum("ihd,jhd->hij", queries, keys, precision=exact_precision) * jnp.transpose(
        weights, (2, 0, 1)
    )
    query_state = jnp.einsum("ihd,hde->ihe", queries, state, precision=exact_precision)
    outputs = carry_decay[:, :, None] * query_state + jnp.einsum(
        "hij,hje->ihe", scores, pseudo, precision=exact_precision
    )
    last_weights = weights[-1]
    new_state = (carried[-1] * jnp.exp(cumulative[-1]))[:, None, None] * state + jnp.einsum(
        "jh,jhd,hje->hde", last_weights, keys, pseudo, precision=exact_precision
    )
    return (new_state, outputs)


def mixer_sequence(
    q_pre,
    k_pre,
    v_pre,
    g_pre,
    a_pre,
    b_pre,
    segment_ids,
    conv_q,
    conv_k,
    conv_v,
    scale_rate,
    bias_rate,
    out_gain,
):
    length = q_pre.shape[0]
    heads = a_pre.shape[1]
    key_size = q_pre.shape[1] // heads
    value_size = v_pre.shape[1] // heads
    masks = shift_masks(segment_ids, conv_q.shape[0])
    queries = unit_rows(
        jax.nn.silu(short_conv(q_pre, conv_q, masks)).reshape(length, heads, key_size)
    ) * key_size ** (-0.5)
    keys = unit_rows(jax.nn.silu(short_conv(k_pre, conv_k, masks)).reshape(length, heads, key_size))
    values = jax.nn.silu(short_conv(v_pre, conv_v, masks)).reshape(length, heads, value_size)
    betas = jax.nn.sigmoid(b_pre)
    log_decay = -scale_rate * jax.nn.softplus(a_pre + bias_rate)
    blocks = length // CH
    seg_blocks = segment_ids.reshape(blocks, CH)
    previous = jnp.concatenate([jnp.full((1,), -1, jnp.int32), seg_blocks[:-1, -1]])
    state = jnp.zeros((heads, key_size, value_size), jnp.float32)
    carried_in = (
        queries.reshape(blocks, CH, heads, key_size),
        keys.reshape(blocks, CH, heads, key_size),
        values.reshape(blocks, CH, heads, value_size),
        betas.reshape(blocks, CH, heads),
        log_decay.reshape(blocks, CH, heads),
        seg_blocks,
        previous,
    )
    final_state, outputs = lax.scan(jax.checkpoint(block_update), state, carried_in)
    outputs = outputs.reshape(length, heads, value_size)
    gated = rms_scale(outputs, out_gain) * jax.nn.silu(g_pre.reshape(length, heads, value_size))
    return gated.reshape(length, heads * value_size)


def contract_rows(left, right):
    return lax.dot_general(
        left, right, (((0,), (0,)), ((), ())), preferred_element_type=jnp.float32
    )


def contract_cols(left, right):
    return lax.dot_general(
        left, right, (((1,), (1,)), ((), ())), preferred_element_type=jnp.float32
    )


def feed_inputs(normed_rows, gate_weight, up_weight):
    gate_pre = jnp.dot(normed_rows, gate_weight, preferred_element_type=jnp.float32)
    up_pre = jnp.dot(normed_rows, up_weight, preferred_element_type=jnp.float32)
    return (gate_pre, up_pre)


def on_device_split(
    layer_input,
    target,
    segment,
    pad_mask,
    norm1_gain,
    w_query,
    w_key,
    w_value,
    w_gate_out,
    w_decay,
    w_beta,
    conv_query,
    conv_key,
    conv_value,
    decay_scale,
    decay_bias,
    out_norm_gain,
    w_out,
    norm2_gain,
    w_ffn_gate,
    w_ffn_up,
    w_ffn_down,
):
    own_rows, width = layer_input.shape
    group_rows = segment.shape[0]
    sequences = group_rows // LENGTH
    tensor_index = lax.axis_index(TP)
    heads_local = w_decay.shape[1]
    query_cols = w_query.shape[1]
    value_cols = w_value.shape[1]
    input_float = layer_input.astype(jnp.float32)
    normed_own, norm1_pull = jax.vjp(rms_scale, input_float, norm1_gain)
    normed = lax.all_gather(normed_own.astype(jnp.bfloat16), TP, axis=0, tiled=True)
    full_query, full_key, full_value, full_gate, full_decay, full_beta, full_out = (
        lax.all_gather(w_query, DP, axis=0, tiled=True),
        lax.all_gather(w_key, DP, axis=0, tiled=True),
        lax.all_gather(w_value, DP, axis=0, tiled=True),
        lax.all_gather(w_gate_out, DP, axis=0, tiled=True),
        lax.all_gather(w_decay, DP, axis=0, tiled=True),
        lax.all_gather(w_beta, DP, axis=0, tiled=True),
        lax.all_gather(w_out, DP, axis=0, tiled=True),
    )
    proj_weights = (full_query, full_key, full_value, full_gate, full_decay, full_beta)
    projected = [
        jnp.dot(normed, weight, preferred_element_type=jnp.float32) for weight in proj_weights
    ]
    conv_q_local = lax.dynamic_slice_in_dim(conv_query, tensor_index * query_cols, query_cols, 1)
    conv_k_local = lax.dynamic_slice_in_dim(conv_key, tensor_index * query_cols, query_cols, 1)
    conv_v_local = lax.dynamic_slice_in_dim(conv_value, tensor_index * value_cols, value_cols, 1)
    scale_local = lax.dynamic_slice_in_dim(decay_scale, tensor_index * heads_local, heads_local, 0)
    bias_local = lax.dynamic_slice_in_dim(decay_bias, tensor_index * heads_local, heads_local, 0)
    seg_rows = segment.reshape(sequences, LENGTH)

    def mixer_local(
        q_pre,
        k_pre,
        v_pre,
        g_pre,
        a_pre,
        b_pre,
        conv_q,
        conv_k,
        conv_v,
        scale_rate,
        bias_rate,
        out_gain,
    ):
        shaped = [
            item.reshape(sequences, LENGTH, item.shape[1])
            for item in (q_pre, k_pre, v_pre, g_pre, a_pre, b_pre)
        ]
        mixed_rows = jax.vmap(
            mixer_sequence, in_axes=(0, 0, 0, 0, 0, 0, 0, None, None, None, None, None, None)
        )(*shaped, seg_rows, conv_q, conv_k, conv_v, scale_rate, bias_rate, out_gain)
        return mixed_rows.reshape(group_rows, mixed_rows.shape[2])

    mixed, mixer_pull = jax.vjp(
        mixer_local,
        *projected,
        conv_q_local,
        conv_k_local,
        conv_v_local,
        scale_local,
        bias_local,
        out_norm_gain
    )
    mixed_low = mixed.astype(jnp.bfloat16)
    attention = lax.psum_scatter(
        contract_cols(mixed_low, full_out), TP, scatter_dimension=0, tiled=True
    )
    residual = input_float + attention
    normed2_own, norm2_pull = jax.vjp(rms_scale, residual, norm2_gain)
    normed2 = lax.all_gather(normed2_own.astype(jnp.bfloat16), TP, axis=0, tiled=True)
    ffn_gate_w, ffn_up_w, ffn_down_w = (
        lax.all_gather(w_ffn_gate, DP, axis=0, tiled=True),
        lax.all_gather(w_ffn_up, DP, axis=0, tiled=True),
        lax.all_gather(w_ffn_down, DP, axis=0, tiled=True),
    )
    gate_pre, up_pre = feed_inputs(normed2, ffn_gate_w, ffn_up_w)
    hidden = (jax.nn.silu(gate_pre) * up_pre).astype(jnp.bfloat16)
    ffn_out = lax.psum_scatter(
        contract_cols(hidden, ffn_down_w).astype(jnp.bfloat16),
        TP,
        scatter_dimension=0,
        tiled=True,
    ).astype(jnp.float32)
    output = residual + ffn_out
    live = pad_mask.astype(jnp.float32)
    error = output - target.astype(jnp.float32)
    loss_sum, count = lax.psum(
        (jnp.sum(live[:, None] * error * error), jnp.sum(live)), (DP, TP)
    )
    loss = loss_sum / (count * width)
    all_tokens = own_rows * lax.axis_size(DP) * lax.axis_size(TP)
    grad_output = error * live[:, None] * (all_tokens / count)
    grad_ffn = lax.all_gather(grad_output.astype(jnp.bfloat16), TP, axis=0, tiled=True)
    grad_hidden = jnp.dot(grad_ffn, ffn_down_w, preferred_element_type=jnp.float32)
    sigmoid_gate = jax.nn.sigmoid(gate_pre)
    grad_gate = (
        grad_hidden * up_pre * sigmoid_gate * (1.0 + gate_pre * (1.0 - sigmoid_gate))
    ).astype(jnp.bfloat16)
    grad_up = (grad_hidden * gate_pre * sigmoid_gate).astype(jnp.bfloat16)
    grad_down_local = contract_rows(grad_ffn, hidden)
    grad_gate_local = contract_rows(normed2, grad_gate)
    grad_up_local = contract_rows(normed2, grad_up)
    normed2_part = contract_cols(grad_gate, ffn_gate_w) + contract_cols(grad_up, ffn_up_w)
    grad_normed2 = lax.psum_scatter(
        normed2_part.astype(jnp.bfloat16), TP, scatter_dimension=0, tiled=True
    ).astype(jnp.float32)
    grad_residual_norm, grad_gain_two = norm2_pull(grad_normed2)
    grad_residual = grad_output + grad_residual_norm
    grad_attention = lax.all_gather(
        grad_residual.astype(jnp.bfloat16), TP, axis=0, tiled=True
    )
    grad_mixed = jnp.dot(grad_attention, full_out, preferred_element_type=jnp.float32)
    grad_out_local = contract_rows(grad_attention, mixed_low)
    mixer_grads = mixer_pull(grad_mixed)
    pre_grads = [item.astype(jnp.bfloat16) for item in mixer_grads[:6]]
    normed_part = contract_cols(pre_grads[0], full_query)
    for grad_item, weight in zip(pre_grads[1:], proj_weights[1:]):
        normed_part = normed_part + contract_cols(grad_item, weight)
    weight_locals = [contract_rows(normed, grad_item) for grad_item in pre_grads]
    grad_normed = lax.psum_scatter(
        normed_part.astype(jnp.bfloat16), TP, scatter_dimension=0, tiled=True
    ).astype(jnp.float32)
    grad_input_norm, grad_gain_one = norm1_pull(grad_normed)
    grad_input = grad_residual + grad_input_norm
    owned = (
        lax.psum_scatter(
            grad_gate_local.astype(jnp.bfloat16), DP, scatter_dimension=0, tiled=True
        ).astype(jnp.float32),
        lax.psum_scatter(
            grad_up_local.astype(jnp.bfloat16), DP, scatter_dimension=0, tiled=True
        ).astype(jnp.float32),
        lax.psum_scatter(
            grad_down_local.astype(jnp.bfloat16), DP, scatter_dimension=0, tiled=True
        ).astype(jnp.float32),
        lax.psum_scatter(
            weight_locals[0].astype(jnp.bfloat16), DP, scatter_dimension=0, tiled=True
        ).astype(jnp.float32),
        lax.psum_scatter(
            weight_locals[1].astype(jnp.bfloat16), DP, scatter_dimension=0, tiled=True
        ).astype(jnp.float32),
        lax.psum_scatter(
            weight_locals[2].astype(jnp.bfloat16), DP, scatter_dimension=0, tiled=True
        ).astype(jnp.float32),
        lax.psum_scatter(
            weight_locals[3].astype(jnp.bfloat16), DP, scatter_dimension=0, tiled=True
        ).astype(jnp.float32),
        lax.psum_scatter(
            weight_locals[4].astype(jnp.bfloat16), DP, scatter_dimension=0, tiled=True
        ).astype(jnp.float32),
        lax.psum_scatter(
            weight_locals[5].astype(jnp.bfloat16), DP, scatter_dimension=0, tiled=True
        ).astype(jnp.float32),
        lax.psum_scatter(
            grad_out_local.astype(jnp.bfloat16), DP, scatter_dimension=0, tiled=True
        ).astype(jnp.float32),
    )
    conv_q_full = lax.dynamic_update_slice_in_dim(
        jnp.zeros_like(conv_query), mixer_grads[6], tensor_index * query_cols, 1
    )
    conv_k_full = lax.dynamic_update_slice_in_dim(
        jnp.zeros_like(conv_key), mixer_grads[7], tensor_index * query_cols, 1
    )
    conv_v_full = lax.dynamic_update_slice_in_dim(
        jnp.zeros_like(conv_value), mixer_grads[8], tensor_index * value_cols, 1
    )
    scale_full = lax.dynamic_update_slice_in_dim(
        jnp.zeros_like(decay_scale), mixer_grads[9], tensor_index * heads_local, 0
    )
    bias_full = lax.dynamic_update_slice_in_dim(
        jnp.zeros_like(decay_bias), mixer_grads[10], tensor_index * heads_local, 0
    )
    summed = lax.psum(
        (
            grad_gain_one,
            grad_gain_two,
            conv_q_full,
            conv_k_full,
            conv_v_full,
            scale_full,
            bias_full,
            mixer_grads[11],
        ),
        (DP, TP),
    )
    return (
        output,
        loss,
        grad_input,
        summed[0],
        owned[3],
        owned[4],
        owned[5],
        owned[6],
        owned[7],
        owned[8],
        summed[2],
        summed[3],
        summed[4],
        summed[5],
        summed[6],
        summed[7],
        owned[9],
        summed[1],
        owned[0],
        owned[1],
        owned[2],
    )


CORE, SIDE, TENSOR, PLACE = 1, 2, 3, 0
TENSOR_FIRST = (CORE, TENSOR, SIDE, PLACE)
SIDE_FIRST = (CORE, SIDE, TENSOR, PLACE)
TILE = 128
DONE = object()
COST = 4 * 10**10


def mm(left, right, dims=((1,), (0,))):
    return lax.dot_general(
        left.astype(jnp.bfloat16),
        right.astype(jnp.bfloat16),
        (dims, ((), ())),
        preferred_element_type=jnp.float32,
    )


def mm_nt(left, right):
    return mm(left, right, ((1,), (1,)))


def mm_tn(left, right):
    return mm(left, right, ((0,), (0,)))


def mm_fine(left, right):
    left_high, right_high = left.astype(jnp.bfloat16), right.astype(jnp.bfloat16)
    left_rest = left - left_high.astype(jnp.float32)
    right_rest = right - right_high.astype(jnp.float32)
    return mm(left_high, right_high) + (mm(left_high, right_rest) + mm(left_rest, right_high))


def ones_mm(ones, right):
    high = right.astype(jnp.bfloat16)
    rest = right - high.astype(jnp.float32)
    middle = rest.astype(jnp.bfloat16)
    return mm(ones, high) + (mm(ones, middle) + mm(ones, rest - middle.astype(jnp.float32)))


def unit_lower_inverses(parts, row, col):
    size = parts[0].shape[0]
    eye = (row == col).astype(jnp.float32)
    block = 16
    inside = (row // block) == (col // block)
    powers = [jnp.where(inside, -part, 0.0) for part in parts]
    inverses = [eye + power for power in powers]
    covered = 2
    while covered < block:
        powers = [mm_fine(power, power) for power in powers]
        moves = [mm_fine(inverse, power) for inverse, power in zip(inverses, powers)]
        inverses = [inverse + move for inverse, move in zip(inverses, moves)]
        covered *= 2
    while block < size:
        cross = ((row // (2 * block)) == (col // (2 * block))) & (
            (row // block) != (col // block)
        )
        lows = [inverse.astype(jnp.bfloat16) for inverse in inverses]
        moves = [mm(low, jnp.where(cross, part, 0.0)) for low, part in zip(lows, parts)]
        moves = [mm(move, low) for move, low in zip(moves, lows)]
        inverses = [inverse - move for inverse, move in zip(inverses, moves)]
        block *= 2
    return inverses


def stable_softplus(values):
    return jnp.maximum(values, 0.0) + jnp.log1p(jnp.exp(-jnp.abs(values)))


def decay_tiles(raw, rate, bias):
    shifted = raw + bias
    soft = stable_softplus(shifted)
    return shifted, soft, -rate * soft


def grids():
    row = lax.broadcasted_iota(jnp.int32, (TILE, TILE), 0)
    col = lax.broadcasted_iota(jnp.int32, (TILE, TILE), 1)
    return row, col


def forward_body(
    heads,
    proj_ref,
    info_ref,
    conv_ref,
    rates_ref,
    gain_ref,
    mixed_ref,
    conv_out_ref,
    rows_out_ref,
    state_out_ref,
    inverse_out_ref,
    pseudo_out_ref,
    earlier_ref,
    state_ref,
):
    first = pl.program_id(2) == 0
    blocks = 4 * heads

    @pl.when(first)
    def _():
        earlier_ref[:, 0:8, :] = jnp.zeros((blocks, 8, TILE), jnp.float32)
        state_ref[...] = jnp.zeros(state_ref.shape, jnp.float32)

    row, col = grids()
    info = info_ref[...]
    info_rows = info.T
    masks = [jnp.broadcast_to(info[:, j : j + 1], (TILE, TILE)) for j in range(3)]
    visible = (row >= col) & (info[:, 4:5] == info_rows[4:5, :])
    raw = proj_ref[0, :, 6 * heads * TILE : 6 * heads * TILE + TILE]
    _, _, log_decay = decay_tiles(raw, rates_ref[0, 0:1, :], rates_ref[0, 1:2, :])
    total = ones_mm((row >= col).astype(jnp.float32), log_decay)
    total_rows = total.T
    carry = jnp.exp(total) * info[:, 3:4]
    beta_tile = jax.nn.sigmoid(raw)
    for block in range(blocks):
        earlier_ref[block, 8 : 8 + TILE, :] = proj_ref[0, :, block * TILE : (block + 1) * TILE]

    def conv_block(block):
        lanes = slice(block * TILE, (block + 1) * TILE)
        result = earlier_ref[block, 8 : 8 + TILE, :] * conv_ref[0, 0:1, lanes]
        for j in range(1, 4):
            result = result + masks[j - 1] * (
                earlier_ref[block, 8 - j : 8 - j + TILE, :] * conv_ref[0, j : j + 1, lanes]
            )
        conv_out_ref[0, :, lanes] = result
        return result * jax.nn.sigmoid(result)

    every = range(heads)
    queries, keys, values, parts, scores = [], [], [], [], []
    for head in every:
        query, key = conv_block(head), conv_block(heads + head)
        query = query * (
            lax.rsqrt(jnp.sum(query * query, axis=1, keepdims=True) + 1e-06) * TILE ** (-0.5)
        )
        key = key * lax.rsqrt(jnp.sum(key * key, axis=1, keepdims=True) + 1e-06)
        spread = total[:, head : head + 1] - total_rows[head : head + 1, :]
        weights = jnp.exp(jnp.where(visible, spread, -1e30))
        key_low, query_low = key.astype(jnp.bfloat16), query.astype(jnp.bfloat16)
        grams = mm_nt(jnp.concatenate([key_low, query_low], axis=0), key_low)
        beta = beta_tile[:, heads + head : heads + head + 1]
        parts.append(jnp.where(row > col, beta * weights * grams[:TILE], 0.0))
        scores.append((grams[TILE:] * weights).astype(jnp.bfloat16))
        queries.append(query_low)
        keys.append((key_low, (key.T * weights[TILE - 1 : TILE, :]).astype(jnp.bfloat16)))
    for head in every:
        values.append(
            jnp.concatenate(
                [conv_block(2 * heads + 2 * head), conv_block(2 * heads + 2 * head + 1)], axis=1
            )
        )
    inverses = [item.astype(jnp.bfloat16) for item in unit_lower_inverses(parts, row, col)]
    states = [state_ref[head] for head in every]
    lows = [state.astype(jnp.bfloat16) for state in states]
    from_states = [
        mm(jnp.concatenate([keys[head][0], queries[head]], axis=0), lows[head]) for head in every
    ]
    carries = [carry[:, head : head + 1] for head in every]
    pseudos = [
        mm(
            inverses[head],
            beta_tile[:, heads + head : heads + head + 1]
            * (values[head] - carries[head] * from_states[head][:TILE]),
        ).astype(jnp.bfloat16)
        for head in every
    ]
    for head in every:
        lanes = slice(2 * head * TILE, 2 * (head + 1) * TILE)
        carried, pseudo = carries[head], pseudos[head]
        state_ref[head] = carried[TILE - 1 : TILE, :] * states[head] + mm(keys[head][1], pseudo)
        rows = carried * from_states[head][TILE:] + mm(scores[head], pseudo)
        state_out_ref[0, 0, head] = lows[head]
        inverse_out_ref[0, 0, head] = inverses[head]
        pseudo_out_ref[0, :, lanes] = pseudo
        rows_out_ref[0, :, lanes] = rows
        gate = proj_ref[
            0, :, (4 * heads + 2 * head) * TILE : (4 * heads + 2 * (head + 1)) * TILE
        ]
        scale = lax.rsqrt(jnp.mean(rows * rows, axis=1, keepdims=True) + 1e-06)
        mixed_ref[:, lanes] = (
            rows * scale * gain_ref[...] * (gate * jax.nn.sigmoid(gate))
        ).astype(jnp.bfloat16)
    for block in range(blocks):
        earlier_ref[block, 0:8, :] = earlier_ref[block, TILE : TILE + 8, :]


def backward_body(
    heads,
    proj_ref,
    info_ref,
    conv_ref,
    rates_ref,
    gain_ref,
    conv_out_ref,
    rows_ref,
    state_in_ref,
    inverse_ref,
    pseudo_ref,
    grad_ref,
    grad_proj_ref,
    grad_conv_ref,
    grad_rates_ref,
    grad_gain_ref,
    later_ref,
    grad_state_ref,
):
    step = pl.program_id(2)
    blocks = 4 * heads

    @pl.when(step == 0)
    def _():
        later_ref[:, TILE : TILE + 8, :] = jnp.zeros((blocks, 8, TILE), jnp.float32)
        grad_state_ref[...] = jnp.zeros(grad_state_ref.shape, jnp.float32)

    @pl.when((step == 0) & (pl.program_id(1) == 0))
    def _():
        grad_conv_ref[...] = jnp.zeros(grad_conv_ref.shape, jnp.float32)
        grad_rates_ref[...] = jnp.zeros(grad_rates_ref.shape, jnp.float32)
        grad_gain_ref[...] = jnp.zeros(grad_gain_ref.shape, jnp.float32)

    row, col = grids()
    info = info_ref[...]
    info_rows = info.T
    masks = [jnp.broadcast_to(info[:, 4 + j : 5 + j], (TILE, TILE)) for j in range(1, 4)]
    visible = (row >= col) & (info[:, 4:5] == info_rows[4:5, :])
    raw = proj_ref[0, :, 6 * heads * TILE : 6 * heads * TILE + TILE]
    rate = rates_ref[0, 0:1, :]
    shifted, soft, log_decay = decay_tiles(raw, rate, rates_ref[0, 1:2, :])
    total = ones_mm((row >= col).astype(jnp.float32), log_decay)
    total_rows = total.T
    carry = jnp.exp(total) * info[:, 3:4]
    beta_tile = jax.nn.sigmoid(raw)
    grad_total = jnp.zeros((TILE, TILE), jnp.float32)
    grad_beta = jnp.zeros((TILE, TILE), jnp.float32)
    gain = gain_ref[...]
    gain_sum = jnp.zeros((1, 2 * TILE), jnp.float32)

    def activation(block):
        value = conv_out_ref[0, :, block * TILE : (block + 1) * TILE]
        gate = jax.nn.sigmoid(value)
        return value * gate, gate * (1.0 + value * (1.0 - gate))

    def close_block(block, grad):
        later_ref[block, 0:TILE, :] = grad
        lanes = slice(block * TILE, (block + 1) * TILE)
        own = proj_ref[0, :, lanes]
        result = grad * conv_ref[0, 0:1, lanes]
        sums = [jnp.sum(grad * own, axis=0, keepdims=True)]
        for j in range(1, 4):
            moved = masks[j - 1] * later_ref[block, j : j + TILE, :]
            result = result + moved * conv_ref[0, j : j + 1, lanes]
            sums.append(jnp.sum(moved * own, axis=0, keepdims=True))
        grad_proj_ref[0, :, lanes] = result.astype(jnp.bfloat16)
        for j in range(4):
            grad_conv_ref[0, j : j + 1, lanes] += sums[j]

    def head_steps(head):
        lanes = slice(2 * head * TILE, 2 * (head + 1) * TILE)
        gate_lanes = slice((4 * heads + 2 * head) * TILE, (4 * heads + 2 * (head + 1)) * TILE)
        rows = rows_ref[0, :, lanes]
        gate = proj_ref[0, :, gate_lanes]
        grad = grad_ref[:, lanes]
        scale = lax.rsqrt(jnp.mean(rows * rows, axis=1, keepdims=True) + 1e-06)
        level = rows * scale
        sigmoid = jax.nn.sigmoid(gate)
        through = grad * (gate * sigmoid)
        gain_sums.append(jnp.sum(through * level, axis=0, keepdims=True))
        grad_proj_ref[0, :, gate_lanes] = (
            grad * level * gain * (sigmoid * (1.0 + gate * (1.0 - sigmoid)))
        ).astype(jnp.bfloat16)
        through = through * gain
        grad_rows = scale * (
            through - level * jnp.mean(through * level, axis=1, keepdims=True)
        )

        yield
        query_act, query_slope = activation(head)
        query_scale = lax.rsqrt(jnp.sum(query_act * query_act, axis=1, keepdims=True) + 1e-06)
        query_unit = query_act * query_scale
        query = query_unit * TILE ** (-0.5)
        key_act, key_slope = activation(heads + head)
        key_scale = lax.rsqrt(jnp.sum(key_act * key_act, axis=1, keepdims=True) + 1e-06)
        key = key_act * key_scale
        value_parts = [activation(2 * heads + 2 * head), activation(2 * heads + 2 * head + 1)]
        value = jnp.concatenate([value_parts[0][0], value_parts[1][0]], axis=1)

        yield
        spread = total[:, head : head + 1] - total_rows[head : head + 1, :]
        weights = jnp.exp(jnp.where(visible, spread, -1e30))
        beta = beta_tile[:, heads + head : heads + head + 1]
        carried = carry[:, head : head + 1]
        key_low, query_low = key.astype(jnp.bfloat16), query.astype(jnp.bfloat16)
        both = jnp.concatenate([key_low, query_low], axis=0)
        grams = mm_nt(both, key_low)
        yield
        state_low = state_in_ref[0, 0, head]
        inverse = inverse_ref[0, 0, head]
        pseudo = pseudo_ref[0, :, lanes]
        grad_state = grad_state_ref[head]
        grad_state_low = grad_state.astype(jnp.bfloat16)
        last_row = weights[TILE - 1 : TILE, :]
        last_col = jnp.sum(jnp.where(row == col, last_row, 0.0), axis=1, keepdims=True)
        grad_rows_low = grad_rows.astype(jnp.bfloat16)
        grad_pseudo = mm_tn(grams[TILE:] * weights, grad_rows_low) + mm(
            last_col * key, grad_state_low
        )
        yield
        solved = mm_tn(inverse, grad_pseudo)
        yield
        crossed = mm_nt(
            jnp.concatenate([grad_rows_low, solved.astype(jnp.bfloat16)], axis=0), pseudo
        )
        yield
        grad_scores = crossed[:TILE] * weights
        below = jnp.where(row > col, crossed[TILE:] * weights, 0.0)
        grad_gram = (-beta) * below
        grad_value = beta * solved
        from_state = mm(key_low, state_low)
        grad_beta_col = jnp.sum(
            solved * (value - carried * from_state), axis=1, keepdims=True
        ) - jnp.sum(below * grams[:TILE], axis=1, keepdims=True)
        yield
        out_part = (carried * grad_rows).astype(jnp.bfloat16)
        key_part = ((-carried) * grad_value).astype(jnp.bfloat16)
        stacked = jnp.concatenate([out_part, key_part], axis=0)
        to_inputs = mm_nt(stacked, state_low)
        yield
        scores_low, gram_low = grad_scores.astype(jnp.bfloat16), grad_gram.astype(jnp.bfloat16)
        grad_query = mm(scores_low, key_low) + to_inputs[:TILE]
        key_own = mm(gram_low, key_low) + to_inputs[TILE:]
        key_rest = mm_tn(
            jnp.concatenate([gram_low, scores_low], axis=0), both
        )
        key_state = last_col * mm_nt(pseudo, grad_state_low)
        grad_key = key_own + key_rest + key_state
        grad_state_ref[head] = carried[TILE - 1 : TILE, :] * grad_state + mm_tn(
            jnp.concatenate([query_low, key_low], axis=0), stacked
        )
        yield
        key_exact, query_exact = key_low.astype(jnp.float32), query_low.astype(jnp.float32)
        state_dot = jnp.sum(key_state * key_exact, axis=1, keepdims=True)
        tail = jnp.sum(state_dot, axis=0, keepdims=True) + carried[TILE - 1 : TILE, :] * jnp.sum(
            jnp.sum(grad_state * state_low.astype(jnp.float32), axis=1, keepdims=True),
            axis=0,
            keepdims=True,
        )
        grad_total_col = (
            jnp.sum(
                grad_query * query_exact + (key_own - key_rest) * key_exact, axis=1, keepdims=True
            )
            - state_dot
            + jnp.where(row[:, 0:1] == TILE - 1, tail, 0.0)
        )
        columns_of[head] = (grad_total_col, grad_beta_col)
        yield

        grad_query = grad_query * TILE ** (-0.5)
        close_block(
            head,
            query_scale
            * (
                grad_query
                - query_unit * jnp.sum(grad_query * query_unit, axis=1, keepdims=True)
            )
            * query_slope,
        )
        yield
        close_block(
            heads + head,
            key_scale
            * (grad_key - key * jnp.sum(grad_key * key, axis=1, keepdims=True))
            * key_slope,
        )
        yield
        close_block(2 * heads + 2 * head, grad_value[:, :TILE] * value_parts[0][1])
        close_block(2 * heads + 2 * head + 1, grad_value[:, TILE:] * value_parts[1][1])

    gain_sums, columns_of = [], {}
    waiting = [head_steps(head) for head in range(heads)]
    while waiting:
        waiting = [steps for steps in waiting if next(steps, DONE) is not DONE]
    for head in range(heads):
        grad_total = jnp.where(col == head, columns_of[head][0], grad_total)
        grad_beta = jnp.where(col == heads + head, columns_of[head][1], grad_beta)
        gain_sum = gain_sum + gain_sums[head]

    grad_log = ones_mm((row <= col).astype(jnp.float32), grad_total)
    grad_raw = -rate * grad_log * jax.nn.sigmoid(shifted)
    grad_rates_ref[0, 0:1, :] += -jnp.sum(grad_log * soft, axis=0, keepdims=True)
    grad_rates_ref[0, 1:2, :] += jnp.sum(grad_raw, axis=0, keepdims=True)
    grad_gain_ref[0, 0:1, :] += gain_sum
    grad_proj_ref[0, :, 6 * heads * TILE : 6 * heads * TILE + TILE] = jnp.where(
        col < heads, grad_raw, grad_beta * beta_tile * (1.0 - beta_tile)
    ).astype(jnp.bfloat16)
    for block in range(blocks):
        later_ref[block, TILE : TILE + 8, :] = later_ref[block, 0:8, :]


def mixer_specs(parts, rows, wide, heads, blocks, backward):
    conv_cols, value_cols = 4 * heads * TILE, 2 * heads * TILE

    def place(s, c):
        return s * blocks + ((blocks - 1 - c) if backward else c)

    return SimpleNamespace(
        proj=pl.BlockSpec((1, TILE, wide), lambda p, s, c: (p, place(s, c), 0)),
        info=pl.BlockSpec((TILE, TILE), lambda p, s, c: (place(s, c), 0)),
        conv=pl.BlockSpec((1, 8, conv_cols), lambda p, s, c: (p, 0, 0)),
        rates=pl.BlockSpec((1, 8, TILE), lambda p, s, c: (p, 0, 0)),
        gain=pl.BlockSpec((1, 2 * TILE), lambda p, s, c: (0, 0)),
        flat=pl.BlockSpec((TILE, value_cols), lambda p, s, c: (place(s, c), p)),
        conv_out=pl.BlockSpec((1, TILE, conv_cols), lambda p, s, c: (p, place(s, c), 0)),
        value=pl.BlockSpec((1, TILE, value_cols), lambda p, s, c: (p, place(s, c), 0)),
        state=pl.BlockSpec(
            (1, 1, heads, TILE, 2 * TILE), lambda p, s, c: (p, place(s, c), 0, 0, 0)
        ),
        inverse=pl.BlockSpec(
            (1, 1, heads, TILE, TILE), lambda p, s, c: (p, place(s, c), 0, 0, 0)
        ),
        gain_sum=pl.BlockSpec((1, 8, 2 * TILE), lambda p, s, c: (p, 0, 0)),
    )


def mixer_forward(proj, info, conv, rates, gain, heads):
    parts, rows, wide = proj.shape
    blocks = LENGTH // TILE
    spec = mixer_specs(parts, rows, wide, heads, blocks, False)
    conv_cols, value_cols = 4 * heads * TILE, 2 * heads * TILE
    low, full = jnp.bfloat16, jnp.float32
    return pl.pallas_call(
        functools.partial(forward_body, heads),
        grid=(parts, rows // LENGTH, blocks),
        in_specs=[spec.proj, spec.info, spec.conv, spec.rates, spec.gain],
        out_specs=[
            spec.flat, spec.conv_out, spec.value, spec.state, spec.inverse, spec.value
        ],
        out_shape=[
            jax.ShapeDtypeStruct((rows, parts * value_cols), low),
            jax.ShapeDtypeStruct((parts, rows, conv_cols), full),
            jax.ShapeDtypeStruct((parts, rows, value_cols), full),
            jax.ShapeDtypeStruct((parts, rows // TILE, heads, TILE, 2 * TILE), low),
            jax.ShapeDtypeStruct((parts, rows // TILE, heads, TILE, TILE), low),
            jax.ShapeDtypeStruct((parts, rows, value_cols), low),
        ],
        scratch_shapes=[
            pltpu.VMEM((4 * heads, TILE + 8, TILE), full),
            pltpu.VMEM((heads, TILE, 2 * TILE), full),
        ],
        compiler_params=pltpu.CompilerParams(
            vmem_limit_bytes=48 * 1024 * 1024,
        ),
        cost_estimate=pl.CostEstimate(flops=COST, transcendentals=0, bytes_accessed=10**8),
        name="mixer_forward",
    )(proj, info, conv, rates, gain)


def mixer_backward(proj, info, conv, rates, gain, saved, grad, heads):
    parts, rows, wide = proj.shape
    blocks = LENGTH // TILE
    spec = mixer_specs(parts, rows, wide, heads, blocks, True)
    conv_cols = 4 * heads * TILE
    low, full = jnp.bfloat16, jnp.float32
    return pl.pallas_call(
        functools.partial(backward_body, heads),
        grid=(parts, rows // LENGTH, blocks),
        in_specs=[
            spec.proj, spec.info, spec.conv, spec.rates, spec.gain,
            spec.conv_out, spec.value, spec.state, spec.inverse, spec.value, spec.flat,
        ],
        out_specs=[spec.proj, spec.conv, spec.rates, spec.gain_sum],
        out_shape=[
            jax.ShapeDtypeStruct((parts, rows, wide), low),
            jax.ShapeDtypeStruct((parts, 8, conv_cols), full),
            jax.ShapeDtypeStruct((parts, 8, TILE), full),
            jax.ShapeDtypeStruct((parts, 8, 2 * TILE), full),
        ],
        scratch_shapes=[
            pltpu.VMEM((4 * heads, TILE + 8, TILE), full),
            pltpu.VMEM((heads, TILE, 2 * TILE), full),
        ],
        compiler_params=pltpu.CompilerParams(
            vmem_limit_bytes=48 * 1024 * 1024,
        ),
        cost_estimate=pl.CostEstimate(flops=COST, transcendentals=0, bytes_accessed=10**8),
        name="mixer_backward",
    )(proj, info, conv, rates, gain, *saved, grad)


BLOCK = 256


def rms_backward(values, gain, grad):
    scale = lax.rsqrt(jnp.mean(values * values, axis=1, keepdims=True) + 1e-06)
    level = values * scale
    through = grad * gain
    back = scale * (through - level * jnp.mean(through * level, axis=1, keepdims=True))
    return back, jnp.sum(grad * level, axis=0, keepdims=True)


def dense_forward_body(
    normed_ref,
    gate_w_ref,
    up_w_ref,
    down_w_ref,
    residual_ref,
    target_ref,
    live_ref,
    level_ref,
    gate_ref,
    up_ref,
    hidden_ref,
    output_ref,
    grad_ref,
    grad_turned_ref,
    loss_ref,
    total_ref,
):
    part, step = pl.program_id(0), pl.program_id(1)
    normed = normed_ref[...]
    gate = mm(normed, gate_w_ref[0])
    up = mm(normed, up_w_ref[0])
    hidden = (gate * jax.nn.sigmoid(gate) * up).astype(jnp.bfloat16)
    gate_ref[0] = gate.astype(jnp.bfloat16)
    up_ref[0] = up.astype(jnp.bfloat16)
    hidden_ref[0] = hidden
    share = mm_nt(hidden, down_w_ref[0])
    rows = pl.ds(pl.multiple_of(step * BLOCK, BLOCK), BLOCK)

    @pl.when(part == 0)
    def _():
        total_ref[rows, :] = share

    @pl.when(part == pl.num_programs(0) - 1)
    def _():
        output = residual_ref[...] + (total_ref[rows, :] + share)
        output_ref[...] = output
        error = output - target_ref[...].astype(jnp.float32)
        live = live_ref[:, 0:1]
        grad = error * live * level_ref[0:1, 0:1]
        grad_ref[...] = grad.astype(jnp.bfloat16)
        grad_turned_ref[...] = grad.T.astype(jnp.bfloat16)
        squares = jnp.sum(live * error * error, axis=0, keepdims=True)

        @pl.when(step == 0)
        def _():
            loss_ref[...] = jnp.zeros(loss_ref.shape, jnp.float32)

        loss_ref[0:1, :] += squares


def dense_backward_body(
    grad_ref,
    gate_w_ref,
    up_w_ref,
    down_w_ref,
    gate_ref,
    up_ref,
    residual_ref,
    output_ref,
    target_ref,
    live_ref,
    level_ref,
    gain_ref,
    grad_gate_ref,
    grad_up_ref,
    back_ref,
    back_low_ref,
    back_turned_ref,
    gain_sum_ref,
    total_ref,
):
    part, step = pl.program_id(0), pl.program_id(1)
    grad_hidden = mm(grad_ref[...], down_w_ref[0])
    gate = gate_ref[0].astype(jnp.float32)
    up = up_ref[0].astype(jnp.float32)
    sigmoid = jax.nn.sigmoid(gate)
    grad_gate = (grad_hidden * up * sigmoid * (1.0 + gate * (1.0 - sigmoid))).astype(jnp.bfloat16)
    grad_up = (grad_hidden * gate * sigmoid).astype(jnp.bfloat16)
    grad_gate_ref[0] = grad_gate
    grad_up_ref[0] = grad_up
    share = mm_nt(grad_gate, gate_w_ref[0]) + mm_nt(grad_up, up_w_ref[0])
    rows = pl.ds(pl.multiple_of(step * BLOCK, BLOCK), BLOCK)

    @pl.when(part == 0)
    def _():
        total_ref[rows, :] = share

    @pl.when(part == pl.num_programs(0) - 1)
    def _():
        error = output_ref[...] - target_ref[...].astype(jnp.float32)
        back, gain_sum = rms_backward(
            residual_ref[...], gain_ref[...], total_ref[rows, :] + share
        )
        back = error * live_ref[:, 0:1] * level_ref[0:1, 0:1] + back
        back_ref[...] = back
        back_low_ref[...] = back.astype(jnp.bfloat16)
        back_turned_ref[...] = back.T.astype(jnp.bfloat16)

        @pl.when(step == 0)
        def _():
            gain_sum_ref[...] = jnp.zeros(gain_sum_ref.shape, jnp.float32)

        gain_sum_ref[0:1, :] += gain_sum


def input_backward_body(
    first_ref, second_ref, weight_ref, input_ref, residual_ref, gain_ref, back_ref, gain_sum_ref, total_ref
):
    part, step = pl.program_id(0), pl.program_id(1)
    grad = jnp.where(part == 0, first_ref[0], second_ref[0])
    share = mm_nt(grad, weight_ref[0])
    rows = pl.ds(pl.multiple_of(step * BLOCK, BLOCK), BLOCK)

    @pl.when(part == 0)
    def _():
        total_ref[rows, :] = share

    @pl.when(part == pl.num_programs(0) - 1)
    def _():
        back, gain_sum = rms_backward(
            input_ref[...].astype(jnp.float32), gain_ref[...], total_ref[rows, :] + share
        )
        back_ref[...] = residual_ref[...] + back

        @pl.when(step == 0)
        def _():
            gain_sum_ref[...] = jnp.zeros(gain_sum_ref.shape, jnp.float32)

        gain_sum_ref[0:1, :] += gain_sum


def dense_call(body, flags, arrays, choose, width, units):
    rows = arrays[0].shape[-2]
    full, low = jnp.float32, jnp.bfloat16

    def cut(block, place, shape=None, kind=full):
        return (pl.BlockSpec(block, place), jax.ShapeDtypeStruct(shape or block, kind))

    late = (lambda p, i, flags: (i * p, 0), (rows, width))
    spec = SimpleNamespace(
        row=cut((BLOCK, width), lambda p, i, flags: (i, 0)),
        late=cut((BLOCK, width), *late),
        late_low=cut((BLOCK, width), *late, low),
        turned=cut((width, BLOCK), lambda p, i, flags: (0, i * p), (width, rows), low),
        unit=cut((1, BLOCK, units), lambda p, i, flags: (p, i, 0), (2, rows, units), low),
        first=cut((1, BLOCK, units), lambda p, i, flags: (0, i * (1 - p), 0)),
        second=cut((1, BLOCK, units), lambda p, i, flags: (0, i * p, 0)),
        lane=cut((BLOCK, TILE), lambda p, i, flags: (i * p, 0)),
        level=cut((8, TILE), lambda p, i, flags: (0, 0)),
        gain=cut((1, width), lambda p, i, flags: (0, 0)),
        own=cut((1, width, units), lambda p, i, flags: (lax.rem(p + 1 + flags[1], 2), 0, 0)),
        sums=cut((8, width), lambda p, i, flags: (0, 0)),
        weights=[
            cut((1, width, units), lambda p, i, flags, index=index: (p, 0, index)) for index in range(3)
        ],
    )
    taken, given = choose(spec)
    return pl.pallas_call(
        lambda flags_ref, *refs: body(*refs),
        grid_spec=pltpu.PrefetchScalarGridSpec(
            num_scalar_prefetch=1,
            grid=(2, rows // BLOCK),
            in_specs=[item[0] for item in taken],
            out_specs=[item[0] for item in given],
            scratch_shapes=[pltpu.VMEM((rows, width), full)],
        ),
        out_shape=[item[1] for item in given],
        compiler_params=pltpu.CompilerParams(vmem_limit_bytes=56 * 1024 * 1024),
        cost_estimate=pl.CostEstimate(flops=COST, transcendentals=0, bytes_accessed=10**8),
        name=body.__name__[:-5],
    )(flags, *arrays)


def product_body(own, side_first, paired, flags_ref, left_ref, first_ref, *refs):
    part = pl.program_id(0)
    shape = left_ref.shape
    if paired:
        second_ref, *refs = refs
    left = left_ref[...].reshape(shape[0] * shape[2], shape[3])

    def finish(right_ref):
        result = mm(left, right_ref[...].reshape(right_ref.shape[-2:]))
        if own:
            result = result + refs[0][0].astype(jnp.float32)
        result = result.astype(jnp.bfloat16)
        if not side_first:
            refs[-1][0] = result
            return
        split = result.reshape(shape[0] // 2, 2, shape[2], result.shape[1])
        count = shape[0] * shape[2] // 2
        low = split[:, 0].reshape(count, -1)
        high = split[:, 1].reshape(count, -1)
        here = flags_ref[2] == 0
        refs[-2][0] = jnp.where(here, low, high)
        refs[-1][0] = jnp.where(here, high, low)

    if not paired:
        finish(first_ref)
        return

    @pl.when(part == 0)
    def _():
        finish(first_ref)

    @pl.when(part == 1)
    def _():
        finish(second_ref)


def product(flags, left, rights, received=None, side_first=False, relative=False):
    own = received is not None
    side_first = side_first and own
    groups, _, rows, tokens = left.shape
    cols, count = rights[0].shape[-1], len(rights)
    block = cols if count == 2 else -(-cols // (2 * TILE)) * TILE
    last = -(-cols // block) - 1

    def slot(p, flags):
        return 0 if count == 1 else 1 - p if relative else lax.rem(p + flags[1], 2)

    def right_spec(array, index, which):
        def place(p, j, flags):
            return j * (1 - p) + last * p if which == 0 else j * p

        if array.ndim == 3:
            return pl.BlockSpec(
                (1, tokens, block), lambda p, j, flags: (index, 0, place(p, j, flags))
            )
        return pl.BlockSpec((tokens, block), lambda p, j, flags: (0, place(p, j, flags)))

    result_rows = groups * rows // (2 if side_first else 1)
    result = pl.BlockSpec((1, result_rows, block), lambda p, j, flags: (slot(p, flags), 0, j))
    kept = jax.ShapeDtypeStruct((count, result_rows, cols), jnp.bfloat16)
    in_specs = [
        pl.BlockSpec(
            (groups, 1, rows, tokens),
            lambda p, j, flags: (0, flags[0] if own else 1 - flags[0], 0, 0),
        ),
    ]
    paired = count == 2 and rights[0] is not rights[1]
    arrays = [left, rights[0]]
    if paired:
        arrays.append(rights[1])
        in_specs += [
            right_spec(rights[0], 0, 0),
            right_spec(rights[1], rights[1].shape[0] - 1, 1),
        ]
    else:
        in_specs.append(pl.BlockSpec((1, tokens, block), lambda p, j, flags: (p, 0, j)))
    if own:
        in_specs.append(
            pl.BlockSpec((1, groups * rows, block), lambda p, j, flags: (slot(p, flags), 0, j))
        )
        arrays.append(received)
    many = 2 if side_first else 1
    results = pl.pallas_call(
        functools.partial(product_body, own, side_first, paired),
        grid_spec=pltpu.PrefetchScalarGridSpec(
            num_scalar_prefetch=1,
            grid=(count, last + 1),
            in_specs=in_specs,
            out_specs=[result] * many,
        ),
        out_shape=[kept] * many,
        compiler_params=pltpu.CompilerParams(vmem_limit_bytes=56 * 1024 * 1024),
        cost_estimate=pl.CostEstimate(
            flops=2 * groups * rows * tokens * cols * count, transcendentals=0, bytes_accessed=10**7
        ),
        name="product",
    )(flags, *arrays)
    return results if side_first else results[0]


def token_info(seg):
    sequences, length = seg.shape
    lanes = []
    for j in range(1, 4):
        lanes.append(jnp.pad(seg[:, j:] == seg[:, :-j], ((0, 0), (j, 0))))
    ends = seg.reshape(sequences, length // TILE, TILE)
    before = jnp.pad(ends[:, :-1, -1], ((0, 0), (1, 0)), constant_values=-1)
    lanes.append((ends == before[:, :, None]).reshape(sequences, length))
    lanes.append(seg)
    for j in range(1, 4):
        lanes.append(jnp.pad(seg[:, j:] == seg[:, :-j], ((0, 0), (0, j))))
    table = jnp.stack([item.astype(jnp.float32).reshape(-1) for item in lanes], axis=1)
    return jnp.pad(table, ((0, 0), (0, TILE - table.shape[1])))


def gather_all(local):
    rows = lax.all_gather(local, (TP, DP), axis=0, tiled=True)
    shares = lax.axis_size(TP)
    return rows.reshape(shares, rows.shape[0] // shares, rows.shape[1])


def scatter_all(parts):
    shares, rows, cols = parts.shape
    return lax.psum_scatter(
        parts.reshape(shares * rows, cols), (TP, DP), scatter_dimension=0, tiled=True
    ).astype(jnp.float32)


def exchange(array, axis, bit):
    size = lax.axis_size(axis)
    return lax.ppermute(array, axis, [(i, i ^ bit) for i in range(size)])


def shift(array, step):
    size = lax.axis_size(DP)
    return lax.ppermute(array, DP, [(i, (i + step) % size) for i in range(size)])


def pick(array, index, axis):
    return lax.dynamic_index_in_dim(array, index, axis, keepdims=False)


def add_low(left, right):
    return (left.astype(jnp.float32) + right.astype(jnp.float32)).astype(jnp.bfloat16)


def after(value, *earlier):
    return lax.optimization_barrier((value, earlier))[0]


class Scatter:
    def __init__(self, flags, turned, rights, stages, relative=False):
        self.relative, self.stages = relative, list(stages)
        self.size = lax.axis_size(DP)
        self.flags, self.rights = flags, rights
        self.left = turned.reshape(self.size // 2, 2, -1, turned.shape[1])
        self.rows = self.left.shape[2]
        self.sent = [product(flags, self.left, rights, relative=relative)]

    joined = None

    def routes(self):
        flat = [item.reshape(-1, item.shape[-1]) for item in self.sent]
        stage = self.stages[0]
        return [
            ((stage, step if stage == PLACE else 0, item.shape[0]), item)
            for step, item in enumerate(flat)
        ]

    def take(self, moved):
        stage = self.stages.pop(0)
        if stage == PLACE:
            self.total = self.kept.astype(jnp.float32)
            for item in moved:
                self.total = self.total + item.astype(jnp.float32)
            return
        if stage == CORE:
            side_first = self.stages[0] == SIDE
            held = product(
                self.flags, self.left, self.rights, moved[0], side_first, self.relative
            )
            if side_first:
                self.kept, self.sent = [list(item) for item in held]
            else:
                self.kept, self.sent = [held[0]], [held[1]]
            return
        held = [add_low(kept, item) for kept, item in zip(self.kept, moved)]
        if not self.stages:
            self.held = held[0]
            return
        if self.joined is not None:
            held = [add_low(held[0], self.joined)]
        stage = self.stages[0]
        if stage == TENSOR:
            self.kept, self.sent = held[:1], held[1:]
        elif stage == SIDE:
            held = held[0].reshape(self.size // 4, 2, self.rows, -1)
            self.kept, self.sent = [
                [pick(held, index, 1).reshape(-1, held.shape[-1])]
                for index in (self.flags[2], 1 - self.flags[2])
            ]
        else:
            count = self.size // 4
            held = held[0].reshape(count, self.rows, -1)
            self.sent = [
                pick(held, (self.flags[3] + step) % count, 0) for step in range(1, count)
            ]
            self.kept = pick(held, self.flags[3], 0)


def send(route, array):
    stage, step, _ = route
    if stage == PLACE:
        return shift(array, 4 * (step + 1))
    if stage == TENSOR:
        return exchange(array, TP, 1)
    return exchange(array, DP, stage)


class Transfer:
    def __init__(self, *items):
        self.items, self.routes = items, {}
        for index, item in enumerate(items):
            for slot, (route, array) in enumerate(item.routes()):
                key = route + ((index, slot) if route[0] == CORE else ())
                self.routes.setdefault(key, []).append((index, slot, array))
        self.packed = [
            jnp.concatenate([entry[2] for entry in entries], axis=1)
            for entries in self.routes.values()
        ]

    def send(self):
        return [send(key[:3], array) for key, array in zip(self.routes, self.packed)]

    def land(self):
        self.accept(lax.optimization_barrier(self.send()))

    def accept(self, moved):
        got = [[None] * len(item.sent) for item in self.items]
        for entries, array in zip(self.routes.values(), moved):
            pieces = columns(array, [entry[2].shape[1] for entry in entries])
            for (index, slot, _), piece in zip(entries, pieces):
                got[index][slot] = piece
        for item, mine in zip(self.items, got):
            item.take([piece.reshape(sent.shape) for piece, sent in zip(mine, item.sent)])


class Shared:
    def __init__(self, flat, stages):
        self.flat, self.stages = flat.reshape(1, -1), list(stages)

    @property
    def sent(self):
        return [self.flat]

    def routes(self):
        return [((self.stages[0], 0, 1), self.flat)]

    def take(self, moved):
        self.stages.pop(0)
        self.flat = self.flat + moved[0]


def columns(array, sizes):
    pieces, start = [], 0
    for size in sizes:
        pieces.append(array[..., start : start + size])
        start += size
    return pieces


def on_device_whole(
    layer_input,
    target,
    segment,
    pad_mask,
    norm1_gain,
    w_query,
    w_key,
    w_value,
    w_gate_out,
    w_decay,
    w_beta,
    conv_query,
    conv_key,
    conv_value,
    decay_scale,
    decay_bias,
    out_norm_gain,
    w_out,
    norm2_gain,
    w_ffn_gate,
    w_ffn_up,
    w_ffn_down,
):
    own_rows, width = layer_input.shape
    shares = lax.axis_size(TP)
    sequences = own_rows // LENGTH
    tensor_index = lax.axis_index(TP)
    low = jnp.bfloat16
    proj_local = (w_query, w_key, w_value, w_gate_out, w_decay, w_beta)
    proj_sizes = [item.shape[1] for item in proj_local]
    used = sum(proj_sizes)
    padded = -(-used // 128) * 128
    proj_all = gather_all(
        jnp.concatenate(proj_local + (jnp.zeros((w_query.shape[0], padded - used), low),), axis=1)
    )
    rest_local = (w_ffn_gate, w_ffn_up, w_ffn_down, w_out)
    rest_sizes = [item.shape[1] for item in rest_local]
    rest_all = gather_all(jnp.concatenate(rest_local, axis=1))
    out_all = columns(rest_all, rest_sizes)[3]
    live = pad_mask.astype(jnp.float32)
    count = lax.psum(jnp.sum(live), (DP, TP))
    input_float = layer_input.astype(jnp.float32)
    normed = rms_scale(input_float, norm1_gain).astype(low)
    seg_rows = lax.dynamic_slice_in_dim(segment, tensor_index * own_rows, own_rows, 0).reshape(
        sequences, LENGTH
    )
    parts = (1 - tensor_index, tensor_index)
    proj = [
        jnp.dot(normed, pick(proj_all, part, 0), preferred_element_type=jnp.float32)[None]
        for part in parts
    ]
    heads = w_decay.shape[1]
    info = token_info(seg_rows)

    def by_part(item):
        return item.reshape(item.shape[0], shares, item.shape[1] // shares).transpose(1, 0, 2)

    conv = jnp.pad(
        jnp.concatenate([by_part(c) for c in (conv_query, conv_key, conv_value)], axis=2),
        ((0, 0), (0, 4), (0, 0)),
    )
    rates = jnp.pad(
        by_part(jnp.stack([decay_scale, decay_bias])), ((0, 0), (0, 6), (0, TILE - heads))
    )
    gain = out_norm_gain.reshape(1, -1)
    value_cols = w_value.shape[1]
    mixer_args = [
        (item, info, pick(conv, part, 0)[None], pick(rates, part, 0)[None], gain)
        for item, part in zip(proj, parts)
    ]
    out_parts = [pick(out_all, part, 0) for part in parts]
    saved, mixed, residual = [], [], input_float
    for arguments in mixer_args:
        mixed_low, *kept = mixer_forward(*arguments, heads)
        mixed.append(mixed_low)
        saved.append(kept)
    for item, weight in zip(mixed, out_parts):
        residual = residual + contract_cols(item, weight)
    normed2 = rms_scale(residual, norm2_gain).astype(low)
    units = w_ffn_gate.shape[1]
    all_tokens = own_rows * lax.axis_size(DP) * lax.axis_size(TP)
    level = jnp.full((8, TILE), all_tokens / count, jnp.float32)
    live_lanes = jnp.broadcast_to(live[:, None], (own_rows, TILE))
    mine = lax.axis_index(DP)
    flags = jnp.stack([mine % 2, tensor_index, (mine // 2) % 2, mine // 4]).astype(jnp.int32)
    weights = [rest_all] * 3
    gate_pre, up_pre, hidden, output, grad_ffn, grad_ffn_turned, loss_rows = dense_call(
        dense_forward_body,
        flags,
        [normed2, *weights, residual, target, live_lanes, level],
        lambda s: (
            [s.row, *s.weights, s.late, s.late, s.lane, s.level],
            [s.unit, s.unit, s.unit, s.late, s.late_low, s.turned, s.sums],
        ),
        width,
        units,
    )
    loss_sum = jnp.sum(loss_rows)
    down = Scatter(flags, grad_ffn_turned, [hidden, hidden], SIDE_FIRST)
    cores = Transfer(down)
    grad_gates, grad_ups, grad_residual, grad_attention, back_turned, gain_two_rows = dense_call(
        dense_backward_body,
        flags,
        [
            after(grad_ffn, cores.packed), *weights, gate_pre, up_pre,
            residual, output, target, live_lanes, level, norm2_gain.reshape(1, -1),
        ],
        lambda s: (
            [s.row, *s.weights, s.unit, s.unit, s.late, s.late, s.late, s.lane, s.level, s.gain],
            [s.unit, s.unit, s.late, s.late_low, s.turned, s.sums],
        ),
        width,
        units,
    )
    grad_gain_two = gain_two_rows[0]
    turned2 = normed2.T
    gate = Scatter(flags, turned2, [grad_gates, grad_gates], TENSOR_FIRST)
    up = Scatter(flags, turned2, [grad_ups, grad_ups], SIDE_FIRST)
    cores.land()
    first_down = Transfer(down)
    gate.sent = after(gate.sent, first_down.packed)
    cores = Transfer(gate, up)
    out = Scatter(flags, back_turned, mixed, SIDE_FIRST, True)
    out_cores = Transfer(out)
    later = after(grad_attention, out_cores.packed, cores.packed)
    grad_mixed = [
        jnp.dot(later, weight, preferred_element_type=jnp.float32) for weight in out_parts
    ]
    cores.land()
    out_cores.land()
    middle = Transfer(gate, up, out)
    ready = after(grad_mixed[0], middle.packed)
    per_part = [mixer_backward(*mixer_args[0], saved[0], ready, heads)]
    turned = normed.T
    theirs = Scatter(flags, turned, [per_part[0][0]], (CORE, SIDE))
    theirs_cores = Transfer(theirs)
    middle.land()
    first_down.land()
    middle = Transfer(gate, up, out, down)
    theirs.left = after(theirs.left, middle.packed)
    theirs_cores.land()
    theirs_side = Transfer(theirs)
    ready = after(grad_mixed[1], middle.packed, theirs_side.packed)
    per_part.append(mixer_backward(*mixer_args[1], saved[1], ready, heads))
    grad_conv, grad_rates, grad_gain = [
        jnp.roll(
            jnp.concatenate([item[i] for item in per_part], axis=0), tensor_index + 1, axis=0
        )
        for i in (1, 2, 3)
    ]

    def from_part(item):
        return item.transpose(1, 0, 2).reshape(item.shape[1], -1)

    query_cols = w_query.shape[1]
    small = [
        from_part(item)
        for item in columns(grad_conv[:, :4], (query_cols, query_cols, value_cols))
    ] + [
        grad_rates[:, 0, :heads].reshape(-1),
        grad_rates[:, 1, :heads].reshape(-1),
        jnp.sum(grad_gain[:, 0], axis=0),
        grad_gain_two,
        loss_sum,
    ]
    grad_proj = [item[0] for item in per_part]
    ours = Scatter(flags, turned, [grad_proj[1]], (CORE, SIDE, PLACE))
    ours_cores = Transfer(ours)
    theirs.sent = after(theirs.sent, ours_cores.packed)
    middle.land()
    theirs_side.land()
    middle = Transfer(gate, up, out, down)
    ours.left = after(ours.left, middle.packed, theirs.held)
    ours_cores.land()
    ending = Transfer(ours)
    grad_proj = after(grad_proj, ending.packed)
    grad_input, gain_one_rows = dense_call(
        input_backward_body,
        flags,
        [*grad_proj, proj_all, layer_input, grad_residual, norm1_gain.reshape(1, -1)],
        lambda s: ([s.first, s.second, s.own, s.late, s.late, s.gain], [s.late, s.sums]),
        width,
        padded,
    )
    joined = exchange(theirs.held, TP, 1)
    joined, gain_one_rows, *moved = lax.optimization_barrier(
        [joined, gain_one_rows] + middle.send() + ending.send()
    )
    ours.joined = joined
    middle.accept(moved[: len(middle.packed)])
    ending.accept(moved[len(middle.packed) :])
    size, places = lax.axis_size(DP), []
    while 4 << len(places) < size:
        places.append(4 << len(places))
    small.append(gain_one_rows[0])
    flat = jnp.concatenate([item.reshape(-1) for item in small])
    flat = jnp.pad(flat, (0, -flat.shape[0] % 1024))
    shared = Shared(flat, places + [CORE, SIDE, TENSOR])
    for _ in places:
        Transfer(shared).land()
    ours.sent = after(ours.sent, shared.flat)
    ending = Transfer(ours)
    shared.flat = after(shared.flat, ending.packed)
    while shared.stages:
        Transfer(shared).land()
    ending.land()
    own_gate, own_up, own_out, own_down = [item.total for item in (gate, up, out, down)]
    own_proj = columns(ours.total, proj_sizes)
    summed, start = [], 0
    for item in small:
        summed.append(shared.flat[0, start : start + item.size].reshape(item.shape))
        start += item.size
    loss = summed[7] / (count * width)
    return (
        output,
        loss,
        grad_input,
        summed[8],
        *own_proj,
        *summed[:6],
        own_out,
        summed[6],
        own_gate,
        own_up,
        own_down,
    )


def on_device(layer_input, *others):
    size = lax.axis_size(DP)
    whole = layer_input.shape[0] % LENGTH == 0 and lax.axis_size(TP) == 2
    whole = whole and size >= 4 and size & (size - 1) == 0
    return (on_device_whole if whole else on_device_split)(layer_input, *others)


def solution(mesh):
    return jax.shard_map(
        on_device,
        mesh=mesh,
        in_specs=(
            P((DP, TP), None),
            P((DP, TP), None),
            P(DP),
            P((DP, TP)),
            P(),
            P(DP, TP),
            P(DP, TP),
            P(DP, TP),
            P(DP, TP),
            P(DP, TP),
            P(DP, TP),
            P(),
            P(),
            P(),
            P(),
            P(),
            P(),
            P(DP, TP),
            P(),
            P(DP, TP),
            P(DP, TP),
            P(DP, TP),
        ),
        out_specs=(
            P((DP, TP), None),
            P(),
            P((DP, TP), None),
            P(),
            P(DP, TP),
            P(DP, TP),
            P(DP, TP),
            P(DP, TP),
            P(DP, TP),
            P(DP, TP),
            P(),
            P(),
            P(),
            P(),
            P(),
            P(),
            P(DP, TP),
            P(),
            P(DP, TP),
            P(DP, TP),
            P(DP, TP),
        ),
        check_vma=False,
    )
```
